32 devices in a mesh: groups: 2 (over y), expert: 4 (over z), seq: 4 (over x, core).
Axes of the slice: x: 2, y: 2, z: 4, core: 2. Of those that a mesh axis runs over, the one named last changes fastest.
Arguments:
- inputs: bfloat16 [4096, 1024], P(('groups', 'expert', 'seq')), parts along dimension 0, may hold values from -6 to 6
- grad_out: bfloat16 [4096, 1024], P(('groups', 'expert', 'seq')), parts along dimension 0, may hold values from -4 to 4
- gates: bfloat16 [4096, 4], P(('groups', 'expert', 'seq')), parts along dimension 0, may hold values from 0.049804688 to 0.59765625
- expert_ids: int32 [4096, 4], P(('groups', 'expert', 'seq')), parts along dimension 0, may hold values from 0 to 3, as said below
- slot_index: int32 [4096, 4], P(('groups', 'expert', 'seq')), parts along dimension 0, may hold values from 0 to 127, as said below
- filter_taps: bfloat16 [256, 1024], replicated, may hold values from -0.375 to 0.375
- w_gate: bfloat16 [4, 1024, 512], P('expert', 'seq'), may hold values from -0.1875 to 0.1875
- w_up: bfloat16 [4, 1024, 512], P('expert', 'seq'), may hold values from -0.1875 to 0.1875
- w_down: bfloat16 [4, 512, 1024], P('expert', 'seq'), may hold values from -0.25 to 0.25
Outputs:
- grad_inputs: bfloat16 [4096, 1024], P(('groups', 'expert', 'seq')), parts along dimension 0
- grad_gates: bfloat16 [4096, 4], P(('groups', 'expert', 'seq')), parts along dimension 0
- grad_filter: float32 [512, 1024], P('groups'), parts along dimension 0
- grad_w_gate: bfloat16 [8, 1024, 512], P(('groups', 'expert'), 'seq'), parts along dimension 0
- grad_w_up: bfloat16 [8, 1024, 512], P(('groups', 'expert'), 'seq'), parts along dimension 0
- grad_w_down: bfloat16 [8, 512, 1024], P(('groups', 'expert'), 'seq'), parts along dimension 0
The draws below stay inside these ranges and needn't reach their ends.
There are 2 independent parts, one for each index of `groups`. The reference program is written for one: setup_inputs(seed, part) draws one part's arguments, and reference() takes and returns one part's arrays. A program takes and returns all parts, laid end to end along the dimension named above; an argument that names none is the same for every part. Nothing has to cross between parts.
Inputs may be any that keep to these rules, and one draw needn't show every extreme that they name: `expert_ids`: each row names 4 different experts, and every expert is named by some row. Among the assignments of the 128 rows of one device that name the same expert, slot_index takes each of the values 0, 1, ... once, in an order of priority that is not row order; assignments with a slot of 128 or more are dropped.
All inputs are finite; a program needn't handle non-finite values.
Results may differ from the reference program's by a relative error of at most 0.009.
Values may be sent and summed in bfloat16 or wider, within the bound.
A program may use at most 64 MiB of HBM per device.

```python
import jax
import jax.numpy as jnp
from jax import lax

D = 1024
FF = 512
TAPS = 256
TOP = 4
TOK_DEV = 128
SPECIALIST_COUNT = 4
CAP = 128
LENGTH = 512
TOKENS = 2048
N_EXPERT = 4
N_SEQ = 4


def device_ranks(item):
    chosen_flat, priority = item
    same = chosen_flat[:, None] == chosen_flat[None, :]
    before = priority[None, :] < priority[:, None]
    return jnp.sum((same & before).astype(jnp.int32), axis=1).astype(jnp.int32)


def routing(key):
    drawn_router_preference = jax.random.fold_in(key, 7)
    busiest_rng_branch, favour_rng_branch, jitter_rng_branch = jax.random.split(drawn_router_preference, 3)
    priority_branch = jax.random.fold_in(key, 11)
    busiest_specialist = jax.random.randint(busiest_rng_branch, (), 0, SPECIALIST_COUNT)
    lane_positions = jnp.arange(SPECIALIST_COUNT, dtype=jnp.int32)
    extra_favour_amount = jax.random.randint(favour_rng_branch, (SPECIALIST_COUNT,), 0, 2 ** 20)
    extra_favour_amount = jnp.where(lane_positions == busiest_specialist, 2 ** 21, extra_favour_amount)
    position_mod = jnp.arange(TOKENS, dtype=jnp.int32) % SPECIALIST_COUNT
    pinned_specialist = jnp.where(lane_positions[None, :] == position_mod[:, None], 2 ** 21 - 1, 0)
    jitter_draw = jax.random.randint(jitter_rng_branch, (TOKENS, SPECIALIST_COUNT), 0, 2 ** 20)
    dispatch_preference = (jitter_draw + jnp.maximum(extra_favour_amount[None, :], pinned_specialist)) * SPECIALIST_COUNT + lane_positions[None, :]
    chosen = lax.top_k(dispatch_preference, TOP)[1].astype(jnp.int32)
    blocks = TOKENS // TOK_DEV
    per_block = TOK_DEV * TOP
    local_index = jnp.arange(per_block, dtype=jnp.int32)
    high_part = jax.random.randint(priority_branch, (blocks, per_block), 0, 2 ** 12)
    priority = high_part * per_block + local_index[None, :]
    placed = lax.map(device_ranks, (chosen.reshape(blocks, per_block), priority))
    return (chosen, placed.reshape(TOKENS, TOP).astype(jnp.int32))


def draw_expert_ids(key, part):
    return routing(key)[0]


def draw_slot_index(key, part):
    return routing(key)[1]


def shard_levels(key, extent, cuts, least, top_value):
    factor_of = 1.0
    for dim, blocks in cuts:
        steps = jax.random.uniform(jax.random.fold_in(jax.random.fold_in(key, 6), dim), (blocks,), jnp.float32, least / len(cuts), top_value / len(cuts))
        factor_of = factor_of * jnp.repeat(jnp.exp(steps), extent[dim] // blocks).reshape((-1,) + (1,) * (len(extent) - 1 - dim))
    return factor_of


def gaussian(stream_key, shape, width, most, cuts=(), kind=jnp.bfloat16):
    factor_of = shard_levels(stream_key, shape, cuts, -0.22, 0.18) if cuts else 1.0
    entries = jax.random.normal(stream_key, shape, jnp.float32) * width * factor_of
    return jnp.minimum(jnp.maximum(entries, -most), most).astype(kind)


def setup_inputs(seed: int = 0, part: int = 0) -> dict:
    key_list = jax.random.split(jax.random.key(seed), 10)
    own_keys = jax.random.split(jax.random.fold_in(key_list[9], part), 10)
    inputs = gaussian(own_keys[0], (TOKENS, D), 1.0, 6.0, ((0, 16),))
    grad_out = gaussian(own_keys[1], (TOKENS, D), 0.25, 4.0, ((0, 16),))
    gates = jnp.clip(0.049804688 + 0.54785156 * jax.random.uniform(own_keys[2], (TOKENS, TOP), jnp.float32) ** shard_levels(own_keys[2], (TOKENS, TOP), ((0, 16),), -0.2, 0.2), 0.049804688, 0.59765625).astype(jnp.bfloat16)
    expert_ids = draw_expert_ids(jax.random.fold_in(jax.random.fold_in(key_list[9], part), 71), part)
    slot_index = draw_slot_index(jax.random.fold_in(jax.random.fold_in(key_list[9], part), 71), part)
    filter_taps = gaussian(key_list[5], (TAPS, D), TAPS ** -0.5, 0.375)
    w_gate = gaussian(key_list[6], (SPECIALIST_COUNT, D, FF), D ** -0.5, 0.1875, ((0, 4), (1, 4)))
    w_up = gaussian(key_list[7], (SPECIALIST_COUNT, D, FF), D ** -0.5, 0.1875, ((0, 4), (1, 4)))
    w_down = gaussian(key_list[8], (SPECIALIST_COUNT, FF, D), FF ** -0.5, 0.25, ((0, 4), (1, 4)))
    return dict(inputs=inputs, grad_out=grad_out, gates=gates, expert_ids=expert_ids, slot_index=slot_index, filter_taps=filter_taps, w_gate=w_gate, w_up=w_up, w_down=w_down)


def contract(left, right, left_dim, right_dim):
    return lax.dot_general(left, right, (((left_dim,), (right_dim,)), ((), ())), preferred_element_type=jnp.float32)

def causal_filter(padded, taps_f):

    def add_tap(tap, total):
        window = lax.dynamic_slice_in_dim(padded, TAPS - 1 - tap, LENGTH, 1)
        weights = lax.dynamic_slice_in_dim(taps_f, tap, 1, 0)
        return total + weights[None] * window
    return lax.fori_loop(0, TAPS, add_tap, jnp.zeros((N_EXPERT, LENGTH, D), jnp.float32))

def anticausal_filter(grad_padded, taps_f):

    def add_tap(tap, total):
        window = lax.dynamic_slice_in_dim(grad_padded, tap, LENGTH, 1)
        weights = lax.dynamic_slice_in_dim(taps_f, tap, 1, 0)
        return total + weights[None] * window
    return lax.fori_loop(0, TAPS, add_tap, jnp.zeros((N_EXPERT, LENGTH, D), jnp.float32))

def expert_block(item):
    token_buf, scaled_buf, gate_mat, up_mat, down_mat = item
    grad_list = []
    output_list = []
    sum_gate = jnp.zeros(gate_mat.shape, jnp.float32)
    sum_up = jnp.zeros(up_mat.shape, jnp.float32)
    sum_down = jnp.zeros(down_mat.shape, jnp.float32)
    for quarter in range(N_SEQ):
        token_rows = token_buf[quarter]
        scaled_rows = scaled_buf[quarter]
        pre_gate = jnp.dot(token_rows, gate_mat, preferred_element_type=jnp.float32)
        pre_up = jnp.dot(token_rows, up_mat, preferred_element_type=jnp.float32)
        sigma = jax.nn.sigmoid(pre_gate)
        swish = pre_gate * sigma
        hidden = (swish * pre_up).astype(jnp.bfloat16)
        output_list.append(jnp.dot(hidden, down_mat, preferred_element_type=jnp.float32).astype(jnp.bfloat16))
        grad_hidden = contract(scaled_rows, down_mat, 1, 1)
        grad_pre_gate = (grad_hidden * pre_up * (sigma * (1.0 + pre_gate * (1.0 - sigma)))).astype(jnp.bfloat16)
        grad_pre_up = (grad_hidden * swish).astype(jnp.bfloat16)
        part_gate = lax.optimization_barrier(contract(token_rows, grad_pre_gate, 0, 0).astype(jnp.bfloat16))
        part_up = lax.optimization_barrier(contract(token_rows, grad_pre_up, 0, 0).astype(jnp.bfloat16))
        part_down = lax.optimization_barrier(contract(hidden, scaled_rows, 0, 0).astype(jnp.bfloat16))
        sum_gate = sum_gate + part_gate.astype(jnp.float32)
        sum_up = sum_up + part_up.astype(jnp.float32)
        sum_down = sum_down + part_down.astype(jnp.float32)
        grad_rows = contract(grad_pre_gate, gate_mat, 1, 1) + contract(grad_pre_up, up_mat, 1, 1)
        grad_list.append(grad_rows.astype(jnp.bfloat16))
    return (jnp.stack(grad_list), jnp.stack(output_list), sum_gate.astype(jnp.bfloat16), sum_up.astype(jnp.bfloat16), sum_down.astype(jnp.bfloat16))

def reference(inputs, grad_out, gates, expert_ids, slot_index, filter_taps, w_gate, w_up, w_down):
    taps_f = filter_taps.astype(jnp.float32)
    seq_inputs = inputs.astype(jnp.float32).reshape(N_EXPERT, LENGTH, D)
    padded = jnp.pad(seq_inputs, ((0, 0), (TAPS - 1, 0), (0, 0)))
    filtered = causal_filter(padded, taps_f).reshape(TOKENS, D).astype(jnp.bfloat16)
    kept = slot_index < CAP
    device = jnp.arange(TOKENS, dtype=jnp.int32) // TOK_DEV
    source = (device // N_SEQ)[:, None]
    quarter = (device % N_SEQ)[:, None]
    limit = SPECIALIST_COUNT * N_SEQ * N_EXPERT * CAP
    dest = jnp.where(kept, ((expert_ids * N_SEQ + quarter) * N_EXPERT + source) * CAP + slot_index, limit)
    dest = dest.reshape(-1).astype(jnp.int32)
    token_rows = jnp.broadcast_to(filtered[:, None, :], (TOKENS, TOP, D)).reshape(-1, D)
    scaled = (gates.astype(jnp.float32)[:, :, None] * grad_out.astype(jnp.float32)[:, None, :]).astype(jnp.bfloat16).reshape(-1, D)
    block_rows = N_EXPERT * CAP
    token_buf = jnp.zeros((limit, D), jnp.bfloat16).at[dest].set(token_rows, mode='drop').reshape(SPECIALIST_COUNT, N_SEQ, block_rows, D)
    scaled_buf = jnp.zeros((limit, D), jnp.bfloat16).at[dest].set(scaled, mode='drop').reshape(SPECIALIST_COUNT, N_SEQ, block_rows, D)
    grad_buf, output_buf, grad_w_gate, grad_w_up, grad_w_down = lax.map(expert_block, (token_buf, scaled_buf, w_gate, w_up, w_down))
    grad_back = jnp.take(grad_buf.reshape(limit, D), dest, axis=0, mode='fill', fill_value=0).reshape(TOKENS, TOP, D)
    output_back = jnp.take(output_buf.reshape(limit, D), dest, axis=0, mode='fill', fill_value=0).reshape(TOKENS, TOP, D)
    grad_gates = lax.optimization_barrier(jnp.sum(grad_out.astype(jnp.float32)[:, None, :] * output_back.astype(jnp.float32), axis=2)).astype(jnp.bfloat16)
    grad_filtered = lax.optimization_barrier(jnp.sum(grad_back.astype(jnp.float32), axis=1)).astype(jnp.bfloat16)
    seq_grad = grad_filtered.astype(jnp.float32).reshape(N_EXPERT, LENGTH, D)
    grad_padded = jnp.pad(seq_grad, ((0, 0), (0, TAPS - 1), (0, 0)))
    grad_inputs = anticausal_filter(grad_padded, taps_f).reshape(TOKENS, D).astype(jnp.bfloat16)

    def tap_grad(tap):
        window = lax.dynamic_slice_in_dim(padded, TAPS - 1 - tap, LENGTH, 1)
        return lax.optimization_barrier(jnp.sum(seq_grad * window, axis=(0, 1)))
    grad_filter = lax.map(tap_grad, jnp.arange(TAPS, dtype=jnp.int32))
    return (grad_inputs, grad_gates, grad_filter, grad_w_gate, grad_w_up, grad_w_down)
```

```python
import functools

import jax
import jax.numpy as jnp
import numpy as np
from jax import lax
from jax.experimental import pallas as pl
from jax.experimental.pallas import tpu as pltpu
from jax.sharding import PartitionSpec as P

MESH = pl.DeviceIdType.MESH
F32 = jnp.float32
BF16 = jnp.bfloat16


def from_behind(block, axis, distance):
    devices = range(lax.axis_size(axis))
    route = [(i - distance, i) for i in devices if i - distance in devices]
    return lax.ppermute(block, axis, route)


def depthwise(signal, kernel):
    return lax.conv_general_dilated(
        signal[None],
        kernel[:, None, :],
        (1,),
        "VALID",
        dimension_numbers=("NWC", "WIO", "NWC"),
        feature_group_count=signal.shape[1],
        preferred_element_type=jnp.float32,
    )[0]


def contract(left, right, left_dim, right_dim):
    return lax.dot_general(
        left, right, (((left_dim,), (right_dim,)), ((), ())), preferred_element_type=jnp.float32
    )


def expert_pass(token_rows, scaled_rows, gate_mat, up_mat, down_mat):
    pre_gate = jnp.dot(token_rows, gate_mat, preferred_element_type=jnp.float32)
    pre_up = jnp.dot(token_rows, up_mat, preferred_element_type=jnp.float32)
    sigma = jax.nn.sigmoid(pre_gate)
    swish = pre_gate * sigma
    hidden = (swish * pre_up).astype(jnp.bfloat16)
    outputs = jnp.dot(hidden, down_mat, preferred_element_type=jnp.float32).astype(jnp.bfloat16)
    grad_hidden = contract(scaled_rows, down_mat, 1, 1)
    grad_pre_gate = (grad_hidden * pre_up * (sigma * (1.0 + pre_gate * (1.0 - sigma)))).astype(
        jnp.bfloat16
    )
    grad_pre_up = (grad_hidden * swish).astype(jnp.bfloat16)
    part_gate = contract(token_rows, grad_pre_gate, 0, 0)
    part_up = contract(token_rows, grad_pre_up, 0, 0)
    part_down = contract(hidden, scaled_rows, 0, 0)
    grad_rows = (
        contract(grad_pre_gate, gate_mat, 1, 1) + contract(grad_pre_up, up_mat, 1, 1)
    ).astype(jnp.bfloat16)
    return (grad_rows, outputs, (part_gate, part_up, part_down))


def routed_body(inputs, grad_out, gates, expert_ids, slot_index, filter_taps, w_gate, w_up, w_down):
    tok_count, width = inputs.shape
    taps = filter_taps.shape[0]
    top_count = expert_ids.shape[1]
    experts = lax.axis_size("expert")
    capacity = tok_count * top_count // experts
    reach = taps - 1
    shift_count = (reach + tok_count - 1) // tok_count
    earlier = [from_behind(inputs, "seq", shift_by) for shift_by in range(shift_count, 0, -1)]
    extended = jnp.concatenate(earlier + [inputs], axis=0)[-(tok_count + reach) :]
    filtered = depthwise(extended, filter_taps[::-1]).astype(jnp.bfloat16)
    kept = slot_index < capacity
    dest = jnp.where(kept, expert_ids * capacity + slot_index, experts * capacity).reshape(-1)

    def place(values):
        rest = values.shape[1:]
        empty = jnp.zeros((experts * capacity,) + rest, values.dtype)
        return empty.at[dest].set(values, mode="drop").reshape((experts, capacity) + rest)

    def fetch(buffer):
        rest = buffer.shape[2:]
        flat = buffer.reshape((experts * capacity,) + rest)
        return jnp.take(flat, dest, axis=0, mode="fill", fill_value=0).reshape(
            (tok_count, top_count) + rest
        )

    token_send = place(
        jnp.broadcast_to(filtered[:, None, :], (tok_count, top_count, width)).reshape(-1, width)
    )
    gate_full, up_full, down_full = (
        lax.all_gather(w_gate, "seq", axis=1, tiled=True),
        lax.all_gather(w_up, "seq", axis=1, tiled=True),
        lax.all_gather(w_down, "seq", axis=1, tiled=True),
    )
    gate_mat = gate_full[0]
    up_mat = up_full[0]
    down_mat = down_full[0]
    scaled = (
        gates.astype(jnp.float32)[:, :, None] * grad_out.astype(jnp.float32)[:, None, :]
    ).astype(jnp.bfloat16)
    token_recv, scaled_recv = (
        lax.all_to_all(token_send, "expert", split_axis=0, concat_axis=0, tiled=True),
        lax.all_to_all(
            place(scaled.reshape(-1, width)), "expert", split_axis=0, concat_axis=0, tiled=True
        ),
    )
    grad_rows, outputs, partials = expert_pass(
        token_recv.reshape(-1, width), scaled_recv.reshape(-1, width), gate_mat, up_mat, down_mat
    )
    grad_back, output_back = (
        lax.all_to_all(
            grad_rows.reshape(experts, capacity, width),
            "expert",
            split_axis=0,
            concat_axis=0,
            tiled=True,
        ),
        lax.all_to_all(
            outputs.reshape(experts, capacity, width),
            "expert",
            split_axis=0,
            concat_axis=0,
            tiled=True,
        ),
    )
    output_rows = fetch(output_back)
    grad_gates = jnp.sum(
        grad_out.astype(jnp.float32)[:, None, :] * output_rows.astype(jnp.float32), axis=2
    ).astype(jnp.bfloat16)
    summed_gate, summed_up, summed_down = (
        lax.psum_scatter(
            partials[0][None].astype(jnp.bfloat16), "seq", scatter_dimension=1, tiled=True
        ).astype(jnp.float32),
        lax.psum_scatter(
            partials[1][None].astype(jnp.bfloat16), "seq", scatter_dimension=1, tiled=True
        ).astype(jnp.float32),
        lax.psum_scatter(
            partials[2][None].astype(jnp.bfloat16), "seq", scatter_dimension=1, tiled=True
        ).astype(jnp.float32),
    )
    grad_filtered = jnp.sum(fetch(grad_back).astype(jnp.float32), axis=1).astype(jnp.bfloat16)
    later = [from_behind(grad_filtered, "seq", -shift_by) for shift_by in range(1, shift_count + 1)]
    grad_extended = jnp.concatenate([grad_filtered] + later, axis=0)[: tok_count + reach]
    grad_inputs = depthwise(grad_extended, filter_taps).astype(jnp.bfloat16)
    local_taps = depthwise(extended, grad_filtered)[::-1]
    grad_filter = lax.psum(local_taps, ("expert", "seq"))
    return (
        grad_inputs,
        grad_gates,
        grad_filter,
        summed_gate.astype(jnp.bfloat16),
        summed_up.astype(jnp.bfloat16),
        summed_down.astype(jnp.bfloat16),
    )


def transforms(size):
    freq = 2.0 * np.pi * (np.arange(size // 2) + 0.5) / size
    angle = freq[:, None] * np.arange(size)[None, :]
    forward = np.concatenate([np.cos(angle), np.sin(angle)], axis=0)
    inverse = forward.T * (2.0 / size)

    def pieces(matrix):
        high = matrix.astype(jnp.bfloat16)
        low = (matrix - high.astype(np.float64)).astype(jnp.bfloat16)
        return high, low

    return pieces(forward) + pieces(inverse)


def mm(left, right):
    return jnp.dot(left, right, preferred_element_type=F32)


def turned(left, right):
    return lax.dot_general(left, right, (((1,), (1,)), ((), ())), preferred_element_type=F32)


def across(left, right):
    return lax.dot_general(left, right, (((0,), (0,)), ((), ())), preferred_element_type=F32)


PIECES = 6
PARTS = 4


def dense_kernel(
    rows_ref, cot_ref, gates_ref, ids_ref, slots_ref, wg_ref, wu_ref, wd_ref, taps_ref,
    fh_ref, fl_ref, ih_ref, il_ref,
    gin_ref, gg_ref, gf_ref, dgu_ref, dd_ref,
    fh, fl, ih, il, taps, x_spec, tap_spec, g_spec, seq_x, seq_f, seq_g, seq_in,
    tall, gall, wgu, wdn, hid, gpre, scaled, back, rall, pre_in, gfb,
    part, sib_in, pair, cross_in, gfz, gfz_in,
    weigh, sums, sums_in,
    load_sem, send_sem, recv_sem,
):
    z = lax.axis_index("expert")
    q = lax.axis_index("seq")
    tok, width = rows_ref.shape
    slab = width // 4
    ff = hid.shape[1]
    fq = ff // 4
    size = x_spec.shape[0]
    half = size // 2
    n_taps = taps.shape[0]
    piece = n_taps // 4
    length = 4 * tok
    sib = q + 1 - 2 * (q % 2)
    cross = (q + 2) % 4
    far = (sib + 2) % 4
    middle = jnp.logical_or(z == 1, z == 2)
    end = jnp.logical_or(z == 0, z == 3)

    barrier = pltpu.get_barrier_semaphore()
    for s in range(1, 4):
        pl.semaphore_signal(barrier, inc=1, device_id={"expert": (z + s) % 4}, device_id_type=MESH)
        pl.semaphore_signal(barrier, inc=1, device_id={"seq": (q + s) % 4}, device_id_type=MESH)

    def slab_at(k):
        return pl.ds(pl.multiple_of(k * slab, slab), slab)

    loads = [
        pltpu.make_async_copy(src, dst, load_sem.at[n])
        for n, (src, dst) in enumerate([
            (cot_ref, gall.at[z]),
            (rows_ref.at[:, slab_at(q)], seq_x.at[q]),
            (wg_ref.at[0], wgu.at[q, :, pl.ds(0, ff)]),
            (wu_ref.at[0], wgu.at[q, :, pl.ds(ff, ff)]),
            (wd_ref.at[0], wdn.at[q]),
            (taps_ref.at[:, slab_at(q)], taps),
            (fh_ref, fh), (fl_ref, fl), (ih_ref, ih), (il_ref, il),
        ])
    ]
    for load in loads:
        load.start()

    def link(n, src, dst, axis, peer, arrival=None):
        return pltpu.make_async_remote_copy(
            src_ref=src, dst_ref=dst, send_sem=send_sem.at[n],
            recv_sem=recv_sem.at[n if arrival is None else arrival],
            device_id={axis: peer}, device_id_type=MESH,
        )

    def pick(a, b, c, d):
        return jnp.where(z == 0, a, jnp.where(z == 1, b, jnp.where(z == 2, c, d)))

    def hop(base, view, origin, step):
        return link(
            base + (0 if step > 0 else 4) + origin, view(origin), view(origin),
            "expert", (z + 4 + step) % 4, base + origin,
        )

    def spread(base, view, distance, send=True):
        for step in (1, -1):
            origin = z - step * distance
            has_origin = origin >= 0 if step > 0 else origin <= 3
            has_next = z < 3 if step > 0 else z > 0

            @pl.when(has_origin)
            def _(origin=origin, has_next=has_next, step=step):
                if distance and send:
                    hop(base, view, origin, step).wait_recv()

                @pl.when(has_next)
                def _():
                    if send:
                        hop(base, view, origin, step).start()
                    else:
                        hop(base, view, origin, step).wait_send()

    def cot_of(origin):
        return gall.at[origin]

    def tok_of(origin):
        return tall.at[:, origin]

    G, T = 0, 8
    W, S, B, X, F, GS, GI, Z, A = 16, 20, 24, 28, 32, 36, 40, 44, 48
    C, R, Q, P, O = 52, 64, 72, 74, 80

    ids = ids_ref[...]
    kept = slots_ref[...] < tok
    held = jnp.where(kept, gates_ref[...].astype(F32), 0.0)
    eye = lax.broadcasted_iota(jnp.int32, (tok, tok), 0) == lax.broadcasted_iota(
        jnp.int32, (tok, tok), 1
    )

    def as_row(column):
        return jnp.sum(jnp.where(eye, column, 0.0), axis=0, keepdims=True)

    def as_column(row):
        return jnp.sum(jnp.where(eye, row, 0.0), axis=1, keepdims=True)

    weigh[z] = jnp.zeros(weigh.shape[1:], F32)
    for e in range(4):
        weigh[z, e:e + 1] = jnp.sum(jnp.where(ids == e, held, 0.0), axis=0, keepdims=True)

    @pl.when(end)
    def _():
        rall[pick(2, 0, 0, 1)] = jnp.zeros(rall.shape[1:], BF16)

    loads[0].wait()
    with jax.named_scope("entry"):
        pl.semaphore_wait(barrier, 6)

    spread(G, cot_of, 0)
    to_slabs = [
        link(X + s, rows_ref.at[:, slab_at((q + s) % 4)], seq_x.at[q], "seq", (q + s) % 4)
        for s in (2, 1, 3)
    ]
    for copy in to_slabs:
        copy.start()
    for load in loads[1:6]:
        load.wait()

    def piece_of(k, n):
        step = (slab + fq) // PIECES
        at = n * step
        if at < slab:
            return wgu.at[k, pl.ds(at, step)]
        return wdn.at[k, pl.ds(at - slab, step)]

    w_cross = [
        link(C + n, piece_of(q, n), piece_of(q, n), "seq", cross) for n in range(PIECES)
    ]
    w_far = [
        link(C + PIECES + n, piece_of(cross, n), piece_of(cross, n), "seq", sib)
        for n in range(PIECES)
    ]
    w_sib = [
        link(R, wgu.at[q], wgu.at[q], "seq", sib), link(R + 1, wdn.at[q], wdn.at[q], "seq", sib)
    ]
    w_cross[0].start()
    weighs = [
        link(W + s, weigh.at[z], weigh.at[z], "expert", (z + s) % 4, W + z + O) for s in range(1, 4)
    ]
    for copy in weighs + w_sib:
        copy.start()

    def forward(dest, count, values):
        for at in range(0, size, slab):
            span = pl.ds(at, slab)
            dest[span] = mm(fh[span, :count], values) + mm(fl[span, :count], values)

    def backward(count, spec):
        high = spec.astype(BF16)
        low = (spec - high.astype(F32)).astype(BF16)
        return mm(ih[:count], high) + mm(il[:count], high) + mm(ih[:count], low)

    def whole(ref):
        return ref[...].reshape(length, slab)

    for load in loads[6:]:
        load.wait()
    with jax.named_scope("tap spectrum"):
        forward(tap_spec, n_taps, taps[...])
    with jax.named_scope("x wait"):
        for copy in to_slabs:
            copy.wait_recv()
    with jax.named_scope("filter"):
        forward(x_spec, length, whole(seq_x))
        xc, xs = x_spec[:half], x_spec[half:]
        hc, hs = tap_spec[:half], tap_spec[half:]
        prod = jnp.concatenate([xc * hc - xs * hs, xc * hs + xs * hc], axis=0)
        seq_f[...] = backward(length, prod).astype(BF16).reshape(4, tok, slab)
    to_rows = [
        link(F + s, seq_f.at[(q + s) % 4], tall.at[q, z], "seq", (q + s) % 4) for s in (2, 1, 3)
    ]
    for copy in to_rows:
        copy.start()
    tall[q, z] = seq_f[q]
    for copy in w_cross[1:]:
        copy.start()
    with jax.named_scope("cot 1"):
        spread(G, cot_of, 1)
    with jax.named_scope("rows wait"):
        for copy in to_rows:
            copy.wait_recv()
    spread(T, tok_of, 0)
    with jax.named_scope("cot 2"):
        spread(G, cot_of, 2)
    with jax.named_scope("weigh wait"):
        for k in range(1, 4):
            peer = (z + k) % 4
            link(W + k, weigh.at[peer], weigh.at[peer], "expert", peer, W + peer + O).wait_recv()
    with jax.named_scope("rows 1"):
        spread(T, tok_of, 1)
    with jax.named_scope("weights wait"):
        for n in range(PIECES):
            w_cross[n].wait_recv()
            w_far[n].start()
        for copy in w_sib + w_far:
            copy.wait_recv()

    origins = [z, pick(1, 3, 0, 2), pick(2, 2, 1, 1), pick(3, 0, 3, 0)]
    peers = [z, pick(1, 2, 1, 2), pick(2, 2, 1, 1), pick(3, 0, 3, 0)]
    sublanes = lax.broadcasted_iota(jnp.int32, weigh.shape[1:], 0)
    gate_sums = [
        link(S + s, sums.at[s], sums_in.at[z], "expert", origins[s], S + z + O) for s in range(1, 4)
    ]
    backs = [
        link(B + s, back.at[s], rall.at[z], "expert", peers[s], B + z + O) for s in range(1, 4)
    ]
    to_pre = link(B + 1, back.at[1], pre_in, "expert", 3 - z, B + O + 4)

    def block(s):
        origin = origins[s]
        span = pl.ds(pl.multiple_of(origin * tok, tok), tok)
        pre = mm(tall[0, origin], wgu[0])
        for k in range(1, 4):
            pre += mm(tall[k, origin], wgu[k])
        cot = gall[origin]
        weight = as_column(
            jnp.sum(jnp.where(sublanes == z, weigh[origin], 0.0), axis=0, keepdims=True)
        )
        raw = turned(cot, wdn[...].reshape(ff, width))
        gate, up = pre[:, :ff], pre[:, ff:]
        sigma = jax.nn.sigmoid(gate)
        swish = gate * sigma
        hidden = (swish * up).astype(BF16)
        gg = jnp.sum(hidden.astype(F32) * raw, axis=1, keepdims=True)
        grad_hidden = raw * weight
        grad_gate = grad_hidden * up * (sigma * (1.0 + gate * (1.0 - sigma)))
        gp = jnp.concatenate([grad_gate.astype(BF16), (grad_hidden * swish).astype(BF16)], axis=1)
        hid[span] = hidden
        gpre[span] = gp
        scaled[span] = (weight * cot.astype(F32)).astype(BF16)
        target, at = (back, s) if s else (rall, z)
        for k in range(4):
            target[at, k] = turned(gp, wgu[k]).astype(BF16)
        (sums if s else sums_in)[at] = jnp.broadcast_to(as_row(gg), sums.shape[1:])

    with jax.named_scope("block 0"):
        block(0)

    @pl.when(middle)
    def _():
        with jax.named_scope("rows 2 middle"):
            spread(T, tok_of, 2)

    with jax.named_scope("block 1"):
        block(1)
    gate_sums[0].start()

    @pl.when(middle)
    def _():
        to_pre.start()

    @pl.when(end)
    def _():
        backs[0].start()
        with jax.named_scope("rows 2 end"):
            spread(T, tok_of, 2)

    with jax.named_scope("block 2"):
        block(2)
    gate_sums[1].start()
    backs[1].start()

    @pl.when(end)
    def _():
        with jax.named_scope("rows 3"):
            spread(G, cot_of, 3)
            spread(T, tok_of, 3)

    with jax.named_scope("block 3"):
        block(3)
    gate_sums[2].start()

    @pl.when(end)
    def _():
        backs[2].start()

    def partial(slot, dest):
        thin = pl.ds(pl.multiple_of(dest * fq, fq), fq)
        top = across(tall[dest].reshape(length, slab), gpre[...])
        part[slot, :slab] = top.astype(BF16)
        part[slot, slab:] = across(hid[:, thin], scaled[...]).astype(BF16)

    to_sib = [link(Q + n, part.at[n], sib_in.at[n], "seq", sib) for n in range(2)]
    rows = slab + fq
    share = rows // PARTS
    to_cross = [
        link(
            P + n, pair.at[pl.ds(n * share, share)], cross_in.at[pl.ds(n * share, share)],
            "seq", cross,
        )
        for n in range(PARTS)
    ]
    with jax.named_scope("partial 0"):
        partial(0, far)
    to_sib[0].start()
    with jax.named_scope("partial 2"):
        partial(2, cross)
    to_sib[0].wait_recv()
    pair[...] = (part[2].astype(F32) + sib_in[0].astype(F32)).astype(BF16)
    to_cross[0].start()
    to_cross[1].start()
    with jax.named_scope("partial 1"):
        partial(1, sib)
    to_sib[1].start()
    with jax.named_scope("partial 3"):
        partial(3, q)

    @pl.when(middle)
    def _():
        with jax.named_scope("pre wait"):
            to_pre.wait_recv()
        back[3] = (back[3].astype(F32) + pre_in[...].astype(F32)).astype(BF16)
        backs[2].start()

    with jax.named_scope("back wait"):
        for s in range(1, 4):
            peer = (z + s) % 4

            @pl.when(jnp.logical_or(middle, peer != pick(2, 0, 0, 1)))
            def _(peer=peer):
                link(B + 1, back.at[1], rall.at[peer], "expert", peer, B + peer + O).wait_recv()

    total = rall[0].astype(F32)
    for s in range(1, 4):
        total += rall[s].astype(F32)
    gfb[...] = total.astype(BF16)
    seq_g[q] = gfb[q]
    g_slabs = [
        link(GS + s, gfb.at[(q + s) % 4], seq_g.at[q], "seq", (q + s) % 4) for s in (2, 1, 3)
    ]
    for copy in g_slabs:
        copy.start()
    to_cross[2].start()

    for s in range(1, 4):
        peer = (z + s) % 4
        link(S + s, sums.at[s], sums_in.at[peer], "expert", peer, S + peer + O).wait_recv()
    gate_grads = jnp.zeros(ids.shape, F32)
    for s in range(4):
        gate_grads += jnp.where(ids == s, sums_in[s, 0:1], 0.0)
    gg_ref[...] = jnp.where(kept, gate_grads, 0.0).astype(BF16)

    with jax.named_scope("grad wait"):
        for copy in g_slabs:
            copy.wait_recv()
    with jax.named_scope("tap grad"):
        forward(g_spec, length, whole(seq_g))
        gc, gs = g_spec[:half], g_spec[half:]
        xc, xs = x_spec[:half], x_spec[half:]
        prod = jnp.concatenate([gc * xc + gs * xs, gs * xc - gc * xs], axis=0)
        gfz[...] = backward(n_taps, prod).astype(BF16).reshape(4, piece, slab)
    gf_exp = [
        link(Z + s, gfz.at[(z + s) % 4], gfz_in.at[s], "expert", (z + s) % 4) for s in range(1, 4)
    ]
    for copy in gf_exp:
        copy.start()
    with jax.named_scope("input grad"):
        gc, gs = g_spec[:half], g_spec[half:]
        hc, hs = tap_spec[:half], tap_spec[half:]
        prod = jnp.concatenate([gc * hc + gs * hs, gs * hc - gc * hs], axis=0)
        seq_in[...] = backward(length, prod).astype(BF16).reshape(4, tok, slab)
    gin_out = [
        link(GI + s, seq_in.at[(q + s) % 4], gin_ref.at[q], "seq", (q + s) % 4) for s in (2, 1, 3)
    ]
    for copy in gin_out:
        copy.start()
    gin_ref[q] = seq_in[q]
    to_cross[3].start()

    with jax.named_scope("taps z wait"):
        for copy in gf_exp:
            copy.wait_recv()
    mine = gfz[z].astype(F32)
    for s in range(1, 4):
        mine += gfz_in[s].astype(F32)
    gf_ref[q, z] = mine.astype(BF16)
    gf_out = [
        link(A + s, gf_ref.at[q, z], gf_ref.at[q, z], "expert", (z + s) % 4) for s in range(1, 4)
    ]
    for copy in gf_out:
        copy.start()
    with jax.named_scope("taps out wait"):
        for copy in gf_out:
            copy.wait_recv()
    gf_last = [
        link(R + 2, gf_ref.at[q], gf_ref.at[q], "seq", cross),
        link(R + 3, gf_ref.at[q], gf_ref.at[q], "seq", sib),
    ]
    for copy in gf_last:
        copy.start()
    with jax.named_scope("taps cross wait"):
        gf_last[0].wait_recv()
    gf_last.append(link(R + 4, gf_ref.at[cross], gf_ref.at[cross], "seq", sib))
    gf_last[2].start()

    to_sib[1].wait_recv()
    with jax.named_scope("pair wait"):
        for copy in to_cross:
            copy.wait_recv()
    with jax.named_scope("weight sums"):
        dgu_ref[...] = (
            part[3, :slab].astype(F32) + sib_in[1, :slab].astype(F32) + cross_in[:slab].astype(F32)
        ).astype(BF16)
        dd_ref[...] = (
            part[3, slab:].astype(F32) + sib_in[1, slab:].astype(F32) + cross_in[slab:].astype(F32)
        ).astype(BF16)
    with jax.named_scope("last waits"):
        for copy in gin_out:
            copy.wait_recv()
        for copy in gf_last[1:]:
            copy.wait_recv()
        for d in range(3):
            spread(G, cot_of, d, False)
            spread(T, tok_of, d, False)

        @pl.when(middle)
        def _():
            to_pre.wait_send()

        @pl.when(end)
        def _():
            backs[0].wait_send()

        for copy in (
            to_slabs + w_cross + w_far + w_sib + weighs + to_rows + gate_sums + backs[1:] + to_sib
            + to_cross + g_slabs + gf_exp + gin_out + gf_out + gf_last
        ):
            copy.wait_send()


def finish_kernel(
    gin_ref, gg_ref, gf_ref, dgu_ref, dd_ref,
    gin_out, gg_out, gf_out, dg_out, du_out, dd_out, wide, sem,
):
    slab = gin_ref.shape[2]
    ff = dg_out.shape[2]
    copies = [
        (gin_ref.at[k], gin_out.at[:, pl.ds(k * slab, slab)]) for k in range(4)
    ] + [
        (dgu_ref.at[:, pl.ds(0, ff)], dg_out.at[0]), (dgu_ref.at[:, pl.ds(ff, ff)], du_out.at[0]),
        (dd_ref, dd_out.at[0]), (gg_ref, gg_out),
    ]
    copies = [pltpu.make_async_copy(a, b, sem.at[n]) for n, (a, b) in enumerate(copies)]
    for copy in copies:
        copy.start()
    piece = gf_ref.shape[2]
    for a in range(4):
        span = pl.ds(a * piece, piece)
        for k in range(4):
            wide[span, pl.ds(k * slab, slab)] = gf_ref[k, a].astype(F32)
        copies.append(pltpu.make_async_copy(wide.at[span], gf_out.at[span], sem.at[8 + a]))
        copies[-1].start()
    for copy in copies:
        copy.wait()


def dense_body(inputs, grad_out, gates, expert_ids, slot_index, filter_taps, w_gate, w_up, w_down):
    tok, width = inputs.shape
    taps = filter_taps.shape[0]
    ff = w_gate.shape[2]
    top = gates.shape[1]
    length = 4 * tok
    size = taps + length
    slab = width // 4
    rows = slab + ff // 4
    vm = lambda *shape: pltpu.VMEM(shape, BF16)
    vf = lambda *shape: pltpu.VMEM(shape, F32)
    st = lambda *shape: jax.ShapeDtypeStruct(shape, BF16)
    near = pl.BlockSpec(memory_space=pltpu.VMEM)
    hbm = pl.BlockSpec(memory_space=pltpu.HBM)
    far_away = lambda array: pltpu.with_memory_space_constraint(array, pltpu.HBM)
    fh, fl, ih, il = transforms(size)
    outs = pl.pallas_call(
        dense_kernel,
        out_shape=(
            vm(4, tok, slab), vm(top, tok), vm(4, 4, taps // 4, slab), vm(slab, 2 * ff),
            vm(ff // 4, width),
        ),
        in_specs=[hbm] * 2 + [near] * 3 + [hbm] * 8,
        out_specs=(near,) * 5,
        scratch_shapes=[
            vm(size, length), vm(size, length), vm(length, size), vm(length, size), vm(taps, slab),
            vf(size, slab), vf(size, slab), vf(size, slab),
            vm(4, tok, slab), vm(4, tok, slab), vm(4, tok, slab), vm(4, tok, slab),
            vm(4, 4, tok, slab), vm(4, tok, width), vm(4, slab, 2 * ff), vm(4, ff // 4, width),
            vm(length, ff), vm(length, 2 * ff), vm(length, width),
            vm(4, 4, tok, slab), vm(4, 4, tok, slab), vm(4, tok, slab), vm(4, tok, slab),
            vm(4, rows, width), vm(2, rows, width), vm(rows, width), vm(rows, width),
            vm(4, taps // 4, slab), vm(4, taps // 4, slab),
            vf(4, 8, tok), vf(4, 8, tok), vf(4, 8, tok),
            pltpu.SemaphoreType.DMA((10,)),
            pltpu.SemaphoreType.DMA((80,)), pltpu.SemaphoreType.DMA((112,)),
        ],
        compiler_params=pltpu.CompilerParams(
            collective_id=0, has_side_effects=True, vmem_limit_bytes=48 * 1024 * 1024
        ),
    )(
        far_away(inputs), far_away(grad_out), gates.T, expert_ids.T, slot_index.T,
        *[far_away(m) for m in (w_gate, w_up, w_down, filter_taps)],
        *[far_away(jnp.asarray(m)) for m in (fh[:, :length], fl[:, :length], ih[:length], il[:length])],
    )
    grads = pl.pallas_call(
        finish_kernel,
        out_shape=(
            st(tok, width), st(top, tok), jax.ShapeDtypeStruct((taps, width), F32),
            st(*w_gate.shape), st(*w_up.shape), st(*w_down.shape),
        ),
        in_specs=[near] * 5,
        out_specs=(hbm,) * 6,
        scratch_shapes=[vf(taps, width), pltpu.SemaphoreType.DMA((12,))],
        compiler_params=pltpu.CompilerParams(vmem_limit_bytes=8 * 1024 * 1024),
    )(*[pltpu.with_memory_space_constraint(array, pltpu.VMEM) for array in outs])
    return (grads[0], grads[1].T) + grads[2:]


def body_of(mesh):
    def body(*args):
        top_count = args[3].shape[1]
        tok, taps, dq = args[0].shape[0], args[5].shape[0], args[6].shape[1]
        small = mesh.shape["expert"] == top_count == 4 and mesh.shape["seq"] == 4
        if small and tok == 128 and taps == 2 * tok and dq == 2 * tok and 2 * args[6].shape[2] == args[0].shape[1]:
            return dense_body(*args)
        return routed_body(*args)

    return body


def solution(mesh):
    return jax.shard_map(
        body_of(mesh),
        mesh=mesh,
        in_specs=(
            P(("groups", "expert", "seq"), None),
            P(("groups", "expert", "seq"), None),
            P(("groups", "expert", "seq"), None),
            P(("groups", "expert", "seq"), None),
            P(("groups", "expert", "seq"), None),
            P(),
            P("expert", "seq", None),
            P("expert", "seq", None),
            P("expert", "seq", None),
        ),
        out_specs=(
            P(("groups", "expert", "seq"), None),
            P(("groups", "expert", "seq"), None),
            P("groups", None),
            P(("groups", "expert"), "seq", None),
            P(("groups", "expert"), "seq", None),
            P(("groups", "expert"), "seq", None),
        ),
        check_vma=False,
    )
```

```python
import functools

import jax
import jax.numpy as jnp
import numpy as np
from jax import lax
from jax.experimental import pallas as pl
from jax.experimental.pallas import tpu as pltpu
from jax.sharding import PartitionSpec as P

MESH = pl.DeviceIdType.MESH
F32 = jnp.float32
BF16 = jnp.bfloat16


def from_behind(block, axis, distance):
    devices = range(lax.axis_size(axis))
    route = [(i - distance, i) for i in devices if i - distance in devices]
    return lax.ppermute(block, axis, route)


def depthwise(signal, kernel):
    return lax.conv_general_dilated(
        signal[None],
        kernel[:, None, :],
        (1,),
        "VALID",
        dimension_numbers=("NWC", "WIO", "NWC"),
        feature_group_count=signal.shape[1],
        preferred_element_type=jnp.float32,
    )[0]


def contract(left, right, left_dim, right_dim):
    return lax.dot_general(
        left, right, (((left_dim,), (right_dim,)), ((), ())), preferred_element_type=jnp.float32
    )


def expert_pass(token_rows, scaled_rows, gate_mat, up_mat, down_mat):
    pre_gate = jnp.dot(token_rows, gate_mat, preferred_element_type=jnp.float32)
    pre_up = jnp.dot(token_rows, up_mat, preferred_element_type=jnp.float32)
    sigma = jax.nn.sigmoid(pre_gate)
    swish = pre_gate * sigma
    hidden = (swish * pre_up).astype(jnp.bfloat16)
    outputs = jnp.dot(hidden, down_mat, preferred_element_type=jnp.float32).astype(jnp.bfloat16)
    grad_hidden = contract(scaled_rows, down_mat, 1, 1)
    grad_pre_gate = (grad_hidden * pre_up * (sigma * (1.0 + pre_gate * (1.0 - sigma)))).astype(
        jnp.bfloat16
    )
    grad_pre_up = (grad_hidden * swish).astype(jnp.bfloat16)
    part_gate = contract(token_rows, grad_pre_gate, 0, 0)
    part_up = contract(token_rows, grad_pre_up, 0, 0)
    part_down = contract(hidden, scaled_rows, 0, 0)
    grad_rows = (
        contract(grad_pre_gate, gate_mat, 1, 1) + contract(grad_pre_up, up_mat, 1, 1)
    ).astype(jnp.bfloat16)
    return (grad_rows, outputs, (part_gate, part_up, part_down))


def routed_body(inputs, grad_out, gates, expert_ids, slot_index, filter_taps, w_gate, w_up, w_down):
    tok_count, width = inputs.shape
    taps = filter_taps.shape[0]
    top_count = expert_ids.shape[1]
    experts = lax.axis_size("expert")
    capacity = tok_count * top_count // experts
    reach = taps - 1
    shift_count = (reach + tok_count - 1) // tok_count
    earlier = [from_behind(inputs, "seq", shift_by) for shift_by in range(shift_count, 0, -1)]
    extended = jnp.concatenate(earlier + [inputs], axis=0)[-(tok_count + reach) :]
    filtered = depthwise(extended, filter_taps[::-1]).astype(jnp.bfloat16)
    kept = slot_index < capacity
    dest = jnp.where(kept, expert_ids * capacity + slot_index, experts * capacity).reshape(-1)

    def place(values):
        rest = values.shape[1:]
        empty = jnp.zeros((experts * capacity,) + rest, values.dtype)
        return empty.at[dest].set(values, mode="drop").reshape((experts, capacity) + rest)

    def fetch(buffer):
        rest = buffer.shape[2:]
        flat = buffer.reshape((experts * capacity,) + rest)
        return jnp.take(flat, dest, axis=0, mode="fill", fill_value=0).reshape(
            (tok_count, top_count) + rest
        )

    token_send = place(
        jnp.broadcast_to(filtered[:, None, :], (tok_count, top_count, width)).reshape(-1, width)
    )
    gate_full, up_full, down_full = (
        lax.all_gather(w_gate, "seq", axis=1, tiled=True),
        lax.all_gather(w_up, "seq", axis=1, tiled=True),
        lax.all_gather(w_down, "seq", axis=1, tiled=True),
    )
    gate_mat = gate_full[0]
    up_mat = up_full[0]
    down_mat = down_full[0]
    scaled = (
        gates.astype(jnp.float32)[:, :, None] * grad_out.astype(jnp.float32)[:, None, :]
    ).astype(jnp.bfloat16)
    token_recv, scaled_recv = (
        lax.all_to_all(token_send, "expert", split_axis=0, concat_axis=0, tiled=True),
        lax.all_to_all(
            place(scaled.reshape(-1, width)), "expert", split_axis=0, concat_axis=0, tiled=True
        ),
    )
    grad_rows, outputs, partials = expert_pass(
        token_recv.reshape(-1, width), scaled_recv.reshape(-1, width), gate_mat, up_mat, down_mat
    )
    grad_back, output_back = (
        lax.all_to_all(
            grad_rows.reshape(experts, capacity, width),
            "expert",
            split_axis=0,
            concat_axis=0,
            tiled=True,
        ),
        lax.all_to_all(
            outputs.reshape(experts, capacity, width),
            "expert",
            split_axis=0,
            concat_axis=0,
            tiled=True,
        ),
    )
    output_rows = fetch(output_back)
    grad_gates = jnp.sum(
        grad_out.astype(jnp.float32)[:, None, :] * output_rows.astype(jnp.float32), axis=2
    ).astype(jnp.bfloat16)
    summed_gate, summed_up, summed_down = (
        lax.psum_scatter(
            partials[0][None].astype(jnp.bfloat16), "seq", scatter_dimension=1, tiled=True
        ).astype(jnp.float32),
        lax.psum_scatter(
            partials[1][None].astype(jnp.bfloat16), "seq", scatter_dimension=1, tiled=True
        ).astype(jnp.float32),
        lax.psum_scatter(
            partials[2][None].astype(jnp.bfloat16), "seq", scatter_dimension=1, tiled=True
        ).astype(jnp.float32),
    )
    grad_filtered = jnp.sum(fetch(grad_back).astype(jnp.float32), axis=1).astype(jnp.bfloat16)
    later = [from_behind(grad_filtered, "seq", -shift_by) for shift_by in range(1, shift_count + 1)]
    grad_extended = jnp.concatenate([grad_filtered] + later, axis=0)[: tok_count + reach]
    grad_inputs = depthwise(grad_extended, filter_taps).astype(jnp.bfloat16)
    local_taps = depthwise(extended, grad_filtered)[::-1]
    grad_filter = lax.psum(local_taps, ("expert", "seq"))
    return (
        grad_inputs,
        grad_gates,
        grad_filter,
        summed_gate.astype(jnp.bfloat16),
        summed_up.astype(jnp.bfloat16),
        summed_down.astype(jnp.bfloat16),
    )


def transforms(size):
    freq = 2.0 * np.pi * (np.arange(size // 2) + 0.5) / size
    angle = freq[:, None] * np.arange(size)[None, :]
    forward = np.concatenate([np.cos(angle), np.sin(angle)], axis=0)
    inverse = forward.T * (2.0 / size)

    def pieces(matrix):
        high = matrix.astype(jnp.bfloat16)
        low = (matrix - high.astype(np.float64)).astype(jnp.bfloat16)
        return high, low

    return pieces(forward) + pieces(inverse)


def mm(left, right):
    return jnp.dot(left, right, preferred_element_type=F32)


def turned(left, right):
    return lax.dot_general(left, right, (((1,), (1,)), ((), ())), preferred_element_type=F32)


def across(left, right):
    return lax.dot_general(left, right, (((0,), (0,)), ((), ())), preferred_element_type=F32)


PIECES = 3
PARTS = 8


def dense_kernel(
    rows_ref, cot_ref, gates_ref, ids_ref, slots_ref, wg_ref, wu_ref, wd_ref, taps_ref,
    fh_ref, fl_ref, ih_ref, il_ref,
    gin_ref, gg_ref, gf_ref, dgu_ref, dd_ref,
    gates_in, ids_in, slots_in, fh, fl, ih, il, taps, x_spec, tap_spec, g_spec, seq_x, seq_f, seq_g, seq_in,
    tall, gall, wgu, wdn, hid, gpre, scaled, back, rall, pre_in, gfb,
    part, sib_in, pair, cross_in, gfz, gfz_in,
    weigh, sums, sums_in,
    load_sem, send_sem, recv_sem,
):
    g = lax.axis_index("groups")
    z = lax.axis_index("expert")
    q = lax.axis_index("seq")
    tok, width = rows_ref.shape
    slab = width // 4
    ff = hid.shape[1]
    fq = ff // 4
    size = x_spec.shape[0]
    half = size // 2
    n_taps = taps.shape[0]
    piece = n_taps // 4
    length = 4 * tok
    sib = q + 1 - 2 * (q % 2)
    cross = (q + 2) % 4
    far = (sib + 2) % 4
    middle = jnp.logical_or(z == 1, z == 2)
    end = jnp.logical_or(z == 0, z == 3)

    barrier = pltpu.get_barrier_semaphore()
    for s in range(1, 4):
        pl.semaphore_signal(barrier, inc=1, device_id={"expert": (z + s) % 4}, device_id_type=MESH)
        pl.semaphore_signal(barrier, inc=1, device_id={"seq": (q + s) % 4}, device_id_type=MESH)
    pl.semaphore_signal(barrier, inc=1, device_id={"groups": 1 - g}, device_id_type=MESH)

    def slab_at(k):
        return pl.ds(pl.multiple_of(k * slab, slab), slab)

    loads = [
        pltpu.make_async_copy(src, dst, load_sem.at[n])
        for n, (src, dst) in enumerate([
            (cot_ref, gall.at[z]),
            (gates_ref, gates_in), (ids_ref, ids_in), (slots_ref, slots_in),
            (rows_ref.at[:, slab_at(q)], seq_x.at[q]),
            (wg_ref.at[0], wgu.at[q, :, pl.ds(0, ff)]),
            (wu_ref.at[0], wgu.at[q, :, pl.ds(ff, ff)]),
            (wd_ref.at[0], wdn.at[q]),
            (taps_ref.at[:, slab_at(q)], taps),
            (fh_ref, fh), (fl_ref, fl), (ih_ref, ih), (il_ref, il),
        ])
    ]
    for load in loads:
        load.start()

    def link(n, src, dst, axis, peer, arrival):
        return pltpu.make_async_remote_copy(
            src_ref=src, dst_ref=dst, send_sem=send_sem.at[n],
            recv_sem=recv_sem.at[arrival],
            device_id={axis: peer}, device_id_type=MESH,
        )

    def pick(a, b, c, d):
        return jnp.where(z == 0, a, jnp.where(z == 1, b, jnp.where(z == 2, c, d)))

    GATHER, WEIGH, SUM, BACK, SLAB, ROW, TAP, OUT = 0, 24, 27, 30, 33, 36, 39, 42
    WEIGHT, SIB, HALF, PART, LAST = 45, 57, 59, 61, 69
    GATHERED, WEIGHED, SUMMED, BACKED, SLABBED, ROWED, TAPPED, OUTED = 0, 16, 20, 24, 30, 33, 36, 39
    WEIGHTED, SIBBED, HALVED, PARTED, LASTED = 43, 55, 57, 59, 67

    def hop(base, view, origin, step, distance):
        return link(
            GATHER + 6 * base + (0 if step > 0 else 3) + distance, view(origin), view(origin),
            "expert", (z + 4 + step) % 4, GATHERED + 4 * base + origin,
        )

    def spread(base, view, distance, send=True):
        for step in (1, -1):
            origin = z - step * distance
            has_origin = origin >= 0 if step > 0 else origin <= 3
            has_next = z < 3 if step > 0 else z > 0

            @pl.when(has_origin)
            def _(origin=origin, has_next=has_next, step=step):
                if distance and send:
                    hop(base, view, origin, step, 0).wait_recv()

                if distance < 3:
                    @pl.when(has_next)
                    def _():
                        if send:
                            hop(base, view, origin, step, distance).start()
                        else:
                            hop(base, view, origin, step, distance).wait_send()

    def cot_ahead(distance, first, last=2):
        for part in range(first, last):
            spread(part, cot_of(part), distance)

    def rows_ahead(distance, first, last=2):
        for part in range(first, last):
            spread(2 + part, tok_of(part), distance)

    def cot_of(part):
        return lambda origin: gall.at[origin, pl.ds(part * (tok // 2), tok // 2)]

    def tok_of(part):
        return lambda origin: tall.at[:, origin, pl.ds(part * (tok // 2), tok // 2)]

    for load in loads[:4]:
        load.wait()
    ids = ids_in[...]
    kept = slots_in[...] < tok
    held = jnp.where(kept, gates_in[...].astype(F32), 0.0)
    eye = lax.broadcasted_iota(jnp.int32, (tok, tok), 0) == lax.broadcasted_iota(
        jnp.int32, (tok, tok), 1
    )

    def as_row(column):
        return jnp.sum(jnp.where(eye, column, 0.0), axis=0, keepdims=True)

    def as_column(row):
        return jnp.sum(jnp.where(eye, row, 0.0), axis=1, keepdims=True)

    weigh[z] = jnp.zeros(weigh.shape[1:], F32)
    for e in range(4):
        weigh[z, e:e + 1] = jnp.sum(jnp.where(ids == e, held, 0.0), axis=0, keepdims=True)

    with jax.named_scope("entry"):
        pl.semaphore_wait(barrier, 7)

    cot_ahead(0, 0)

    def to_others(send, arrive, source, dest):
        return [
            link(send + s, source((q + s) % 4), dest, "seq", (q + s) % 4, arrive + s)
            for s in (2, 1, 3)
        ]

    to_slabs = to_others(
        SLAB - 1, SLABBED - 1, lambda k: rows_ref.at[:, slab_at(k)], seq_x.at[q]
    )
    for copy in to_slabs:
        copy.start()
    for load in loads[4:9]:
        load.wait()

    step = (slab + fq) // (2 * PIECES)
    wide_pieces = slab // (2 * step)

    def piece_of(k, n, part):
        if n < wide_pieces:
            return wgu.at[k, pl.ds(pl.multiple_of((2 * n + part) * step, step), step)]
        at = pl.multiple_of((2 * (n - wide_pieces) + part) * step, step)
        return wdn.at[k, pl.ds(at, step)]

    def weight_copy(kind, source, n, part, axis, peer):
        at = kind * PIECES + n
        return link(
            WEIGHT + at, piece_of(source, n, part), piece_of(source, n, part), axis, peer,
            WEIGHTED + at,
        )

    w_cross = [weight_copy(0, q, n, g, "seq", cross) for n in range(PIECES)]
    w_group = [weight_copy(1, cross, n, g, "groups", 1 - g) for n in range(PIECES)]
    w_far = [
        [weight_copy(2 + h, cross, n, (g + h) % 2, "seq", sib) for n in range(PIECES)]
        for h in range(2)
    ]

    def pass_on(n):
        w_cross[n].wait_recv()
        w_group[n].start()
        w_far[0][n].start()

    def take(n):
        w_group[n].wait_recv()
        w_far[1][n].start()

    w_sib = [
        link(SIB, wgu.at[q], wgu.at[q], "seq", sib, SIBBED),
        link(SIB + 1, wdn.at[q], wdn.at[q], "seq", sib, SIBBED + 1),
    ]
    weighs = [
        link(WEIGH + s - 1, weigh.at[z], weigh.at[z], "expert", (z + s) % 4, WEIGHED + z)
        for s in range(1, 4)
    ]
    for copy in weighs + w_sib:
        copy.start()

    def forward(dest, count, values):
        for at in range(0, size, slab):
            span = pl.ds(at, slab)
            dest[span] = mm(fh[span, :count], values) + mm(fl[span, :count], values)

    def backward(count, spec):
        high = spec.astype(BF16)
        low = (spec - high.astype(F32)).astype(BF16)
        return mm(ih[:count], high) + mm(il[:count], high) + mm(ih[:count], low)

    def whole(ref):
        return ref[...].reshape(length, slab)

    for load in loads[9:]:
        load.wait()
    with jax.named_scope("tap spectrum"):
        forward(tap_spec, n_taps, taps[...])
    with jax.named_scope("x wait"):
        for copy in to_slabs:
            copy.wait_recv()
    w_cross[0].start()
    with jax.named_scope("cot 1 first"):
        cot_ahead(1, 0, 1)
    with jax.named_scope("filter"):
        forward(x_spec, length, whole(seq_x))
        xc, xs = x_spec[:half], x_spec[half:]
        hc, hs = tap_spec[:half], tap_spec[half:]
        prod = jnp.concatenate([xc * hc - xs * hs, xc * hs + xs * hc], axis=0)
        seq_f[...] = backward(length, prod).astype(BF16).reshape(4, tok, slab)
    to_rows = to_others(ROW - 1, ROWED - 1, lambda k: seq_f.at[k], tall.at[q, z])
    for copy in to_rows + w_cross[1:]:
        copy.start()
    tall[q, z] = seq_f[q]
    with jax.named_scope("cot 1"):
        cot_ahead(1, 1)
    with jax.named_scope("rows wait"):
        for copy in to_rows:
            copy.wait_recv()
    rows_ahead(0, 0)
    with jax.named_scope("pass 0"):
        pass_on(0)
    with jax.named_scope("pass 1"):
        pass_on(1)

    @pl.when(middle)
    def _():
        with jax.named_scope("rows 1 first"):
            rows_ahead(1, 0, 1)

    with jax.named_scope("pass 2"):
        pass_on(2)
    with jax.named_scope("take 0"):
        take(0)

    @pl.when(middle)
    def _():
        with jax.named_scope("rows 1"):
            rows_ahead(1, 1)
        with jax.named_scope("cot 2"):
            cot_ahead(2, 0)

    with jax.named_scope("take 1"):
        take(1)
    with jax.named_scope("weigh wait"):
        for k in range(1, 4):
            peer = (z + k) % 4
            link(WEIGH, weigh.at[peer], weigh.at[peer], "expert", peer, WEIGHED + peer).wait_recv()

    @pl.when(middle)
    def _():
        with jax.named_scope("rows 2 middle first"):
            rows_ahead(2, 0, 1)

    with jax.named_scope("take 2"):
        take(2)
    with jax.named_scope("weights wait"):
        for copy in w_sib + w_far[0] + w_far[1]:
            copy.wait_recv()

    origins = [z, pick(2, 3, 0, 1), pick(1, 0, 3, 2), pick(3, 2, 1, 0)]
    sublanes = lax.broadcasted_iota(jnp.int32, weigh.shape[1:], 0)
    gate_sums = [
        link(SUM + s - 1, sums.at[s], sums_in.at[z], "expert", origins[s], SUMMED + z)
        for s in range(1, 4)
    ]
    backs = [
        link(BACK + s - 1, back.at[s], rall.at[z], "expert", origins[s], BACKED + z)
        for s in range(2, 4)
    ]
    to_pre = link(BACK, back.at[1], pre_in.at[0], "expert", 3 - z, BACKED + 4)
    to_next = link(BACK, back.at[1], pre_in.at[1], "expert", origins[2], BACKED + 5)

    def block(s):
        origin = origins[s]
        span = pl.ds(pl.multiple_of(origin * tok, tok), tok)
        pre = mm(tall[0, origin], wgu[0])
        for k in range(1, 4):
            pre += mm(tall[k, origin], wgu[k])
        cot = gall[origin]
        weight = as_column(
            jnp.sum(jnp.where(sublanes == z, weigh[origin], 0.0), axis=0, keepdims=True)
        )
        raw = turned(cot, wdn[...].reshape(ff, width))
        gate, up = pre[:, :ff], pre[:, ff:]
        sigma = jax.nn.sigmoid(gate)
        swish = gate * sigma
        hidden = (swish * up).astype(BF16)
        gg = jnp.sum(hidden.astype(F32) * raw, axis=1, keepdims=True)
        grad_hidden = raw * weight
        grad_gate = grad_hidden * up * (sigma * (1.0 + gate * (1.0 - sigma)))
        gp = jnp.concatenate([grad_gate.astype(BF16), (grad_hidden * swish).astype(BF16)], axis=1)
        hid[span] = hidden
        gpre[span] = gp
        scaled[span] = (weight * cot.astype(F32)).astype(BF16)
        target, at = (back, s) if s else (rall, z)
        for k in range(4):
            target[at, k] = turned(gp, wgu[k]).astype(BF16)
        (sums if s else sums_in)[at] = jnp.broadcast_to(as_row(gg), sums.shape[1:])

    with jax.named_scope("block 0"):
        block(0)

    @pl.when(middle)
    def _():
        with jax.named_scope("rows 2 middle"):
            rows_ahead(2, 1)

    @pl.when(end)
    def _():
        with jax.named_scope("rows 2 end"):
            cot_ahead(2, 0)
            rows_ahead(2, 0)

    with jax.named_scope("block 1"):
        block(1)
    gate_sums[0].start()

    @pl.when(middle)
    def _():
        to_pre.start()

    @pl.when(end)
    def _():
        to_next.start()
        with jax.named_scope("rows 1 end"):
            rows_ahead(1, 0)

    with jax.named_scope("block 2"):
        block(2)
    gate_sums[1].start()

    @pl.when(end)
    def _():
        backs[0].start()
        with jax.named_scope("rows 3"):
            cot_ahead(3, 0)
            rows_ahead(3, 0)

    with jax.named_scope("block 3"):
        block(3)
    gate_sums[2].start()

    @pl.when(end)
    def _():
        backs[1].start()

    def partial(slot, dest):
        thin = pl.ds(pl.multiple_of(dest * fq, fq), fq)
        top = across(tall[dest].reshape(length, slab), gpre[...])
        part[slot, :slab] = top.astype(BF16)
        part[slot, slab:] = across(hid[:, thin], scaled[...]).astype(BF16)

    to_sib = [link(HALF + n, part.at[n], sib_in.at[n], "seq", sib, HALVED + n) for n in range(2)]
    rows = slab + fq
    share = rows // PARTS
    to_cross = [
        link(
            PART + n, pair.at[pl.ds(n * share, share)], cross_in.at[pl.ds(n * share, share)],
            "seq", cross, PARTED + n,
        )
        for n in range(PARTS)
    ]
    with jax.named_scope("partial 0"):
        partial(0, far)
    to_sib[0].start()
    with jax.named_scope("partial 2"):
        partial(2, cross)
    to_sib[0].wait_recv()
    pair[...] = (part[2].astype(F32) + sib_in[0].astype(F32)).astype(BF16)
    for copy in to_cross[:4]:
        copy.start()

    @pl.when(middle)
    def _():
        for copy in to_cross[4:]:
            copy.start()

    with jax.named_scope("partial 1"):
        partial(1, sib)
    to_sib[1].start()
    with jax.named_scope("partial 3"):
        partial(3, q)

    @pl.when(middle)
    def _():
        with jax.named_scope("pre wait"):
            to_pre.wait_recv()
        back[2] = (back[2].astype(F32) + pre_in[0].astype(F32)).astype(BF16)
        backs[0].start()
        with jax.named_scope("next wait"):
            to_next.wait_recv()
        back[3] = (back[3].astype(F32) + pre_in[1].astype(F32)).astype(BF16)
        backs[1].start()

    with jax.named_scope("back wait"):
        for s in (1, 3):
            peer = (z + s) % 4
            link(BACK, back.at[1], rall.at[peer], "expert", peer, BACKED + peer).wait_recv()

    total = rall[z].astype(F32)
    for s in (1, 3):
        total += rall[(z + s) % 4].astype(F32)
    gfb[...] = total.astype(BF16)
    seq_g[q] = gfb[q]
    for copy in to_slabs:
        copy.wait_send()
    g_slabs = to_others(SLAB - 1, SLABBED - 1, lambda k: gfb.at[k], seq_g.at[q])
    for copy in g_slabs:
        copy.start()

    @pl.when(end)
    def _():
        for copy in to_cross[4:6]:
            copy.start()

    for s in range(1, 4):
        peer = (z + s) % 4
        link(SUM, sums.at[s], sums_in.at[peer], "expert", peer, SUMMED + peer).wait_recv()
    gate_grads = jnp.zeros(ids.shape, F32)
    for s in range(4):
        gate_grads += jnp.where(ids == s, sums_in[s, 0:1], 0.0)
    gg_ref[...] = jnp.where(kept, gate_grads, 0.0).astype(BF16)

    with jax.named_scope("grad wait"):
        for copy in g_slabs:
            copy.wait_recv()
    with jax.named_scope("tap grad"):
        forward(g_spec, length, whole(seq_g))
        gc, gs = g_spec[:half], g_spec[half:]
        xc, xs = x_spec[:half], x_spec[half:]
        prod = jnp.concatenate([gc * xc + gs * xs, gs * xc - gc * xs], axis=0)
        gfz[...] = backward(n_taps, prod).astype(BF16).reshape(4, piece, slab)
    gf_exp = [
        link(TAP + s - 1, gfz.at[(z + s) % 4], gfz_in.at[s], "expert", (z + s) % 4, TAPPED + s - 1)
        for s in range(1, 4)
    ]
    for copy in gf_exp:
        copy.start()
    with jax.named_scope("input grad"):
        gc, gs = g_spec[:half], g_spec[half:]
        hc, hs = tap_spec[:half], tap_spec[half:]
        prod = jnp.concatenate([gc * hc + gs * hs, gs * hc - gc * hs], axis=0)
        seq_in[...] = backward(length, prod).astype(BF16).reshape(4, tok, slab)
    for copy in to_rows:
        copy.wait_send()
    gin_out = to_others(ROW - 1, ROWED - 1, lambda k: seq_in.at[k], gin_ref.at[q])
    for copy in gin_out:
        copy.start()
    gin_ref[q] = seq_in[q]

    @pl.when(end)
    def _():
        for copy in to_cross[6:]:
            copy.start()

    with jax.named_scope("taps z wait"):
        for copy in gf_exp:
            copy.wait_recv()
    mine = gfz[z].astype(F32)
    for s in range(1, 4):
        mine += gfz_in[s].astype(F32)
    gf_ref[q, z] = mine.astype(BF16)
    near = [z, pick(1, 2, 1, 2), pick(2, 0, 3, 1), pick(3, 3, 0, 0)]
    gf_out = [
        link(OUT + s - 1, gf_ref.at[q, z], gf_ref.at[q, z], "expert", near[s], OUTED + z)
        for s in range(1, 4)
    ]
    gf_cross = [
        link(
            LAST + s, gf_ref.at[q, near[s]], gf_ref.at[q, near[s]], "seq", cross, LASTED + near[s]
        )
        for s in range(4)
    ]
    gf_sib = [
        link(SIB, gf_ref.at[q], gf_ref.at[q], "seq", sib, SIBBED),
        link(SIB + 1, gf_ref.at[cross], gf_ref.at[cross], "seq", sib, SIBBED + 1),
    ]
    for copy in w_sib:
        copy.wait_send()
    for copy in gf_out + gf_cross[:1]:
        copy.start()
    with jax.named_scope("taps out wait"):
        for s in range(1, 4):
            link(OUT, gf_ref.at[q, z], gf_ref.at[q, z], "expert", z, OUTED + near[s]).wait_recv()
            gf_cross[s].start()
    gf_sib[0].start()
    to_sib[1].wait_recv()
    with jax.named_scope("pair wait"):
        for copy in to_cross:
            copy.wait_recv()
    with jax.named_scope("weight sums"):
        dgu_ref[...] = (
            part[3, :slab].astype(F32) + sib_in[1, :slab].astype(F32) + cross_in[:slab].astype(F32)
        ).astype(BF16)
        dd_ref[...] = (
            part[3, slab:].astype(F32) + sib_in[1, slab:].astype(F32) + cross_in[slab:].astype(F32)
        ).astype(BF16)
    with jax.named_scope("taps cross wait"):
        for copy in gf_cross:
            copy.wait_recv()
    gf_sib[1].start()
    with jax.named_scope("last waits"):
        for copy in gin_out:
            copy.wait_recv()
        for copy in gf_sib:
            copy.wait_recv()
        for d in range(3):
            for part in range(2):
                spread(part, cot_of(part), d, False)
                spread(2 + part, tok_of(part), d, False)

        to_pre.wait_send()

        for copy in (
            w_cross + w_group + w_far[0] + w_far[1] + weighs + gate_sums + backs + to_sib
            + to_cross + g_slabs + gf_exp + gin_out + gf_out + gf_cross + gf_sib
        ):
            copy.wait_send()


def finish_kernel(
    gin_ref, gg_ref, gf_ref, dgu_ref, dd_ref,
    gin_out, gg_out, gf_out, dg_out, du_out, dd_out, wide, sem,
):
    slab = gin_ref.shape[2]
    ff = dg_out.shape[2]
    copies = [
        (gin_ref.at[k], gin_out.at[:, pl.ds(k * slab, slab)]) for k in range(4)
    ] + [
        (dgu_ref.at[:, pl.ds(0, ff)], dg_out.at[0]), (dgu_ref.at[:, pl.ds(ff, ff)], du_out.at[0]),
        (dd_ref, dd_out.at[0]), (gg_ref, gg_out),
    ]
    copies = [pltpu.make_async_copy(a, b, sem.at[n]) for n, (a, b) in enumerate(copies)]
    for copy in copies:
        copy.start()
    piece = gf_ref.shape[2]
    for a in range(4):
        span = pl.ds(a * piece, piece)
        for k in range(4):
            wide[span, pl.ds(k * slab, slab)] = gf_ref[k, a].astype(F32)
        copies.append(pltpu.make_async_copy(wide.at[span], gf_out.at[span], sem.at[8 + a]))
        copies[-1].start()
    for copy in copies:
        copy.wait()


def dense_body(inputs, grad_out, gates, expert_ids, slot_index, filter_taps, w_gate, w_up, w_down):
    tok, width = inputs.shape
    taps = filter_taps.shape[0]
    ff = w_gate.shape[2]
    top = gates.shape[1]
    length = 4 * tok
    size = taps + length
    slab = width // 4
    rows = slab + ff // 4
    vm = lambda *shape: pltpu.VMEM(shape, BF16)
    vf = lambda *shape: pltpu.VMEM(shape, F32)
    st = lambda *shape: jax.ShapeDtypeStruct(shape, BF16)
    near = pl.BlockSpec(memory_space=pltpu.VMEM)
    hbm = pl.BlockSpec(memory_space=pltpu.HBM)
    far_away = lambda array: pltpu.with_memory_space_constraint(array, pltpu.HBM)
    fh, fl, ih, il = transforms(size)
    outs = pl.pallas_call(
        dense_kernel,
        out_shape=(
            vm(4, tok, slab), vm(top, tok), vm(4, 4, taps // 4, slab), vm(slab, 2 * ff),
            vm(ff // 4, width),
        ),
        in_specs=[hbm] * 13,
        out_specs=(near,) * 5,
        scratch_shapes=[
            vm(top, tok), pltpu.VMEM((top, tok), jnp.int32), pltpu.VMEM((top, tok), jnp.int32),
            vm(size, length), vm(size, length), vm(length, size), vm(length, size), vm(taps, slab),
            vf(size, slab), vf(size, slab), vf(size, slab),
            vm(4, tok, slab), vm(4, tok, slab), vm(4, tok, slab), vm(4, tok, slab),
            vm(4, 4, tok, slab), vm(4, tok, width), vm(4, slab, 2 * ff), vm(4, ff // 4, width),
            vm(length, ff), vm(length, 2 * ff), vm(length, width),
            vm(4, 4, tok, slab), vm(4, 4, tok, slab), vm(2, 4, tok, slab), vm(4, tok, slab),
            vm(4, rows, width), vm(2, rows, width), vm(rows, width), vm(rows, width),
            vm(4, taps // 4, slab), vm(4, taps // 4, slab),
            vf(4, 8, tok), vf(4, 8, tok), vf(4, 8, tok),
            pltpu.SemaphoreType.DMA((13,)),
            pltpu.SemaphoreType.DMA((73,)), pltpu.SemaphoreType.DMA((71,)),
        ],
        compiler_params=pltpu.CompilerParams(
            collective_id=0, has_side_effects=True, vmem_limit_bytes=48 * 1024 * 1024
        ),
    )(
        *[far_away(m) for m in (inputs, grad_out, gates.T, expert_ids.T, slot_index.T)],
        *[far_away(m) for m in (w_gate, w_up, w_down, filter_taps)],
        *[far_away(jnp.asarray(m)) for m in (fh[:, :length], fl[:, :length], ih[:length], il[:length])],
    )
    grads = pl.pallas_call(
        finish_kernel,
        out_shape=(
            st(tok, width), st(top, tok), jax.ShapeDtypeStruct((taps, width), F32),
            st(*w_gate.shape), st(*w_up.shape), st(*w_down.shape),
        ),
        in_specs=[near] * 5,
        out_specs=(hbm,) * 6,
        scratch_shapes=[vf(taps, width), pltpu.SemaphoreType.DMA((12,))],
        compiler_params=pltpu.CompilerParams(vmem_limit_bytes=8 * 1024 * 1024),
    )(*[pltpu.with_memory_space_constraint(array, pltpu.VMEM) for array in outs])
    return (grads[0], grads[1].T) + grads[2:]


def body_of(mesh):
    def body(*args):
        top_count = args[3].shape[1]
        tok, taps, dq = args[0].shape[0], args[5].shape[0], args[6].shape[1]
        small = mesh.shape["expert"] == top_count == 4 and mesh.shape["seq"] == 4
        small = small and mesh.shape["groups"] == 2
        if small and tok == 128 and taps == 2 * tok and dq == 2 * tok and 2 * args[6].shape[2] == args[0].shape[1]:
            return dense_body(*args)
        return routed_body(*args)

    return body


def solution(mesh):
    return jax.shard_map(
        body_of(mesh),
        mesh=mesh,
        in_specs=(
            P(("groups", "expert", "seq"), None),
            P(("groups", "expert", "seq"), None),
            P(("groups", "expert", "seq"), None),
            P(("groups", "expert", "seq"), None),
            P(("groups", "expert", "seq"), None),
            P(),
            P("expert", "seq", None),
            P("expert", "seq", None),
            P("expert", "seq", None),
        ),
        out_specs=(
            P(("groups", "expert", "seq"), None),
            P(("groups", "expert", "seq"), None),
            P("groups", None),
            P(("groups", "expert"), "seq", None),
            P(("groups", "expert"), "seq", None),
            P(("groups", "expert"), "seq", None),
        ),
        check_vma=False,
    )
```

```python
import functools

import jax
import jax.numpy as jnp
import numpy as np
from jax import lax
from jax.experimental import pallas as pl
from jax.experimental.pallas import tpu as pltpu
from jax.sharding import PartitionSpec as P

MESH = pl.DeviceIdType.MESH
F32 = jnp.float32
BF16 = jnp.bfloat16


def from_behind(block, axis, distance):
    devices = range(lax.axis_size(axis))
    route = [(i - distance, i) for i in devices if i - distance in devices]
    return lax.ppermute(block, axis, route)


def depthwise(signal, kernel):
    return lax.conv_general_dilated(
        signal[None],
        kernel[:, None, :],
        (1,),
        "VALID",
        dimension_numbers=("NWC", "WIO", "NWC"),
        feature_group_count=signal.shape[1],
        preferred_element_type=jnp.float32,
    )[0]


def contract(left, right, left_dim, right_dim):
    return lax.dot_general(
        left, right, (((left_dim,), (right_dim,)), ((), ())), preferred_element_type=jnp.float32
    )


def expert_pass(token_rows, scaled_rows, gate_mat, up_mat, down_mat):
    pre_gate = jnp.dot(token_rows, gate_mat, preferred_element_type=jnp.float32)
    pre_up = jnp.dot(token_rows, up_mat, preferred_element_type=jnp.float32)
    sigma = jax.nn.sigmoid(pre_gate)
    swish = pre_gate * sigma
    hidden = (swish * pre_up).astype(jnp.bfloat16)
    outputs = jnp.dot(hidden, down_mat, preferred_element_type=jnp.float32).astype(jnp.bfloat16)
    grad_hidden = contract(scaled_rows, down_mat, 1, 1)
    grad_pre_gate = (grad_hidden * pre_up * (sigma * (1.0 + pre_gate * (1.0 - sigma)))).astype(
        jnp.bfloat16
    )
    grad_pre_up = (grad_hidden * swish).astype(jnp.bfloat16)
    part_gate = contract(token_rows, grad_pre_gate, 0, 0)
    part_up = contract(token_rows, grad_pre_up, 0, 0)
    part_down = contract(hidden, scaled_rows, 0, 0)
    grad_rows = (
        contract(grad_pre_gate, gate_mat, 1, 1) + contract(grad_pre_up, up_mat, 1, 1)
    ).astype(jnp.bfloat16)
    return (grad_rows, outputs, (part_gate, part_up, part_down))


def routed_body(inputs, grad_out, gates, expert_ids, slot_index, filter_taps, w_gate, w_up, w_down):
    tok_count, width = inputs.shape
    taps = filter_taps.shape[0]
    top_count = expert_ids.shape[1]
    experts = lax.axis_size("expert")
    capacity = tok_count * top_count // experts
    reach = taps - 1
    shift_count = (reach + tok_count - 1) // tok_count
    earlier = [from_behind(inputs, "seq", shift_by) for shift_by in range(shift_count, 0, -1)]
    extended = jnp.concatenate(earlier + [inputs], axis=0)[-(tok_count + reach) :]
    filtered = depthwise(extended, filter_taps[::-1]).astype(jnp.bfloat16)
    kept = slot_index < capacity
    dest = jnp.where(kept, expert_ids * capacity + slot_index, experts * capacity).reshape(-1)

    def place(values):
        rest = values.shape[1:]
        empty = jnp.zeros((experts * capacity,) + rest, values.dtype)
        return empty.at[dest].set(values, mode="drop").reshape((experts, capacity) + rest)

    def fetch(buffer):
        rest = buffer.shape[2:]
        flat = buffer.reshape((experts * capacity,) + rest)
        return jnp.take(flat, dest, axis=0, mode="fill", fill_value=0).reshape(
            (tok_count, top_count) + rest
        )

    token_send = place(
        jnp.broadcast_to(filtered[:, None, :], (tok_count, top_count, width)).reshape(-1, width)
    )
    gate_full, up_full, down_full = (
        lax.all_gather(w_gate, "seq", axis=1, tiled=True),
        lax.all_gather(w_up, "seq", axis=1, tiled=True),
        lax.all_gather(w_down, "seq", axis=1, tiled=True),
    )
    gate_mat = gate_full[0]
    up_mat = up_full[0]
    down_mat = down_full[0]
    scaled = (
        gates.astype(jnp.float32)[:, :, None] * grad_out.astype(jnp.float32)[:, None, :]
    ).astype(jnp.bfloat16)
    token_recv, scaled_recv = (
        lax.all_to_all(token_send, "expert", split_axis=0, concat_axis=0, tiled=True),
        lax.all_to_all(
            place(scaled.reshape(-1, width)), "expert", split_axis=0, concat_axis=0, tiled=True
        ),
    )
    grad_rows, outputs, partials = expert_pass(
        token_recv.reshape(-1, width), scaled_recv.reshape(-1, width), gate_mat, up_mat, down_mat
    )
    grad_back, output_back = (
        lax.all_to_all(
            grad_rows.reshape(experts, capacity, width),
            "expert",
            split_axis=0,
            concat_axis=0,
            tiled=True,
        ),
        lax.all_to_all(
            outputs.reshape(experts, capacity, width),
            "expert",
            split_axis=0,
            concat_axis=0,
            tiled=True,
        ),
    )
    output_rows = fetch(output_back)
    grad_gates = jnp.sum(
        grad_out.astype(jnp.float32)[:, None, :] * output_rows.astype(jnp.float32), axis=2
    ).astype(jnp.bfloat16)
    summed_gate, summed_up, summed_down = (
        lax.psum_scatter(
            partials[0][None].astype(jnp.bfloat16), "seq", scatter_dimension=1, tiled=True
        ).astype(jnp.float32),
        lax.psum_scatter(
            partials[1][None].astype(jnp.bfloat16), "seq", scatter_dimension=1, tiled=True
        ).astype(jnp.float32),
        lax.psum_scatter(
            partials[2][None].astype(jnp.bfloat16), "seq", scatter_dimension=1, tiled=True
        ).astype(jnp.float32),
    )
    grad_filtered = jnp.sum(fetch(grad_back).astype(jnp.float32), axis=1).astype(jnp.bfloat16)
    later = [from_behind(grad_filtered, "seq", -shift_by) for shift_by in range(1, shift_count + 1)]
    grad_extended = jnp.concatenate([grad_filtered] + later, axis=0)[: tok_count + reach]
    grad_inputs = depthwise(grad_extended, filter_taps).astype(jnp.bfloat16)
    local_taps = depthwise(extended, grad_filtered)[::-1]
    grad_filter = lax.psum(local_taps, ("expert", "seq"))
    return (
        grad_inputs,
        grad_gates,
        grad_filter,
        summed_gate.astype(jnp.bfloat16),
        summed_up.astype(jnp.bfloat16),
        summed_down.astype(jnp.bfloat16),
    )


def transforms(size):
    freq = 2.0 * np.pi * (np.arange(size // 2) + 0.5) / size
    angle = freq[:, None] * np.arange(size)[None, :]
    forward = np.concatenate([np.cos(angle), np.sin(angle)], axis=0)
    inverse = forward.T * (2.0 / size)

    def pieces(matrix):
        high = matrix.astype(jnp.bfloat16)
        low = (matrix - high.astype(np.float64)).astype(jnp.bfloat16)
        return high, low

    return pieces(forward) + pieces(inverse)


def mm(left, right):
    return jnp.dot(left, right, preferred_element_type=F32)


def turned(left, right):
    return lax.dot_general(left, right, (((1,), (1,)), ((), ())), preferred_element_type=F32)


def across(left, right):
    return lax.dot_general(left, right, (((0,), (0,)), ((), ())), preferred_element_type=F32)


PIECES = 3
PARTS = 6


def dense_kernel(
    rows_ref, cot_ref, gates_ref, ids_ref, slots_ref, wg_ref, wu_ref, wd_ref, taps_ref,
    fh_ref, fl_ref, ih_ref, il_ref,
    gin_ref, gg_ref, gf_ref, dgu_ref, dd_ref,
    gates_in, ids_in, slots_in, fh, fl, ih, il, taps, x_spec, tap_spec, g_spec, seq_x, seq_f, seq_g, seq_in,
    tall, gall, wgu, wdn, hid, gpre, scaled, back, rall, pre_in, gfb,
    part, sib_in, pair, cross_in, relay_in, gfz, gfz_in,
    weigh, sums, sums_in,
    load_sem, send_sem, recv_sem,
):
    g = lax.axis_index("groups")
    z = lax.axis_index("expert")
    q = lax.axis_index("seq")
    tok, width = rows_ref.shape
    slab = width // 4
    ff = hid.shape[1]
    fq = ff // 4
    size = x_spec.shape[0]
    half = size // 2
    n_taps = taps.shape[0]
    piece = n_taps // 4
    length = 4 * tok
    sib = q + 1 - 2 * (q % 2)
    cross = (q + 2) % 4
    far = (sib + 2) % 4
    middle = jnp.logical_or(z == 1, z == 2)
    end = jnp.logical_or(z == 0, z == 3)

    across_end = {
        "expert": jnp.where(z < 2, 1 - z, 5 - z), "seq": cross
    }
    barrier = pltpu.get_barrier_semaphore()
    pl.semaphore_signal(barrier, inc=1, device_id=across_end, device_id_type=MESH)
    for s in range(1, 4):
        pl.semaphore_signal(barrier, inc=1, device_id={"expert": (z + s) % 4}, device_id_type=MESH)
        pl.semaphore_signal(barrier, inc=1, device_id={"seq": (q + s) % 4}, device_id_type=MESH)
    pl.semaphore_signal(barrier, inc=1, device_id={"groups": 1 - g}, device_id_type=MESH)

    def slab_at(k):
        return pl.ds(pl.multiple_of(k * slab, slab), slab)

    loads = [
        pltpu.make_async_copy(src, dst, load_sem.at[n])
        for n, (src, dst) in enumerate([
            (cot_ref, gall.at[z]),
            (gates_ref, gates_in), (ids_ref, ids_in), (slots_ref, slots_in),
            (rows_ref.at[:, slab_at(q)], seq_x.at[q]),
            (wg_ref.at[0], wgu.at[q, :, pl.ds(0, ff)]),
            (wu_ref.at[0], wgu.at[q, :, pl.ds(ff, ff)]),
            (wd_ref.at[0], wdn.at[q]),
            (taps_ref.at[:, slab_at(q)], taps),
            (fh_ref, fh), (fl_ref, fl), (ih_ref, ih), (il_ref, il),
        ])
    ]
    for load in loads:
        load.start()

    def link(n, src, dst, axis, peer, arrival):
        device = peer if isinstance(peer, dict) else {axis: peer}
        return pltpu.make_async_remote_copy(
            src_ref=src, dst_ref=dst, send_sem=send_sem.at[n],
            recv_sem=recv_sem.at[arrival], device_id=device, device_id_type=MESH,
        )

    def pick(a, b, c, d):
        return jnp.where(z == 0, a, jnp.where(z == 1, b, jnp.where(z == 2, c, d)))

    GATHER, WEIGH, SUM, BACK, SLAB, ROW, TAP, OUT = 0, 24, 27, 30, 32, 35, 38, 42
    WEIGHT, SIB, HALF, PART, LAST, MORE, RELAY = 46, 58, 60, 63, 69, 73, 75
    GATHERED, WEIGHED, SUMMED, BACKED, SLABBED, ROWED, TAPPED, OUTED = 0, 16, 20, 24, 30, 33, 36, 40
    WEIGHTED, SIBBED, HALVED, PARTED, LASTED, RELAYED = 44, 56, 58, 61, 67, 71

    def hop(base, view, origin, step, distance):
        return link(
            GATHER + 6 * base + (0 if step > 0 else 3) + distance, view(origin), view(origin),
            "expert", (z + 4 + step) % 4, GATHERED + 4 * base + origin,
        )

    def spread(base, view, distance, send=True):
        for step in (1, -1):
            origin = z - step * distance
            has_origin = origin >= 0 if step > 0 else origin <= 3
            has_next = z < 3 if step > 0 else z > 0

            @pl.when(has_origin)
            def _(origin=origin, has_next=has_next, step=step):
                if distance and send:
                    hop(base, view, origin, step, 0).wait_recv()

                if distance < 3:
                    @pl.when(has_next)
                    def _():
                        if send:
                            hop(base, view, origin, step, distance).start()
                        else:
                            hop(base, view, origin, step, distance).wait_send()

    def cot_ahead(distance, first, last=2):
        for part in range(first, last):
            spread(part, cot_of(part), distance)

    def rows_ahead(distance, first, last=2):
        for part in range(first, last):
            spread(2 + part, tok_of(part), distance)

    def cot_of(part):
        return lambda origin: gall.at[origin, pl.ds(part * (tok // 2), tok // 2)]

    def tok_of(part):
        return lambda origin: tall.at[:, origin, pl.ds(part * (tok // 2), tok // 2)]

    for load in loads[:4]:
        load.wait()
    ids = ids_in[...]
    kept = slots_in[...] < tok
    held = jnp.where(kept, gates_in[...].astype(F32), 0.0)
    eye = lax.broadcasted_iota(jnp.int32, (tok, tok), 0) == lax.broadcasted_iota(
        jnp.int32, (tok, tok), 1
    )

    def as_row(column):
        return jnp.sum(jnp.where(eye, column, 0.0), axis=0, keepdims=True)

    def as_column(row):
        return jnp.sum(jnp.where(eye, row, 0.0), axis=1, keepdims=True)

    weigh[z] = jnp.zeros(weigh.shape[1:], F32)
    for e in range(4):
        weigh[z, e:e + 1] = jnp.sum(jnp.where(ids == e, held, 0.0), axis=0, keepdims=True)

    with jax.named_scope("entry"):
        pl.semaphore_wait(barrier, 8)

    cot_ahead(0, 0)

    def to_others(send, arrive, source, dest):
        return [
            link(send + s, source((q + s) % 4), dest, "seq", (q + s) % 4, arrive + s)
            for s in (2, 1, 3)
        ]

    to_slabs = to_others(
        SLAB - 1, SLABBED - 1, lambda k: rows_ref.at[:, slab_at(k)], seq_x.at[q]
    )
    for copy in to_slabs:
        copy.start()
    for load in loads[4:9]:
        load.wait()

    step = (slab + fq) // (2 * PIECES)
    wide_pieces = slab // (2 * step)

    def piece_of(k, n, part):
        if n < wide_pieces:
            return wgu.at[k, pl.ds(pl.multiple_of((2 * n + part) * step, step), step)]
        at = pl.multiple_of((2 * (n - wide_pieces) + part) * step, step)
        return wdn.at[k, pl.ds(at, step)]

    def weight_copy(kind, source, n, part, axis, peer):
        at = kind * PIECES + n
        return link(
            WEIGHT + at, piece_of(source, n, part), piece_of(source, n, part), axis, peer,
            WEIGHTED + at,
        )

    w_cross = [weight_copy(0, q, n, g, "seq", cross) for n in range(PIECES)]
    w_group = [weight_copy(1, cross, n, g, "groups", 1 - g) for n in range(PIECES)]
    w_far = [
        [weight_copy(2 + h, cross, n, (g + h) % 2, "seq", sib) for n in range(PIECES)]
        for h in range(2)
    ]

    def pass_on(n):
        w_cross[n].wait_recv()
        w_group[n].start()
        w_far[0][n].start()

    def take(n):
        w_group[n].wait_recv()
        w_far[1][n].start()

    w_sib = [
        link(SIB, wgu.at[q], wgu.at[q], "seq", sib, SIBBED),
        link(SIB + 1, wdn.at[q], wdn.at[q], "seq", sib, SIBBED + 1),
    ]
    weighs = [
        link(WEIGH + s - 1, weigh.at[z], weigh.at[z], "expert", (z + s) % 4, WEIGHED + z)
        for s in range(1, 4)
    ]
    for copy in weighs + w_sib:
        copy.start()

    def forward(dest, count, values, exact=True):
        for at in range(0, size, slab):
            span = pl.ds(at, slab)
            dest[span] = mm(fh[span, :count], values)
            if exact:
                dest[span] += mm(fl[span, :count], values)

    def backward(count, spec, exact=True):
        high = spec.astype(BF16)
        if not exact:
            return mm(ih[:count], high)
        low = (spec - high.astype(F32)).astype(BF16)
        return mm(ih[:count], high) + mm(il[:count], high) + mm(ih[:count], low)

    def whole(ref):
        return ref[...].reshape(length, slab)

    for load in loads[9:]:
        load.wait()
    with jax.named_scope("tap spectrum"):
        forward(tap_spec, n_taps, taps[...])
    with jax.named_scope("x wait"):
        for copy in to_slabs:
            copy.wait_recv()
    w_cross[0].start()
    with jax.named_scope("cot 1 first"):
        cot_ahead(1, 0, 1)
    with jax.named_scope("filter"):
        forward(x_spec, length, whole(seq_x))
        xc, xs = x_spec[:half], x_spec[half:]
        hc, hs = tap_spec[:half], tap_spec[half:]
        prod = jnp.concatenate([xc * hc - xs * hs, xc * hs + xs * hc], axis=0)
        seq_f[...] = backward(length, prod).astype(BF16).reshape(4, tok, slab)
    to_rows = to_others(ROW - 1, ROWED - 1, lambda k: seq_f.at[k], tall.at[q, z])
    for copy in to_rows + w_cross[1:]:
        copy.start()
    tall[q, z] = seq_f[q]
    with jax.named_scope("cot 1"):
        cot_ahead(1, 1)
    with jax.named_scope("rows wait"):
        for copy in to_rows:
            copy.wait_recv()
    rows_ahead(0, 0)
    with jax.named_scope("pass 0"):
        pass_on(0)
    with jax.named_scope("pass 1"):
        pass_on(1)

    @pl.when(middle)
    def _():
        with jax.named_scope("rows 1 first"):
            rows_ahead(1, 0, 1)

    with jax.named_scope("pass 2"):
        pass_on(2)
    with jax.named_scope("take 0"):
        take(0)

    @pl.when(middle)
    def _():
        with jax.named_scope("rows 1"):
            rows_ahead(1, 1)
        with jax.named_scope("cot 2"):
            cot_ahead(2, 0)

    with jax.named_scope("take 1"):
        take(1)
    with jax.named_scope("weigh wait"):
        for k in range(1, 4):
            peer = (z + k) % 4
            link(WEIGH, weigh.at[peer], weigh.at[peer], "expert", peer, WEIGHED + peer).wait_recv()

    @pl.when(middle)
    def _():
        with jax.named_scope("rows 2 middle first"):
            rows_ahead(2, 0, 1)

    with jax.named_scope("take 2"):
        take(2)
    with jax.named_scope("weights wait"):
        for copy in w_sib + w_far[0] + w_far[1]:
            copy.wait_recv()

    origins = [z, pick(2, 3, 0, 1), pick(1, 0, 3, 2), pick(3, 2, 1, 0)]
    sublanes = lax.broadcasted_iota(jnp.int32, weigh.shape[1:], 0)
    gate_sums = [
        link(SUM + s - 1, sums.at[s], sums_in.at[z], "expert", origins[s], SUMMED + z)
        for s in range(1, 4)
    ]
    backs = [
        link(BACK + s - 2, back.at[s], rall.at[z], "expert", origins[s], BACKED + z)
        for s in range(2, 4)
    ]
    to_pre = link(TAP, back.at[1], pre_in.at[0], "expert", 3 - z, BACKED + 4)
    to_next = link(TAP, back.at[1], pre_in.at[1], "expert", origins[2], BACKED + 5)

    def block(s):
        origin = origins[s]
        span = pl.ds(pl.multiple_of(origin * tok, tok), tok)
        pre = mm(tall[0, origin], wgu[0])
        for k in range(1, 4):
            pre += mm(tall[k, origin], wgu[k])
        cot = gall[origin]
        weight = as_column(
            jnp.sum(jnp.where(sublanes == z, weigh[origin], 0.0), axis=0, keepdims=True)
        )
        raw = turned(cot, wdn[...].reshape(ff, width))
        gate, up = pre[:, :ff], pre[:, ff:]
        sigma = jax.nn.sigmoid(gate)
        swish = gate * sigma
        hidden = (swish * up).astype(BF16)
        gg = jnp.sum(hidden.astype(F32) * raw, axis=1, keepdims=True)
        grad_hidden = raw * weight
        grad_gate = grad_hidden * up * (sigma * (1.0 + gate * (1.0 - sigma)))
        gp = jnp.concatenate([grad_gate.astype(BF16), (grad_hidden * swish).astype(BF16)], axis=1)
        hid[span] = hidden
        gpre[span] = gp
        scaled[span] = (weight * cot.astype(F32)).astype(BF16)
        target, at = (back, s) if s else (rall, z)
        for k in range(4):
            target[at, k] = turned(gp, wgu[k]).astype(BF16)
        (sums if s else sums_in)[at] = jnp.broadcast_to(as_row(gg), sums.shape[1:])

    with jax.named_scope("block 0"):
        block(0)

    @pl.when(middle)
    def _():
        with jax.named_scope("rows 2 middle"):
            rows_ahead(2, 1)

    @pl.when(end)
    def _():
        with jax.named_scope("rows 2 end"):
            cot_ahead(2, 0)
            rows_ahead(2, 0)

    with jax.named_scope("block 1"):
        block(1)
    gate_sums[0].start()

    @pl.when(middle)
    def _():
        to_pre.start()

    @pl.when(end)
    def _():
        to_next.start()
        with jax.named_scope("rows 1 end"):
            rows_ahead(1, 0)

    with jax.named_scope("block 2"):
        block(2)
    gate_sums[1].start()

    @pl.when(end)
    def _():
        backs[0].start()
        with jax.named_scope("rows 3"):
            cot_ahead(3, 0)
            rows_ahead(3, 0)

    with jax.named_scope("block 3"):
        block(3)
    gate_sums[2].start()

    @pl.when(end)
    def _():
        backs[1].start()

    def partial_low(slot, dest):
        thin = pl.ds(pl.multiple_of(dest * fq, fq), fq)
        part[slot, slab:] = across(hid[:, thin], scaled[...]).astype(BF16)

    def partial_top(slot, dest):
        top = across(tall[dest].reshape(length, slab), gpre[...])
        part[slot, :slab] = top.astype(BF16)

    rows = slab + fq
    share = rows // PARTS
    low, top = pl.ds(slab, fq), pl.ds(0, slab)
    to_sib = [
        link(HALF, part.at[0, low], sib_in.at[0, low], "seq", sib, HALVED),
        link(HALF + 1, part.at[0, top], sib_in.at[0, top], "seq", sib, HALVED + 1),
        link(HALF + 2, part.at[1], sib_in.at[1], "seq", sib, HALVED + 2),
    ]
    to_cross = [
        link(
            PART + n, pair.at[pl.ds(n * share, share)], cross_in.at[pl.ds(n * share, share)],
            "seq", cross, PARTED + n,
        )
        for n in [*range(slab // share, PARTS), *range(slab // share)]
    ]
    near_end = pick(1, 0, 3, 2)
    around = []
    passed = []
    for n in range(2):
        span = pl.ds((slab // share - 1 - n) * share, share)
        around.append(link(MORE + n, pair.at[span], relay_in.at[n], "", across_end, RELAYED + n))
        passed.append(
            link(
                RELAY + n, relay_in.at[n], cross_in.at[span], "expert", near_end,
                PARTED + slab // share - 1 - n,
            )
        )

    def pass_part(n):
        around[n].wait_recv()
        passed[n].start()

    with jax.named_scope("partial 0"):
        partial_low(0, far)
        to_sib[0].start()
        partial_top(0, far)
        to_sib[1].start()
    with jax.named_scope("partial 2"):
        partial_low(2, cross)
        to_sib[0].wait_recv()
        pair[low] = (part[2, low].astype(F32) + sib_in[0, low].astype(F32)).astype(BF16)
        for copy in to_cross[:2]:
            copy.start()
        partial_top(2, cross)
        to_sib[1].wait_recv()
        pair[top] = (part[2, top].astype(F32) + sib_in[0, top].astype(F32)).astype(BF16)
        to_cross[2].start()

    @pl.when(end)
    def _():
        around[0].start()

    @pl.when(middle)
    def _():
        for copy in to_cross[3:5]:
            copy.start()

    with jax.named_scope("partial 1"):
        partial_low(1, sib)
        partial_top(1, sib)
    to_sib[2].start()
    with jax.named_scope("partial 3"):
        partial_low(3, q)
        partial_top(3, q)

    @pl.when(middle)
    def _():
        with jax.named_scope("pre wait"):
            to_pre.wait_recv()
        back[2] = (back[2].astype(F32) + pre_in[0].astype(F32)).astype(BF16)
        backs[0].start()
        with jax.named_scope("next wait"):
            to_next.wait_recv()
        back[3] = (back[3].astype(F32) + pre_in[1].astype(F32)).astype(BF16)
        backs[1].start()

    with jax.named_scope("back wait"):
        for s in (1, 3):
            peer = (z + s) % 4
            link(BACK, back.at[1], rall.at[peer], "expert", peer, BACKED + peer).wait_recv()

    total = rall[z].astype(F32)
    for s in (1, 3):
        total += rall[(z + s) % 4].astype(F32)
    gfb[...] = total.astype(BF16)
    seq_g[q] = gfb[q]
    for copy in to_slabs:
        copy.wait_send()
    g_slabs = to_others(SLAB - 1, SLABBED - 1, lambda k: gfb.at[k], seq_g.at[q])
    for copy in g_slabs:
        copy.start()

    @pl.when(middle)
    def _():
        with jax.named_scope("part 0"):
            pass_part(0)

    for s in range(1, 4):
        peer = (z + s) % 4
        link(SUM, sums.at[s], sums_in.at[peer], "expert", peer, SUMMED + peer).wait_recv()
    gate_grads = jnp.zeros(ids.shape, F32)
    for s in range(4):
        gate_grads += jnp.where(ids == s, sums_in[s, 0:1], 0.0)
    gg_ref[...] = jnp.where(kept, gate_grads, 0.0).astype(BF16)

    with jax.named_scope("grad wait"):
        for copy in g_slabs:
            copy.wait_recv()

    @pl.when(middle)
    def _():
        to_cross[5].start()

    @pl.when(end)
    def _():
        to_cross[3].start()

    with jax.named_scope("tap grad"):
        forward(g_spec, length, whole(seq_g), False)
        gc, gs = g_spec[:half], g_spec[half:]
        xc, xs = x_spec[:half], x_spec[half:]
        prod = jnp.concatenate([gc * xc + gs * xs, gs * xc - gc * xs], axis=0)
        gfz[...] = backward(n_taps, prod, False).astype(BF16).reshape(4, piece, slab)
    near = [z, pick(1, 2, 1, 2), pick(2, 0, 3, 1), pick(3, 3, 0, 0)]
    tap_in = [
        link(TAP + s, gfz.at[near[s]], gfz_in.at[z], "expert", near[s], TAPPED + z)
        for s in (3, 2, 1)
    ]
    tap_out = [
        link(OUT + s, gf_ref.at[q, z], gf_ref.at[q, z], "expert", near[s], OUTED + z)
        for s in (3, 2, 1)
    ]
    tap_cross = [
        link(
            LAST + s, gf_ref.at[q, near[s]], gf_ref.at[q, near[s]], "seq", cross, LASTED + near[s]
        )
        for s in range(4)
    ]
    to_pre.wait_send()

    for copy in tap_in:
        copy.start()

    @pl.when(end)
    def _():
        around[1].start()

    with jax.named_scope("input grad"):
        gc, gs = g_spec[:half], g_spec[half:]
        hc, hs = tap_spec[:half], tap_spec[half:]
        prod = jnp.concatenate([gc * hc + gs * hs, gs * hc - gc * hs], axis=0)
        seq_in[...] = backward(length, prod).astype(BF16).reshape(4, tok, slab)
    for copy in to_rows:
        copy.wait_send()
    gin_out = to_others(ROW - 1, ROWED - 1, lambda k: seq_in.at[k], gin_ref.at[q])
    for copy in gin_out:
        copy.start()
    gin_ref[q] = seq_in[q]

    def tap_from(base, peer):
        link(TAP, gfz.at[0], gfz_in.at[0], "expert", peer, base + peer).wait_recv()

    with jax.named_scope("taps in"):
        mine = gfz[z].astype(F32)
        for s in range(1, 4):
            tap_from(TAPPED, near[s])
            mine += gfz_in[near[s]].astype(F32)
    gf_ref[q, z] = mine.astype(BF16)
    for copy in tap_out + tap_cross[:1]:
        copy.start()

    @pl.when(middle)
    def _():
        with jax.named_scope("part 1"):
            pass_part(1)

    with jax.named_scope("taps out"):
        for s in range(1, 4):
            tap_from(OUTED, near[s])
            tap_cross[s].start()

    to_sib[2].wait_recv()
    with jax.named_scope("pair wait"):
        for copy in to_cross:
            copy.wait_recv()
    with jax.named_scope("weight sums"):
        dgu_ref[...] = (
            part[3, :slab].astype(F32) + sib_in[1, :slab].astype(F32) + cross_in[:slab].astype(F32)
        ).astype(BF16)
        dd_ref[...] = (
            part[3, slab:].astype(F32) + sib_in[1, slab:].astype(F32) + cross_in[slab:].astype(F32)
        ).astype(BF16)

    with jax.named_scope("taps cross"):
        for copy in tap_cross:
            copy.wait_recv()

    gf_sib = [
        link(SIB, gf_ref.at[q], gf_ref.at[q], "seq", sib, SIBBED),
        link(SIB + 1, gf_ref.at[cross], gf_ref.at[cross], "seq", sib, SIBBED + 1),
    ]
    for copy in w_sib:
        copy.wait_send()
    for copy in gf_sib:
        copy.start()
    with jax.named_scope("last waits"):
        for copy in gin_out:
            copy.wait_recv()
        for copy in gf_sib:
            copy.wait_recv()
        for d in range(3):
            for part in range(2):
                spread(part, cot_of(part), d, False)
                spread(2 + part, tok_of(part), d, False)

        @pl.when(middle)
        def _():
            for copy in to_cross[4:] + passed:
                copy.wait_send()

        @pl.when(end)
        def _():
            for copy in around:
                copy.wait_send()

        for copy in (
            w_cross + w_group + w_far[0] + w_far[1] + weighs + gate_sums + backs + to_sib
            + to_cross[:4] + tap_in + tap_out + tap_cross + g_slabs + gin_out + gf_sib
        ):
            copy.wait_send()


def finish_kernel(
    gin_ref, gg_ref, gf_ref, dgu_ref, dd_ref,
    gin_out, gg_out, gf_out, dg_out, du_out, dd_out, wide, sem,
):
    slab = gin_ref.shape[2]
    ff = dg_out.shape[2]
    copies = [
        (gin_ref.at[k], gin_out.at[:, pl.ds(k * slab, slab)]) for k in range(4)
    ] + [
        (dgu_ref.at[:, pl.ds(0, ff)], dg_out.at[0]), (dgu_ref.at[:, pl.ds(ff, ff)], du_out.at[0]),
        (dd_ref, dd_out.at[0]), (gg_ref, gg_out),
    ]
    copies = [pltpu.make_async_copy(a, b, sem.at[n]) for n, (a, b) in enumerate(copies)]
    for copy in copies:
        copy.start()
    piece = gf_ref.shape[2]
    for a in range(4):
        span = pl.ds(a * piece, piece)
        for k in range(4):
            wide[span, pl.ds(k * slab, slab)] = gf_ref[k, a].astype(F32)
        copies.append(pltpu.make_async_copy(wide.at[span], gf_out.at[span], sem.at[8 + a]))
        copies[-1].start()
    for copy in copies:
        copy.wait()


def dense_body(inputs, grad_out, gates, expert_ids, slot_index, filter_taps, w_gate, w_up, w_down):
    tok, width = inputs.shape
    taps = filter_taps.shape[0]
    ff = w_gate.shape[2]
    top = gates.shape[1]
    length = 4 * tok
    size = taps + length
    slab = width // 4
    rows = slab + ff // 4
    vm = lambda *shape: pltpu.VMEM(shape, BF16)
    vf = lambda *shape: pltpu.VMEM(shape, F32)
    st = lambda *shape: jax.ShapeDtypeStruct(shape, BF16)
    near = pl.BlockSpec(memory_space=pltpu.VMEM)
    hbm = pl.BlockSpec(memory_space=pltpu.HBM)
    far_away = lambda array: pltpu.with_memory_space_constraint(array, pltpu.HBM)
    fh, fl, ih, il = transforms(size)
    outs = pl.pallas_call(
        dense_kernel,
        out_shape=(
            vm(4, tok, slab), vm(top, tok), vm(4, 4, taps // 4, slab), vm(slab, 2 * ff),
            vm(ff // 4, width),
        ),
        in_specs=[hbm] * 13,
        out_specs=(near,) * 5,
        scratch_shapes=[
            vm(top, tok), pltpu.VMEM((top, tok), jnp.int32), pltpu.VMEM((top, tok), jnp.int32),
            vm(size, length), vm(size, length), vm(length, size), vm(length, size), vm(taps, slab),
            vf(size, slab), vf(size, slab), vf(size, slab),
            vm(4, tok, slab), vm(4, tok, slab), vm(4, tok, slab), vm(4, tok, slab),
            vm(4, 4, tok, slab), vm(4, tok, width), vm(4, slab, 2 * ff), vm(4, ff // 4, width),
            vm(length, ff), vm(length, 2 * ff), vm(length, width),
            vm(4, 4, tok, slab), vm(4, 4, tok, slab), vm(2, 4, tok, slab), vm(4, tok, slab),
            vm(4, rows, width), vm(2, rows, width), vm(rows, width), vm(rows, width), vm(2, rows // PARTS, width),
            vm(4, taps // 4, slab), vm(4, taps // 4, slab),
            vf(4, 8, tok), vf(4, 8, tok), vf(4, 8, tok),
            pltpu.SemaphoreType.DMA((13,)),
            pltpu.SemaphoreType.DMA((77,)), pltpu.SemaphoreType.DMA((73,)),
        ],
        compiler_params=pltpu.CompilerParams(
            collective_id=0, has_side_effects=True, vmem_limit_bytes=48 * 1024 * 1024
        ),
    )(
        *[far_away(m) for m in (inputs, grad_out, gates.T, expert_ids.T, slot_index.T)],
        *[far_away(m) for m in (w_gate, w_up, w_down, filter_taps)],
        *[far_away(jnp.asarray(m)) for m in (fh[:, :length], fl[:, :length], ih[:length], il[:length])],
    )
    grads = pl.pallas_call(
        finish_kernel,
        out_shape=(
            st(tok, width), st(top, tok), jax.ShapeDtypeStruct((taps, width), F32),
            st(*w_gate.shape), st(*w_up.shape), st(*w_down.shape),
        ),
        in_specs=[near] * 5,
        out_specs=(hbm,) * 6,
        scratch_shapes=[vf(taps, width), pltpu.SemaphoreType.DMA((12,))],
        compiler_params=pltpu.CompilerParams(vmem_limit_bytes=8 * 1024 * 1024),
    )(*[pltpu.with_memory_space_constraint(array, pltpu.VMEM) for array in outs])
    return (grads[0], grads[1].T) + grads[2:]


def body_of(mesh):
    def body(*args):
        top_count = args[3].shape[1]
        tok, taps, dq = args[0].shape[0], args[5].shape[0], args[6].shape[1]
        small = mesh.shape["expert"] == top_count == 4 and mesh.shape["seq"] == 4
        small = small and mesh.shape["groups"] == 2
        if small and tok == 128 and taps == 2 * tok and dq == 2 * tok and 2 * args[6].shape[2] == args[0].shape[1]:
            return dense_body(*args)
        return routed_body(*args)

    return body


def solution(mesh):
    return jax.shard_map(
        body_of(mesh),
        mesh=mesh,
        in_specs=(
            P(("groups", "expert", "seq"), None),
            P(("groups", "expert", "seq"), None),
            P(("groups", "expert", "seq"), None),
            P(("groups", "expert", "seq"), None),
            P(("groups", "expert", "seq"), None),
            P(),
            P("expert", "seq", None),
            P("expert", "seq", None),
            P("expert", "seq", None),
        ),
        out_specs=(
            P(("groups", "expert", "seq"), None),
            P(("groups", "expert", "seq"), None),
            P("groups", None),
            P(("groups", "expert"), "seq", None),
            P(("groups", "expert"), "seq", None),
            P(("groups", "expert"), "seq", None),
        ),
        check_vma=False,
    )
```

```python
import functools

import jax
import jax.numpy as jnp
import numpy as np
from jax import lax
from jax.experimental import pallas as pl
from jax.experimental.pallas import tpu as pltpu
from jax.sharding import PartitionSpec as P

MESH = pl.DeviceIdType.MESH
F32 = jnp.float32
BF16 = jnp.bfloat16


def from_behind(block, axis, distance):
    devices = range(lax.axis_size(axis))
    route = [(i - distance, i) for i in devices if i - distance in devices]
    return lax.ppermute(block, axis, route)


def depthwise(signal, kernel):
    return lax.conv_general_dilated(
        signal[None],
        kernel[:, None, :],
        (1,),
        "VALID",
        dimension_numbers=("NWC", "WIO", "NWC"),
        feature_group_count=signal.shape[1],
        preferred_element_type=jnp.float32,
    )[0]


def contract(left, right, left_dim, right_dim):
    return lax.dot_general(
        left, right, (((left_dim,), (right_dim,)), ((), ())), preferred_element_type=jnp.float32
    )


def expert_pass(token_rows, scaled_rows, gate_mat, up_mat, down_mat):
    pre_gate = jnp.dot(token_rows, gate_mat, preferred_element_type=jnp.float32)
    pre_up = jnp.dot(token_rows, up_mat, preferred_element_type=jnp.float32)
    sigma = jax.nn.sigmoid(pre_gate)
    swish = pre_gate * sigma
    hidden = (swish * pre_up).astype(jnp.bfloat16)
    outputs = jnp.dot(hidden, down_mat, preferred_element_type=jnp.float32).astype(jnp.bfloat16)
    grad_hidden = contract(scaled_rows, down_mat, 1, 1)
    grad_pre_gate = (grad_hidden * pre_up * (sigma * (1.0 + pre_gate * (1.0 - sigma)))).astype(
        jnp.bfloat16
    )
    grad_pre_up = (grad_hidden * swish).astype(jnp.bfloat16)
    part_gate = contract(token_rows, grad_pre_gate, 0, 0)
    part_up = contract(token_rows, grad_pre_up, 0, 0)
    part_down = contract(hidden, scaled_rows, 0, 0)
    grad_rows = (
        contract(grad_pre_gate, gate_mat, 1, 1) + contract(grad_pre_up, up_mat, 1, 1)
    ).astype(jnp.bfloat16)
    return (grad_rows, outputs, (part_gate, part_up, part_down))


def routed_body(inputs, grad_out, gates, expert_ids, slot_index, filter_taps, w_gate, w_up, w_down):
    tok_count, width = inputs.shape
    taps = filter_taps.shape[0]
    top_count = expert_ids.shape[1]
    experts = lax.axis_size("expert")
    capacity = tok_count * top_count // experts
    reach = taps - 1
    shift_count = (reach + tok_count - 1) // tok_count
    earlier = [from_behind(inputs, "seq", shift_by) for shift_by in range(shift_count, 0, -1)]
    extended = jnp.concatenate(earlier + [inputs], axis=0)[-(tok_count + reach) :]
    filtered = depthwise(extended, filter_taps[::-1]).astype(jnp.bfloat16)
    kept = slot_index < capacity
    dest = jnp.where(kept, expert_ids * capacity + slot_index, experts * capacity).reshape(-1)

    def place(values):
        rest = values.shape[1:]
        empty = jnp.zeros((experts * capacity,) + rest, values.dtype)
        return empty.at[dest].set(values, mode="drop").reshape((experts, capacity) + rest)

    def fetch(buffer):
        rest = buffer.shape[2:]
        flat = buffer.reshape((experts * capacity,) + rest)
        return jnp.take(flat, dest, axis=0, mode="fill", fill_value=0).reshape(
            (tok_count, top_count) + rest
        )

    token_send = place(
        jnp.broadcast_to(filtered[:, None, :], (tok_count, top_count, width)).reshape(-1, width)
    )
    gate_full, up_full, down_full = (
        lax.all_gather(w_gate, "seq", axis=1, tiled=True),
        lax.all_gather(w_up, "seq", axis=1, tiled=True),
        lax.all_gather(w_down, "seq", axis=1, tiled=True),
    )
    gate_mat = gate_full[0]
    up_mat = up_full[0]
    down_mat = down_full[0]
    scaled = (
        gates.astype(jnp.float32)[:, :, None] * grad_out.astype(jnp.float32)[:, None, :]
    ).astype(jnp.bfloat16)
    token_recv, scaled_recv = (
        lax.all_to_all(token_send, "expert", split_axis=0, concat_axis=0, tiled=True),
        lax.all_to_all(
            place(scaled.reshape(-1, width)), "expert", split_axis=0, concat_axis=0, tiled=True
        ),
    )
    grad_rows, outputs, partials = expert_pass(
        token_recv.reshape(-1, width), scaled_recv.reshape(-1, width), gate_mat, up_mat, down_mat
    )
    grad_back, output_back = (
        lax.all_to_all(
            grad_rows.reshape(experts, capacity, width),
            "expert",
            split_axis=0,
            concat_axis=0,
            tiled=True,
        ),
        lax.all_to_all(
            outputs.reshape(experts, capacity, width),
            "expert",
            split_axis=0,
            concat_axis=0,
            tiled=True,
        ),
    )
    output_rows = fetch(output_back)
    grad_gates = jnp.sum(
        grad_out.astype(jnp.float32)[:, None, :] * output_rows.astype(jnp.float32), axis=2
    ).astype(jnp.bfloat16)
    summed_gate, summed_up, summed_down = (
        lax.psum_scatter(
            partials[0][None].astype(jnp.bfloat16), "seq", scatter_dimension=1, tiled=True
        ).astype(jnp.float32),
        lax.psum_scatter(
            partials[1][None].astype(jnp.bfloat16), "seq", scatter_dimension=1, tiled=True
        ).astype(jnp.float32),
        lax.psum_scatter(
            partials[2][None].astype(jnp.bfloat16), "seq", scatter_dimension=1, tiled=True
        ).astype(jnp.float32),
    )
    grad_filtered = jnp.sum(fetch(grad_back).astype(jnp.float32), axis=1).astype(jnp.bfloat16)
    later = [from_behind(grad_filtered, "seq", -shift_by) for shift_by in range(1, shift_count + 1)]
    grad_extended = jnp.concatenate([grad_filtered] + later, axis=0)[: tok_count + reach]
    grad_inputs = depthwise(grad_extended, filter_taps).astype(jnp.bfloat16)
    local_taps = depthwise(extended, grad_filtered)[::-1]
    grad_filter = lax.psum(local_taps, ("expert", "seq"))
    return (
        grad_inputs,
        grad_gates,
        grad_filter,
        summed_gate.astype(jnp.bfloat16),
        summed_up.astype(jnp.bfloat16),
        summed_down.astype(jnp.bfloat16),
    )


def transforms(size):
    freq = 2.0 * np.pi * (np.arange(size // 2) + 0.5) / size
    angle = freq[:, None] * np.arange(size)[None, :]
    forward = np.concatenate([np.cos(angle), np.sin(angle)], axis=0)
    inverse = forward.T * (2.0 / size)

    def pieces(matrix):
        high = matrix.astype(jnp.bfloat16)
        low = (matrix - high.astype(np.float64)).astype(jnp.bfloat16)
        return high, low

    return pieces(forward) + pieces(inverse)


def mm(left, right):
    return jnp.dot(left, right, preferred_element_type=F32)


def turned(left, right):
    return lax.dot_general(left, right, (((1,), (1,)), ((), ())), preferred_element_type=F32)


def across(left, right):
    return lax.dot_general(left, right, (((0,), (0,)), ((), ())), preferred_element_type=F32)


PIECES = 3
PARTS = 6


def dense_kernel(
    rows_ref, cot_ref, gates_ref, ids_ref, slots_ref, wg_ref, wu_ref, wd_ref, taps_ref,
    fh_ref, fl_ref, ih_ref, il_ref,
    gin_ref, gg_ref, gf_ref, dgu_ref, dd_ref,
    gates_in, ids_in, slots_in, fh, fl, ih, il, taps, x_spec, tap_spec, g_spec, seq_x, seq_f, seq_g, seq_in,
    tall, gall, wgu, wdn, hid, gpre, scaled, back, rall, pre_in, gfb,
    part, sib_in, pair, cross_in, relay_in, gfz, gfz_in,
    weigh, sums, sums_in,
    load_sem, send_sem, recv_sem,
):
    g = lax.axis_index("groups")
    z = lax.axis_index("expert")
    q = lax.axis_index("seq")
    tok, width = rows_ref.shape
    slab = width // 4
    ff = hid.shape[1]
    fq = ff // 4
    size = x_spec.shape[0]
    half = size // 2
    n_taps = taps.shape[0]
    piece = n_taps // 4
    length = 4 * tok
    sib = q + 1 - 2 * (q % 2)
    cross = (q + 2) % 4
    far = (sib + 2) % 4
    middle = jnp.logical_or(z == 1, z == 2)
    end = jnp.logical_or(z == 0, z == 3)

    across_end = {
        "expert": jnp.where(z < 2, 1 - z, 5 - z), "seq": cross
    }
    barrier = pltpu.get_barrier_semaphore()
    pl.semaphore_signal(barrier, inc=1, device_id=across_end, device_id_type=MESH)
    for s in range(1, 4):
        pl.semaphore_signal(barrier, inc=1, device_id={"expert": (z + s) % 4}, device_id_type=MESH)
        pl.semaphore_signal(barrier, inc=1, device_id={"seq": (q + s) % 4}, device_id_type=MESH)
    pl.semaphore_signal(barrier, inc=1, device_id={"groups": 1 - g}, device_id_type=MESH)

    def slab_at(k):
        return pl.ds(pl.multiple_of(k * slab, slab), slab)

    loads = [
        pltpu.make_async_copy(src, dst, load_sem.at[n])
        for n, (src, dst) in enumerate([
            (cot_ref, gall.at[z]),
            (gates_ref, gates_in), (ids_ref, ids_in), (slots_ref, slots_in),
            (rows_ref.at[:, slab_at(q)], seq_x.at[q]),
            (wg_ref.at[0], wgu.at[q, :, pl.ds(0, ff)]),
            (wu_ref.at[0], wgu.at[q, :, pl.ds(ff, ff)]),
            (wd_ref.at[0], wdn.at[q]),
            (taps_ref.at[:, slab_at(q)], taps),
            (fh_ref, fh), (fl_ref, fl), (ih_ref, ih), (il_ref, il),
        ])
    ]
    for load in loads:
        load.start()

    def link(n, src, dst, axis, peer, arrival):
        device = peer if isinstance(peer, dict) else {axis: peer}
        return pltpu.make_async_remote_copy(
            src_ref=src, dst_ref=dst, send_sem=send_sem.at[n],
            recv_sem=recv_sem.at[arrival], device_id=device, device_id_type=MESH,
        )

    def pick(a, b, c, d):
        return jnp.where(z == 0, a, jnp.where(z == 1, b, jnp.where(z == 2, c, d)))

    GATHER, WEIGH, SUM, BACK, SLAB, ROW, WEIGHT, SIB, RELAY, FIRST = 0, 24, 27, 30, 32, 35, 38, 50, 52, 54
    TAP, OUT, LAST, PART, HALF = 0, 8, 16, WEIGHT, WEIGHT + 6
    GATHERED, WEIGHED, SUMMED, BACKED, SLABBED, ROWED, WEIGHTED, SIBBED = 0, 16, 20, 24, 30, 33, 36, 48
    PARTED, RELAYED, LASTED = 50, 56, 57
    TAPPED, OUTED, HALVED = 0, 8, WEIGHTED

    def hop(base, view, origin, step, distance):
        return link(
            GATHER + 6 * base + (0 if step > 0 else 3) + distance, view(origin), view(origin),
            "expert", (z + 4 + step) % 4, GATHERED + 4 * base + origin,
        )

    def spread(base, view, distance, send=True):
        for step in (1, -1):
            origin = z - step * distance
            has_origin = origin >= 0 if step > 0 else origin <= 3
            has_next = z < 3 if step > 0 else z > 0

            @pl.when(has_origin)
            def _(origin=origin, has_next=has_next, step=step):
                if distance and send:
                    hop(base, view, origin, step, 0).wait_recv()

                if distance < 3:
                    @pl.when(has_next)
                    def _():
                        if send:
                            hop(base, view, origin, step, distance).start()
                        else:
                            hop(base, view, origin, step, distance).wait_send()

    def cot_ahead(distance, first, last=2):
        for part in range(first, last):
            spread(part, cot_of(part), distance)

    def rows_ahead(distance, first, last=2):
        for part in range(first, last):
            spread(2 + part, tok_of(part), distance)

    def cot_of(part):
        return lambda origin: gall.at[origin, pl.ds(part * (tok // 2), tok // 2)]

    def tok_of(part):
        return lambda origin: tall.at[:, origin, pl.ds(part * (tok // 2), tok // 2)]

    for load in loads[:4]:
        load.wait()
    ids = ids_in[...]
    kept = slots_in[...] < tok
    held = jnp.where(kept, gates_in[...].astype(F32), 0.0)
    eye = lax.broadcasted_iota(jnp.int32, (tok, tok), 0) == lax.broadcasted_iota(
        jnp.int32, (tok, tok), 1
    )

    def as_row(column):
        return jnp.sum(jnp.where(eye, column, 0.0), axis=0, keepdims=True)

    def as_column(row):
        return jnp.sum(jnp.where(eye, row, 0.0), axis=1, keepdims=True)

    weigh[z] = jnp.zeros(weigh.shape[1:], F32)
    for e in range(4):
        weigh[z, e:e + 1] = jnp.sum(jnp.where(ids == e, held, 0.0), axis=0, keepdims=True)

    with jax.named_scope("entry"):
        pl.semaphore_wait(barrier, 8)

    cot_ahead(0, 0)

    def to_others(send, arrive, source, dest):
        return [
            link(send + s, source((q + s) % 4), dest, "seq", (q + s) % 4, arrive + s)
            for s in (2, 1, 3)
        ]

    to_slabs = to_others(
        SLAB - 1, SLABBED - 1, lambda k: rows_ref.at[:, slab_at(k)], seq_x.at[q]
    )
    for copy in to_slabs:
        copy.start()
    for load in loads[4:9]:
        load.wait()

    step = (slab + fq) // (2 * PIECES)
    wide_pieces = slab // (2 * step)

    def piece_of(k, n, part):
        if n < wide_pieces:
            return wgu.at[k, pl.ds(pl.multiple_of((2 * n + part) * step, step), step)]
        at = pl.multiple_of((2 * (n - wide_pieces) + part) * step, step)
        return wdn.at[k, pl.ds(at, step)]

    def weight_copy(kind, source, n, part, axis, peer):
        at = kind * PIECES + n
        return link(
            WEIGHT + at, piece_of(source, n, part), piece_of(source, n, part), axis, peer,
            WEIGHTED + at,
        )

    w_cross = [weight_copy(0, q, n, g, "seq", cross) for n in range(PIECES)]
    w_group = [weight_copy(1, cross, n, g, "groups", 1 - g) for n in range(PIECES)]
    w_far = [
        [weight_copy(2 + h, cross, n, (g + h) % 2, "seq", sib) for n in range(PIECES)]
        for h in range(2)
    ]

    def pass_on(n):
        w_cross[n].wait_recv()
        w_group[n].start()
        w_far[0][n].start()

    def take(n):
        w_group[n].wait_recv()
        w_far[1][n].start()

    w_sib = [
        link(SIB, wgu.at[q], wgu.at[q], "seq", sib, SIBBED),
        link(SIB + 1, wdn.at[q], wdn.at[q], "seq", sib, SIBBED + 1),
    ]
    weighs = [
        link(WEIGH + s - 1, weigh.at[z], weigh.at[z], "expert", (z + s) % 4, WEIGHED + z)
        for s in range(1, 4)
    ]
    for copy in weighs + w_sib:
        copy.start()

    def forward(dest, count, values, exact=True):
        for at in range(0, size, slab):
            span = pl.ds(at, slab)
            dest[span] = mm(fh[span, :count], values)
            if exact:
                dest[span] += mm(fl[span, :count], values)

    def backward(count, spec, exact=True):
        high = spec.astype(BF16)
        if not exact:
            return mm(ih[:count], high)
        low = (spec - high.astype(F32)).astype(BF16)
        return mm(ih[:count], high) + mm(il[:count], high) + mm(ih[:count], low)

    def whole(ref):
        return ref[...].reshape(length, slab)

    for load in loads[9:]:
        load.wait()
    with jax.named_scope("tap spectrum"):
        forward(tap_spec, n_taps, taps[...])
    with jax.named_scope("x wait"):
        for copy in to_slabs:
            copy.wait_recv()
    w_cross[0].start()
    with jax.named_scope("cot 1 first"):
        cot_ahead(1, 0, 1)
    with jax.named_scope("filter"):
        forward(x_spec, length, whole(seq_x))
        xc, xs = x_spec[:half], x_spec[half:]
        hc, hs = tap_spec[:half], tap_spec[half:]
        prod = jnp.concatenate([xc * hc - xs * hs, xc * hs + xs * hc], axis=0)
        seq_f[...] = backward(length, prod).astype(BF16).reshape(4, tok, slab)
    to_rows = to_others(ROW - 1, ROWED - 1, lambda k: seq_f.at[k], tall.at[q, z])
    for copy in to_rows + w_cross[1:]:
        copy.start()
    tall[q, z] = seq_f[q]
    with jax.named_scope("cot 1"):
        cot_ahead(1, 1)
    with jax.named_scope("rows wait"):
        for copy in to_rows:
            copy.wait_recv()
    rows_ahead(0, 0)
    with jax.named_scope("pass 0"):
        pass_on(0)
    with jax.named_scope("pass 1"):
        pass_on(1)

    @pl.when(middle)
    def _():
        with jax.named_scope("rows 1 first"):
            rows_ahead(1, 0, 1)

    with jax.named_scope("pass 2"):
        pass_on(2)
    with jax.named_scope("take 0"):
        take(0)

    @pl.when(middle)
    def _():
        with jax.named_scope("rows 1"):
            rows_ahead(1, 1)
        with jax.named_scope("cot 2"):
            cot_ahead(2, 0)

    with jax.named_scope("take 1"):
        take(1)
    with jax.named_scope("weigh wait"):
        for k in range(1, 4):
            peer = (z + k) % 4
            link(WEIGH, weigh.at[peer], weigh.at[peer], "expert", peer, WEIGHED + peer).wait_recv()

    @pl.when(middle)
    def _():
        with jax.named_scope("rows 2 middle first"):
            rows_ahead(2, 0, 1)

    with jax.named_scope("take 2"):
        take(2)
    with jax.named_scope("weights wait"):
        for copy in w_sib + w_far[0] + w_far[1]:
            copy.wait_recv()

    origins = [z, pick(2, 3, 0, 1), pick(1, 0, 3, 2), pick(3, 2, 1, 0)]
    sublanes = lax.broadcasted_iota(jnp.int32, weigh.shape[1:], 0)
    gate_sums = [
        link(SUM + s - 1, sums.at[s], sums_in.at[z], "expert", origins[s], SUMMED + z)
        for s in range(1, 4)
    ]
    backs = [
        link(BACK + s - 2, back.at[s], rall.at[z], "expert", origins[s], BACKED + z)
        for s in range(2, 4)
    ]
    to_pre = link(FIRST, back.at[1], pre_in.at[0], "expert", 3 - z, BACKED + 4)
    to_next = link(FIRST, back.at[1], pre_in.at[1], "expert", origins[2], BACKED + 5)

    def block(s):
        origin = origins[s]
        span = pl.ds(pl.multiple_of(origin * tok, tok), tok)
        pre = mm(tall[0, origin], wgu[0])
        for k in range(1, 4):
            pre += mm(tall[k, origin], wgu[k])
        cot = gall[origin]
        weight = as_column(
            jnp.sum(jnp.where(sublanes == z, weigh[origin], 0.0), axis=0, keepdims=True)
        )
        raw = turned(cot, wdn[...].reshape(ff, width))
        gate, up = pre[:, :ff], pre[:, ff:]
        sigma = jax.nn.sigmoid(gate)
        swish = gate * sigma
        hidden = (swish * up).astype(BF16)
        gg = jnp.sum(hidden.astype(F32) * raw, axis=1, keepdims=True)
        grad_hidden = raw * weight
        grad_gate = grad_hidden * up * (sigma * (1.0 + gate * (1.0 - sigma)))
        gp = jnp.concatenate([grad_gate.astype(BF16), (grad_hidden * swish).astype(BF16)], axis=1)
        hid[span] = hidden
        gpre[span] = gp
        scaled[span] = (weight * cot.astype(F32)).astype(BF16)
        target, at = (back, s) if s else (rall, z)
        for k in range(4):
            target[at, k] = turned(gp, wgu[k]).astype(BF16)
        (sums if s else sums_in)[at] = jnp.broadcast_to(as_row(gg), sums.shape[1:])

    with jax.named_scope("block 0"):
        block(0)

    @pl.when(middle)
    def _():
        with jax.named_scope("rows 2 middle"):
            rows_ahead(2, 1)

    @pl.when(end)
    def _():
        with jax.named_scope("rows 2 end"):
            cot_ahead(2, 0)
            rows_ahead(2, 0)

    with jax.named_scope("block 1"):
        block(1)
    gate_sums[0].start()

    @pl.when(middle)
    def _():
        to_pre.start()

    @pl.when(end)
    def _():
        to_next.start()
        with jax.named_scope("rows 1 end"):
            rows_ahead(1, 0)

    with jax.named_scope("block 2"):
        block(2)
    gate_sums[1].start()

    @pl.when(end)
    def _():
        backs[0].start()
        with jax.named_scope("rows 3"):
            cot_ahead(3, 0)
            rows_ahead(3, 0)

    with jax.named_scope("block 3"):
        block(3)
    gate_sums[2].start()

    @pl.when(end)
    def _():
        backs[1].start()

    def partial_low(slot, dest):
        thin = pl.ds(pl.multiple_of(dest * fq, fq), fq)
        part[slot, slab:] = across(hid[:, thin], scaled[...]).astype(BF16)

    def partial_top(slot, dest):
        top = across(tall[dest].reshape(length, slab), gpre[...])
        part[slot, :slab] = top.astype(BF16)

    rows = slab + fq
    share = rows // PARTS
    low, top = pl.ds(slab, fq), pl.ds(0, slab)
    to_sib = [
        link(HALF, part.at[0, low], sib_in.at[0, low], "seq", sib, HALVED),
        link(HALF + 1, part.at[0, top], sib_in.at[0, top], "seq", sib, HALVED + 1),
        link(HALF + 2, part.at[1], sib_in.at[1], "seq", sib, HALVED + 2),
    ]
    to_cross = [
        link(
            PART + n, pair.at[pl.ds(n * share, share)], cross_in.at[pl.ds(n * share, share)],
            "seq", cross, PARTED + n,
        )
        for n in [*range(slab // share, PARTS), *range(slab // share)]
    ]
    near_end = pick(1, 0, 3, 2)
    last = pl.ds((slab // share - 1) * share, share)
    around = link(FIRST + 1, pair.at[last], relay_in, "", across_end, RELAYED)
    passed = link(
        RELAY, relay_in, cross_in.at[last], "expert", near_end, PARTED + slab // share - 1
    )

    for copy in w_cross + w_group + w_far[0] + w_far[1]:
        copy.wait_send()
    with jax.named_scope("partial 0"):
        partial_low(0, far)
        to_sib[0].start()
        partial_top(0, far)
        to_sib[1].start()
    with jax.named_scope("partial 2"):
        partial_low(2, cross)
        to_sib[0].wait_recv()
        pair[low] = (part[2, low].astype(F32) + sib_in[0, low].astype(F32)).astype(BF16)
        for copy in to_cross[:2]:
            copy.start()
        partial_top(2, cross)
        to_sib[1].wait_recv()
        pair[top] = (part[2, top].astype(F32) + sib_in[0, top].astype(F32)).astype(BF16)
        to_cross[2].start()

    @pl.when(end)
    def _():
        around.start()

    @pl.when(middle)
    def _():
        for copy in to_cross[3:5]:
            copy.start()

    with jax.named_scope("partial 1"):
        partial_low(1, sib)
        partial_top(1, sib)
    to_sib[2].start()
    with jax.named_scope("partial 3"):
        partial_low(3, q)
        partial_top(3, q)

    @pl.when(middle)
    def _():
        with jax.named_scope("pre wait"):
            to_pre.wait_recv()
        back[2] = (back[2].astype(F32) + pre_in[0].astype(F32)).astype(BF16)
        backs[0].start()
        with jax.named_scope("next wait"):
            to_next.wait_recv()
        back[3] = (back[3].astype(F32) + pre_in[1].astype(F32)).astype(BF16)
        backs[1].start()

    for d in range(3):
        for h in range(2):
            spread(h, cot_of(h), d, False)
            spread(2 + h, tok_of(h), d, False)

    with jax.named_scope("back wait"):
        for s in (1, 3):
            peer = (z + s) % 4
            link(BACK, back.at[1], rall.at[peer], "expert", peer, BACKED + peer).wait_recv()

    total = rall[z].astype(F32)
    for s in (1, 3):
        total += rall[(z + s) % 4].astype(F32)
    gfb[...] = total.astype(BF16)
    seq_g[q] = gfb[q]
    for copy in to_slabs:
        copy.wait_send()
    g_slabs = to_others(SLAB - 1, SLABBED - 1, lambda k: gfb.at[k], seq_g.at[q])
    for copy in g_slabs:
        copy.start()

    @pl.when(middle)
    def _():
        with jax.named_scope("part 0"):
            around.wait_recv()
            passed.start()

    for s in range(1, 4):
        peer = (z + s) % 4
        link(SUM, sums.at[s], sums_in.at[peer], "expert", peer, SUMMED + peer).wait_recv()
    gate_grads = jnp.zeros(ids.shape, F32)
    for s in range(4):
        gate_grads += jnp.where(ids == s, sums_in[s, 0:1], 0.0)
    gg_ref[...] = jnp.where(kept, gate_grads, 0.0).astype(BF16)

    with jax.named_scope("grad wait"):
        for copy in g_slabs:
            copy.wait_recv()

    @pl.when(middle)
    def _():
        to_cross[5].start()

    @pl.when(end)
    def _():
        to_cross[3].start()

    with jax.named_scope("tap grad"):
        forward(g_spec, length, whole(seq_g), False)
        gc, gs = g_spec[:half], g_spec[half:]
        xc, xs = x_spec[:half], x_spec[half:]
        prod = jnp.concatenate([gc * xc + gs * xs, gs * xc - gc * xs], axis=0)
        gfz[...] = backward(n_taps, prod, False).astype(BF16).reshape(4, piece, slab)
    near = [z, pick(1, 2, 1, 2), pick(2, 0, 3, 1), pick(3, 3, 0, 0)]
    fold = piece // 2

    def fold_of(ref, h, *at):
        return ref.at[*at, pl.ds(h * fold, fold)]

    tap_in = [
        link(
            TAP + 4 * h + s, fold_of(gfz, h, near[s]), fold_of(gfz_in, h, z), "expert", near[s],
            TAPPED + 4 * h + z,
        )
        for h in range(2) for s in (3, 2, 1)
    ]
    tap_out = [
        [
            link(
                OUT + 4 * h + s, fold_of(gf_ref, h, q, z), fold_of(gf_ref, h, q, z), "expert", near[s],
                OUTED + 4 * h + z,
            )
            for s in (3, 2, 1)
        ]
        for h in range(2)
    ]
    tap_cross = [
        [
            link(
                LAST + 4 * h + s, fold_of(gf_ref, h, q, near[s]), fold_of(gf_ref, h, q, near[s]), "seq",
                cross, LASTED + 4 * h + near[s],
            )
            for s in range(4)
        ]
        for h in range(2)
    ]
    for copy in tap_in:
        copy.start()

    with jax.named_scope("input grad"):
        gc, gs = g_spec[:half], g_spec[half:]
        hc, hs = tap_spec[:half], tap_spec[half:]
        prod = jnp.concatenate([gc * hc + gs * hs, gs * hc - gc * hs], axis=0)
        seq_in[...] = backward(length, prod).astype(BF16).reshape(4, tok, slab)
    for copy in to_rows:
        copy.wait_send()
    gin_out = to_others(ROW - 1, ROWED - 1, lambda k: seq_in.at[k], gin_ref.at[q])
    for copy in gin_out:
        copy.start()
    gin_ref[q] = seq_in[q]

    @pl.when(end)
    def _():
        to_cross[4].start()

    def tap_from(base, peer):
        link(TAP, fold_of(gfz, 0, 0), fold_of(gfz_in, 0, 0), "expert", peer, base + peer).wait_recv()

    with jax.named_scope("taps in"):
        for h in range(2):
            rows_h = pl.ds(h * fold, fold)
            mine = gfz[z, rows_h].astype(F32)
            for s in range(1, 4):
                tap_from(TAPPED + 4 * h, near[s])
                mine += gfz_in[near[s], rows_h].astype(F32)
            gf_ref[q, z, rows_h] = mine.astype(BF16)
            for copy in tap_out[h] + tap_cross[h][:1]:
                copy.start()

    with jax.named_scope("taps out"):
        for h in range(2):
            for s in range(1, 4):
                tap_from(OUTED + 4 * h, near[s])
                tap_cross[h][s].start()

    gf_sib = [
        link(SIB, gf_ref.at[q], gf_ref.at[q], "seq", sib, SIBBED),
        link(SIB + 1, gf_ref.at[cross], gf_ref.at[cross], "seq", sib, SIBBED + 1),
    ]
    for copy in w_sib:
        copy.wait_send()
    gf_sib[0].start()
    to_sib[2].wait_recv()
    with jax.named_scope("pair wait"):
        for copy in to_cross:
            copy.wait_recv()
    with jax.named_scope("weight sums"):
        dgu_ref[...] = (
            part[3, :slab].astype(F32) + sib_in[1, :slab].astype(F32) + cross_in[:slab].astype(F32)
        ).astype(BF16)
        dd_ref[...] = (
            part[3, slab:].astype(F32) + sib_in[1, slab:].astype(F32) + cross_in[slab:].astype(F32)
        ).astype(BF16)

    with jax.named_scope("taps cross"):
        for copy in tap_cross[0] + tap_cross[1]:
            copy.wait_recv()

    gf_sib[1].start()
    with jax.named_scope("last waits"):
        for copy in gin_out:
            copy.wait_recv()
        for copy in gf_sib:
            copy.wait_recv()
        @pl.when(middle)
        def _():
            for copy in to_cross[5:] + [passed]:
                copy.wait_send()

        @pl.when(end)
        def _():
            around.wait_send()

        for copy in (
            weighs + gate_sums + [to_pre] + backs + to_sib
            + to_cross[:5] + tap_in + tap_out[0] + tap_out[1] + tap_cross[0] + tap_cross[1] + g_slabs + gin_out + gf_sib
        ):
            copy.wait_send()


def finish_kernel(
    gin_ref, gg_ref, gf_ref, dgu_ref, dd_ref,
    gin_out, gg_out, gf_out, dg_out, du_out, dd_out, wide, sem,
):
    slab = gin_ref.shape[2]
    ff = dg_out.shape[2]
    pieces = [
        (gin_ref.at[k], gin_out.at[:, pl.ds(k * slab, slab)]) for k in range(4)
    ] + [
        (dgu_ref.at[:, pl.ds(0, ff)], dg_out.at[0]), (dgu_ref.at[:, pl.ds(ff, ff)], du_out.at[0]),
        (dd_ref, dd_out.at[0]), (gg_ref, gg_out),
    ]
    piece = gf_ref.shape[2]
    copies = []

    def send(source, dest):
        copies.append(pltpu.make_async_copy(source, dest, sem.at[len(copies)]))
        copies[-1].start()

    for a in range(4):
        span = pl.ds(a * piece, piece)
        for k in range(4):
            wide[span, pl.ds(k * slab, slab)] = gf_ref[k, a].astype(F32)
        send(wide.at[span], gf_out.at[span])
        for source, dest in pieces[2 * a:2 * a + 2]:
            send(source, dest)
    for copy in copies:
        copy.wait()


def dense_body(inputs, grad_out, gates, expert_ids, slot_index, filter_taps, w_gate, w_up, w_down):
    tok, width = inputs.shape
    taps = filter_taps.shape[0]
    ff = w_gate.shape[2]
    top = gates.shape[1]
    length = 4 * tok
    size = taps + length
    slab = width // 4
    rows = slab + ff // 4
    vm = lambda *shape: pltpu.VMEM(shape, BF16)
    vf = lambda *shape: pltpu.VMEM(shape, F32)
    st = lambda *shape: jax.ShapeDtypeStruct(shape, BF16)
    near = pl.BlockSpec(memory_space=pltpu.VMEM)
    hbm = pl.BlockSpec(memory_space=pltpu.HBM)
    far_away = lambda array: pltpu.with_memory_space_constraint(array, pltpu.HBM)
    fh, fl, ih, il = transforms(size)
    outs = pl.pallas_call(
        dense_kernel,
        out_shape=(
            vm(4, tok, slab), vm(top, tok), vm(4, 4, taps // 4, slab), vm(slab, 2 * ff),
            vm(ff // 4, width),
        ),
        in_specs=[hbm] * 13,
        out_specs=(near,) * 5,
        scratch_shapes=[
            vm(top, tok), pltpu.VMEM((top, tok), jnp.int32), pltpu.VMEM((top, tok), jnp.int32),
            vm(size, length), vm(size, length), vm(length, size), vm(length, size), vm(taps, slab),
            vf(size, slab), vf(size, slab), vf(size, slab),
            vm(4, tok, slab), vm(4, tok, slab), vm(4, tok, slab), vm(4, tok, slab),
            vm(4, 4, tok, slab), vm(4, tok, width), vm(4, slab, 2 * ff), vm(4, ff // 4, width),
            vm(length, ff), vm(length, 2 * ff), vm(length, width),
            vm(4, 4, tok, slab), vm(4, 4, tok, slab), vm(2, 4, tok, slab), vm(4, tok, slab),
            vm(4, rows, width), vm(2, rows, width), vm(rows, width), vm(rows, width), vm(rows // PARTS, width),
            vm(4, taps // 4, slab), vm(4, taps // 4, slab),
            vf(4, 8, tok), vf(4, 8, tok), vf(4, 8, tok),
            pltpu.SemaphoreType.DMA((13,)),
            pltpu.SemaphoreType.DMA((56,)), pltpu.SemaphoreType.DMA((65,)),
        ],
        compiler_params=pltpu.CompilerParams(
            collective_id=0, has_side_effects=True, vmem_limit_bytes=48 * 1024 * 1024
        ),
    )(
        *[far_away(m) for m in (inputs, grad_out, gates.T, expert_ids.T, slot_index.T)],
        *[far_away(m) for m in (w_gate, w_up, w_down, filter_taps)],
        *[far_away(jnp.asarray(m)) for m in (fh[:, :length], fl[:, :length], ih[:length], il[:length])],
    )
    grads = pl.pallas_call(
        finish_kernel,
        out_shape=(
            st(tok, width), st(top, tok), jax.ShapeDtypeStruct((taps, width), F32),
            st(*w_gate.shape), st(*w_up.shape), st(*w_down.shape),
        ),
        in_specs=[near] * 5,
        out_specs=(hbm,) * 6,
        scratch_shapes=[vf(taps, width), pltpu.SemaphoreType.DMA((12,))],
        compiler_params=pltpu.CompilerParams(vmem_limit_bytes=8 * 1024 * 1024),
    )(*[pltpu.with_memory_space_constraint(array, pltpu.VMEM) for array in outs])
    return (grads[0], grads[1].T) + grads[2:]


def body_of(mesh):
    def body(*args):
        top_count = args[3].shape[1]
        tok, taps, dq = args[0].shape[0], args[5].shape[0], args[6].shape[1]
        small = mesh.shape["expert"] == top_count == 4 and mesh.shape["seq"] == 4
        small = small and mesh.shape["groups"] == 2
        if small and tok == 128 and taps == 2 * tok and dq == 2 * tok and 2 * args[6].shape[2] == args[0].shape[1]:
            return dense_body(*args)
        return routed_body(*args)

    return body


def solution(mesh):
    return jax.shard_map(
        body_of(mesh),
        mesh=mesh,
        in_specs=(
            P(("groups", "expert", "seq"), None),
            P(("groups", "expert", "seq"), None),
            P(("groups", "expert", "seq"), None),
            P(("groups", "expert", "seq"), None),
            P(("groups", "expert", "seq"), None),
            P(),
            P("expert", "seq", None),
            P("expert", "seq", None),
            P("expert", "seq", None),
        ),
        out_specs=(
            P(("groups", "expert", "seq"), None),
            P(("groups", "expert", "seq"), None),
            P("groups", None),
            P(("groups", "expert"), "seq", None),
            P(("groups", "expert"), "seq", None),
            P(("groups", "expert"), "seq", None),
        ),
        check_vma=False,
    )
```

```python
import functools

import jax
import jax.numpy as jnp
import numpy as np
from jax import lax
from jax.experimental import pallas as pl
from jax.experimental.pallas import tpu as pltpu
from jax.sharding import PartitionSpec as P

MESH = pl.DeviceIdType.MESH
F32 = jnp.float32
BF16 = jnp.bfloat16


def from_behind(block, axis, distance):
    devices = range(lax.axis_size(axis))
    route = [(i - distance, i) for i in devices if i - distance in devices]
    return lax.ppermute(block, axis, route)


def depthwise(signal, kernel):
    return lax.conv_general_dilated(
        signal[None],
        kernel[:, None, :],
        (1,),
        "VALID",
        dimension_numbers=("NWC", "WIO", "NWC"),
        feature_group_count=signal.shape[1],
        preferred_element_type=jnp.float32,
    )[0]


def contract(left, right, left_dim, right_dim):
    return lax.dot_general(
        left, right, (((left_dim,), (right_dim,)), ((), ())), preferred_element_type=jnp.float32
    )


def expert_pass(token_rows, scaled_rows, gate_mat, up_mat, down_mat):
    pre_gate = jnp.dot(token_rows, gate_mat, preferred_element_type=jnp.float32)
    pre_up = jnp.dot(token_rows, up_mat, preferred_element_type=jnp.float32)
    sigma = jax.nn.sigmoid(pre_gate)
    swish = pre_gate * sigma
    hidden = (swish * pre_up).astype(jnp.bfloat16)
    outputs = jnp.dot(hidden, down_mat, preferred_element_type=jnp.float32).astype(jnp.bfloat16)
    grad_hidden = contract(scaled_rows, down_mat, 1, 1)
    grad_pre_gate = (grad_hidden * pre_up * (sigma * (1.0 + pre_gate * (1.0 - sigma)))).astype(
        jnp.bfloat16
    )
    grad_pre_up = (grad_hidden * swish).astype(jnp.bfloat16)
    part_gate = contract(token_rows, grad_pre_gate, 0, 0)
    part_up = contract(token_rows, grad_pre_up, 0, 0)
    part_down = contract(hidden, scaled_rows, 0, 0)
    grad_rows = (
        contract(grad_pre_gate, gate_mat, 1, 1) + contract(grad_pre_up, up_mat, 1, 1)
    ).astype(jnp.bfloat16)
    return (grad_rows, outputs, (part_gate, part_up, part_down))


def routed_body(inputs, grad_out, gates, expert_ids, slot_index, filter_taps, w_gate, w_up, w_down):
    tok_count, width = inputs.shape
    taps = filter_taps.shape[0]
    top_count = expert_ids.shape[1]
    experts = lax.axis_size("expert")
    capacity = tok_count * top_count // experts
    reach = taps - 1
    shift_count = (reach + tok_count - 1) // tok_count
    earlier = [from_behind(inputs, "seq", shift_by) for shift_by in range(shift_count, 0, -1)]
    extended = jnp.concatenate(earlier + [inputs], axis=0)[-(tok_count + reach) :]
    filtered = depthwise(extended, filter_taps[::-1]).astype(jnp.bfloat16)
    kept = slot_index < capacity
    dest = jnp.where(kept, expert_ids * capacity + slot_index, experts * capacity).reshape(-1)

    def place(values):
        rest = values.shape[1:]
        empty = jnp.zeros((experts * capacity,) + rest, values.dtype)
        return empty.at[dest].set(values, mode="drop").reshape((experts, capacity) + rest)

    def fetch(buffer):
        rest = buffer.shape[2:]
        flat = buffer.reshape((experts * capacity,) + rest)
        return jnp.take(flat, dest, axis=0, mode="fill", fill_value=0).reshape(
            (tok_count, top_count) + rest
        )

    token_send = place(
        jnp.broadcast_to(filtered[:, None, :], (tok_count, top_count, width)).reshape(-1, width)
    )
    gate_full, up_full, down_full = (
        lax.all_gather(w_gate, "seq", axis=1, tiled=True),
        lax.all_gather(w_up, "seq", axis=1, tiled=True),
        lax.all_gather(w_down, "seq", axis=1, tiled=True),
    )
    gate_mat = gate_full[0]
    up_mat = up_full[0]
    down_mat = down_full[0]
    scaled = (
        gates.astype(jnp.float32)[:, :, None] * grad_out.astype(jnp.float32)[:, None, :]
    ).astype(jnp.bfloat16)
    token_recv, scaled_recv = (
        lax.all_to_all(token_send, "expert", split_axis=0, concat_axis=0, tiled=True),
        lax.all_to_all(
            place(scaled.reshape(-1, width)), "expert", split_axis=0, concat_axis=0, tiled=True
        ),
    )
    grad_rows, outputs, partials = expert_pass(
        token_recv.reshape(-1, width), scaled_recv.reshape(-1, width), gate_mat, up_mat, down_mat
    )
    grad_back, output_back = (
        lax.all_to_all(
            grad_rows.reshape(experts, capacity, width),
            "expert",
            split_axis=0,
            concat_axis=0,
            tiled=True,
        ),
        lax.all_to_all(
            outputs.reshape(experts, capacity, width),
            "expert",
            split_axis=0,
            concat_axis=0,
            tiled=True,
        ),
    )
    output_rows = fetch(output_back)
    grad_gates = jnp.sum(
        grad_out.astype(jnp.float32)[:, None, :] * output_rows.astype(jnp.float32), axis=2
    ).astype(jnp.bfloat16)
    summed_gate, summed_up, summed_down = (
        lax.psum_scatter(
            partials[0][None].astype(jnp.bfloat16), "seq", scatter_dimension=1, tiled=True
        ).astype(jnp.float32),
        lax.psum_scatter(
            partials[1][None].astype(jnp.bfloat16), "seq", scatter_dimension=1, tiled=True
        ).astype(jnp.float32),
        lax.psum_scatter(
            partials[2][None].astype(jnp.bfloat16), "seq", scatter_dimension=1, tiled=True
        ).astype(jnp.float32),
    )
    grad_filtered = jnp.sum(fetch(grad_back).astype(jnp.float32), axis=1).astype(jnp.bfloat16)
    later = [from_behind(grad_filtered, "seq", -shift_by) for shift_by in range(1, shift_count + 1)]
    grad_extended = jnp.concatenate([grad_filtered] + later, axis=0)[: tok_count + reach]
    grad_inputs = depthwise(grad_extended, filter_taps).astype(jnp.bfloat16)
    local_taps = depthwise(extended, grad_filtered)[::-1]
    grad_filter = lax.psum(local_taps, ("expert", "seq"))
    return (
        grad_inputs,
        grad_gates,
        grad_filter,
        summed_gate.astype(jnp.bfloat16),
        summed_up.astype(jnp.bfloat16),
        summed_down.astype(jnp.bfloat16),
    )


def transforms(size):
    freq = 2.0 * np.pi * (np.arange(size // 2) + 0.5) / size
    angle = freq[:, None] * np.arange(size)[None, :]
    forward = np.concatenate([np.cos(angle), np.sin(angle)], axis=0)
    inverse = forward.T * (2.0 / size)

    def pieces(matrix):
        high = matrix.astype(jnp.bfloat16)
        low = (matrix - high.astype(np.float64)).astype(jnp.bfloat16)
        return high, low

    return pieces(forward) + pieces(inverse)


def mm(left, right):
    return jnp.dot(left, right, preferred_element_type=F32)


def turned(left, right):
    return lax.dot_general(left, right, (((1,), (1,)), ((), ())), preferred_element_type=F32)


def across(left, right):
    return lax.dot_general(left, right, (((0,), (0,)), ((), ())), preferred_element_type=F32)


PIECES = 3
PARTS = 6


def dense_kernel(
    rows_ref, cot_ref, gates_ref, ids_ref, slots_ref, wg_ref, wu_ref, wd_ref, taps_ref,
    fh_ref, fl_ref, ih_ref, il_ref,
    gin_ref, gg_ref, gf_ref, dgu_ref, dd_ref,
    gates_in, ids_in, slots_in, fh, fl, ih, il, taps, x_spec, tap_spec, g_spec, seq_x, seq_f, seq_g, seq_in,
    tall, gall, wgu, wdn, hid, gpre, scaled, back, rall, pre_in, gfb,
    part, sib_in, pair, cross_in, relay_in, gfz, gfz_in,
    weigh, sums, sums_in,
    load_sem, send_sem, recv_sem,
):
    g = lax.axis_index("groups")
    z = lax.axis_index("expert")
    q = lax.axis_index("seq")
    tok, width = rows_ref.shape
    slab = width // 4
    ff = hid.shape[1]
    fq = ff // 4
    size = x_spec.shape[0]
    half = size // 2
    n_taps = taps.shape[0]
    piece = n_taps // 4
    length = 4 * tok
    sib = q + 1 - 2 * (q % 2)
    cross = (q + 2) % 4
    far = (sib + 2) % 4
    middle = jnp.logical_or(z == 1, z == 2)
    end = jnp.logical_or(z == 0, z == 3)

    across_end = {
        "expert": jnp.where(z < 2, 1 - z, 5 - z), "seq": cross
    }
    barrier = pltpu.get_barrier_semaphore()
    pl.semaphore_signal(barrier, inc=1, device_id=across_end, device_id_type=MESH)
    for s in range(1, 4):
        pl.semaphore_signal(barrier, inc=1, device_id={"expert": (z + s) % 4}, device_id_type=MESH)
        pl.semaphore_signal(barrier, inc=1, device_id={"seq": (q + s) % 4}, device_id_type=MESH)
    pl.semaphore_signal(barrier, inc=1, device_id={"groups": 1 - g}, device_id_type=MESH)

    def slab_at(k):
        return pl.ds(pl.multiple_of(k * slab, slab), slab)

    loads = [
        pltpu.make_async_copy(src, dst, load_sem.at[n])
        for n, (src, dst) in enumerate([
            (cot_ref, gall.at[z]),
            (gates_ref, gates_in), (ids_ref, ids_in), (slots_ref, slots_in),
            (rows_ref.at[:, slab_at(q)], seq_x.at[q]),
            (wg_ref.at[0], wgu.at[q, :, pl.ds(0, ff)]),
            (wu_ref.at[0], wgu.at[q, :, pl.ds(ff, ff)]),
            (wd_ref.at[0], wdn.at[q]),
            (taps_ref.at[:, slab_at(q)], taps),
            (fh_ref, fh), (fl_ref, fl), (ih_ref, ih), (il_ref, il),
        ])
    ]
    for load in loads:
        load.start()

    def link(n, src, dst, axis, peer, arrival):
        device = peer if isinstance(peer, dict) else {axis: peer}
        return pltpu.make_async_remote_copy(
            src_ref=src, dst_ref=dst, send_sem=send_sem.at[n],
            recv_sem=recv_sem.at[arrival], device_id=device, device_id_type=MESH,
        )

    def pick(a, b, c, d):
        return jnp.where(z == 0, a, jnp.where(z == 1, b, jnp.where(z == 2, c, d)))

    GATHER, WEIGH, SUM, BACK, SLAB, ROW, WEIGHT, SIB, RELAY, FIRST = 0, 24, 27, 30, 32, 35, 38, 50, 52, 54
    TAP, OUT, LAST, PART, HALF = 0, 8, 16, WEIGHT, WEIGHT + 6
    GATHERED, WEIGHED, SUMMED, BACKED, SLABBED, ROWED, WEIGHTED, SIBBED = 0, 16, 20, 24, 30, 33, 36, 48
    PARTED, RELAYED, LASTED = 50, 56, 57
    TAPPED, OUTED, HALVED = 0, 8, WEIGHTED

    def hop(base, view, origin, step, distance):
        return link(
            GATHER + 6 * base + (0 if step > 0 else 3) + distance, view(origin), view(origin),
            "expert", (z + 4 + step) % 4, GATHERED + 4 * base + origin,
        )

    def spread(base, view, distance, send=True):
        for step in (1, -1):
            origin = z - step * distance
            has_origin = origin >= 0 if step > 0 else origin <= 3
            has_next = z < 3 if step > 0 else z > 0

            @pl.when(has_origin)
            def _(origin=origin, has_next=has_next, step=step):
                if distance and send:
                    hop(base, view, origin, step, 0).wait_recv()

                if distance < 3:
                    @pl.when(has_next)
                    def _():
                        if send:
                            hop(base, view, origin, step, distance).start()
                        else:
                            hop(base, view, origin, step, distance).wait_send()

    def cot_ahead(distance, first, last=2):
        for part in range(first, last):
            spread(part, cot_of(part), distance)

    def rows_ahead(distance, first, last=2):
        for part in range(first, last):
            spread(2 + part, tok_of(part), distance)

    def cot_of(part):
        return lambda origin: gall.at[origin, pl.ds(part * (tok // 2), tok // 2)]

    def tok_of(part):
        return lambda origin: tall.at[:, origin, pl.ds(part * (tok // 2), tok // 2)]

    for load in loads[:4]:
        load.wait()
    ids = ids_in[...]
    kept = slots_in[...] < tok
    held = jnp.where(kept, gates_in[...].astype(F32), 0.0)
    eye = lax.broadcasted_iota(jnp.int32, (tok, tok), 0) == lax.broadcasted_iota(
        jnp.int32, (tok, tok), 1
    )

    def as_row(column):
        return jnp.sum(jnp.where(eye, column, 0.0), axis=0, keepdims=True)

    def as_column(row):
        return jnp.sum(jnp.where(eye, row, 0.0), axis=1, keepdims=True)

    weigh[z] = jnp.zeros(weigh.shape[1:], F32)
    for e in range(4):
        weigh[z, e:e + 1] = jnp.sum(jnp.where(ids == e, held, 0.0), axis=0, keepdims=True)

    with jax.named_scope("entry"):
        pl.semaphore_wait(barrier, 8)

    cot_ahead(0, 0)

    def to_others(send, arrive, source, dest):
        return [
            link(send + s, source((q + s) % 4), dest, "seq", (q + s) % 4, arrive + s)
            for s in (2, 1, 3)
        ]

    to_slabs = to_others(
        SLAB - 1, SLABBED - 1, lambda k: rows_ref.at[:, slab_at(k)], seq_x.at[q]
    )
    for copy in to_slabs:
        copy.start()
    for load in loads[4:9]:
        load.wait()

    step = (slab + fq) // (2 * PIECES)
    wide_pieces = slab // (2 * step)

    def piece_of(k, n, part):
        if n < wide_pieces:
            return wgu.at[k, pl.ds(pl.multiple_of((2 * n + part) * step, step), step)]
        at = pl.multiple_of((2 * (n - wide_pieces) + part) * step, step)
        return wdn.at[k, pl.ds(at, step)]

    def weight_copy(kind, source, n, part, axis, peer):
        at = kind * PIECES + n
        return link(
            WEIGHT + at, piece_of(source, n, part), piece_of(source, n, part), axis, peer,
            WEIGHTED + at,
        )

    w_cross = [weight_copy(0, q, n, g, "seq", cross) for n in range(PIECES)]
    w_group = [weight_copy(1, cross, n, g, "groups", 1 - g) for n in range(PIECES)]
    w_far = [
        [weight_copy(2 + h, cross, n, (g + h) % 2, "seq", sib) for n in range(PIECES)]
        for h in range(2)
    ]

    def pass_on(n):
        w_cross[n].wait_recv()
        w_group[n].start()
        w_far[0][n].start()

    def take(n):
        w_group[n].wait_recv()
        w_far[1][n].start()

    w_sib = [
        link(SIB, wgu.at[q], wgu.at[q], "seq", sib, SIBBED),
        link(SIB + 1, wdn.at[q], wdn.at[q], "seq", sib, SIBBED + 1),
    ]
    weighs = [
        link(WEIGH + s - 1, weigh.at[z], weigh.at[z], "expert", (z + s) % 4, WEIGHED + z)
        for s in range(1, 4)
    ]
    for copy in weighs + w_sib:
        copy.start()

    def forward(dest, count, values, exact=True):
        for at in range(0, size, slab):
            span = pl.ds(at, slab)
            dest[span] = mm(fh[span, :count], values)
            if exact:
                dest[span] += mm(fl[span, :count], values)

    def backward(count, spec, exact=True):
        high = spec.astype(BF16)
        if not exact:
            return mm(ih[:count], high)
        low = (spec - high.astype(F32)).astype(BF16)
        return mm(ih[:count], high) + mm(il[:count], high) + mm(ih[:count], low)

    def whole(ref):
        return ref[...].reshape(length, slab)

    for load in loads[9:]:
        load.wait()
    with jax.named_scope("tap spectrum"):
        forward(tap_spec, n_taps, taps[...])
    with jax.named_scope("x wait"):
        for copy in to_slabs:
            copy.wait_recv()
    w_cross[0].start()
    with jax.named_scope("cot 1 first"):
        cot_ahead(1, 0, 1)
    with jax.named_scope("filter"):
        forward(x_spec, length, whole(seq_x))
        xc, xs = x_spec[:half], x_spec[half:]
        hc, hs = tap_spec[:half], tap_spec[half:]
        prod = jnp.concatenate([xc * hc - xs * hs, xc * hs + xs * hc], axis=0)
        seq_f[...] = backward(length, prod).astype(BF16).reshape(4, tok, slab)
    to_rows = to_others(ROW - 1, ROWED - 1, lambda k: seq_f.at[k], tall.at[q, z])
    for copy in to_rows:
        copy.start()
    tall[q, z] = seq_f[q]
    with jax.named_scope("cot 1"):
        cot_ahead(1, 1)
    for copy in w_cross[1:]:
        copy.start()
    with jax.named_scope("rows wait"):
        for copy in to_rows:
            copy.wait_recv()
    rows_ahead(0, 0)
    with jax.named_scope("pass 0"):
        pass_on(0)
    with jax.named_scope("pass 1"):
        pass_on(1)

    @pl.when(middle)
    def _():
        with jax.named_scope("rows 1 first"):
            rows_ahead(1, 0, 1)

    with jax.named_scope("pass 2"):
        pass_on(2)
    with jax.named_scope("take 0"):
        take(0)

    @pl.when(middle)
    def _():
        with jax.named_scope("rows 1"):
            rows_ahead(1, 1)
        with jax.named_scope("cot 2"):
            cot_ahead(2, 0)

    with jax.named_scope("take 1"):
        take(1)
    with jax.named_scope("weigh wait"):
        for k in range(1, 4):
            peer = (z + k) % 4
            link(WEIGH, weigh.at[peer], weigh.at[peer], "expert", peer, WEIGHED + peer).wait_recv()

    @pl.when(middle)
    def _():
        with jax.named_scope("rows 2 middle first"):
            rows_ahead(2, 0, 1)

    with jax.named_scope("take 2"):
        take(2)
    with jax.named_scope("weights wait"):
        for copy in w_sib + w_far[0] + w_far[1]:
            copy.wait_recv()

    origins = [z, pick(2, 3, 0, 1), pick(1, 0, 3, 2), pick(3, 2, 1, 0)]
    sublanes = lax.broadcasted_iota(jnp.int32, weigh.shape[1:], 0)
    gate_sums = [
        link(SUM + s - 1, sums.at[s], sums_in.at[z], "expert", origins[s], SUMMED + z)
        for s in range(1, 4)
    ]
    backs = [
        link(BACK + s - 2, back.at[s], rall.at[z], "expert", origins[s], BACKED + z)
        for s in range(2, 4)
    ]
    to_pre = link(FIRST, back.at[1], pre_in.at[0], "expert", 3 - z, BACKED + 4)
    to_next = link(FIRST, back.at[1], pre_in.at[1], "expert", origins[2], BACKED + 5)

    def block(s):
        origin = origins[s]
        span = pl.ds(pl.multiple_of(origin * tok, tok), tok)
        pre = mm(tall[0, origin], wgu[0])
        for k in range(1, 4):
            pre += mm(tall[k, origin], wgu[k])
        cot = gall[origin]
        weight = as_column(
            jnp.sum(jnp.where(sublanes == z, weigh[origin], 0.0), axis=0, keepdims=True)
        )
        raw = turned(cot, wdn[...].reshape(ff, width))
        gate, up = pre[:, :ff], pre[:, ff:]
        sigma = jax.nn.sigmoid(gate)
        swish = gate * sigma
        hidden = (swish * up).astype(BF16)
        gg = jnp.sum(hidden.astype(F32) * raw, axis=1, keepdims=True)
        grad_hidden = raw * weight
        grad_gate = grad_hidden * up * (sigma * (1.0 + gate * (1.0 - sigma)))
        gp = jnp.concatenate([grad_gate.astype(BF16), (grad_hidden * swish).astype(BF16)], axis=1)
        hid[span] = hidden
        gpre[span] = gp
        scaled[span] = (weight * cot.astype(F32)).astype(BF16)
        target, at = (back, s) if s else (rall, z)
        for k in range(4):
            target[at, k] = turned(gp, wgu[k]).astype(BF16)
        (sums if s else sums_in)[at] = jnp.broadcast_to(as_row(gg), sums.shape[1:])

    @pl.when(middle)
    def _():
        with jax.named_scope("block 0"):
            block(0)

    @pl.when(middle)
    def _():
        with jax.named_scope("rows 2 middle"):
            rows_ahead(2, 1)

    @pl.when(end)
    def _():
        with jax.named_scope("rows 2 end"):
            cot_ahead(2, 0)
            rows_ahead(2, 0)

    with jax.named_scope("block 1"):
        block(1)
    gate_sums[0].start()

    @pl.when(middle)
    def _():
        to_pre.start()

    @pl.when(end)
    def _():
        to_next.start()
        with jax.named_scope("block 0"):
            block(0)
        with jax.named_scope("rows 1 end"):
            rows_ahead(1, 0)

    with jax.named_scope("block 2"):
        block(2)
    gate_sums[1].start()

    @pl.when(end)
    def _():
        backs[0].start()
        with jax.named_scope("rows 3"):
            cot_ahead(3, 0)
            rows_ahead(3, 0)

    with jax.named_scope("block 3"):
        block(3)
    gate_sums[2].start()

    @pl.when(end)
    def _():
        backs[1].start()

    def partial_low(slot, dest):
        thin = pl.ds(pl.multiple_of(dest * fq, fq), fq)
        part[slot, slab:] = across(hid[:, thin], scaled[...]).astype(BF16)

    def partial_top(slot, dest):
        top = across(tall[dest].reshape(length, slab), gpre[...])
        part[slot, :slab] = top.astype(BF16)

    rows = slab + fq
    share = rows // PARTS
    low, top = pl.ds(slab, fq), pl.ds(0, slab)
    to_sib = [
        link(HALF, part.at[0, low], sib_in.at[0, low], "seq", sib, HALVED),
        link(HALF + 1, part.at[0, top], sib_in.at[0, top], "seq", sib, HALVED + 1),
        link(HALF + 2, part.at[1], sib_in.at[1], "seq", sib, HALVED + 2),
    ]
    to_cross = [
        link(
            PART + n, pair.at[pl.ds(n * share, share)], cross_in.at[pl.ds(n * share, share)],
            "seq", cross, PARTED + n,
        )
        for n in [*range(slab // share, PARTS), *range(slab // share)]
    ]
    near_end = pick(1, 0, 3, 2)
    last = pl.ds((slab // share - 1) * share, share)
    around = link(FIRST + 1, pair.at[last], relay_in, "", across_end, RELAYED)
    passed = link(
        RELAY, relay_in, cross_in.at[last], "expert", near_end, PARTED + slab // share - 1
    )

    for copy in w_cross + w_group + w_far[0] + w_far[1]:
        copy.wait_send()
    with jax.named_scope("partial 0"):
        partial_low(0, far)
        to_sib[0].start()
        partial_top(0, far)
        to_sib[1].start()
    with jax.named_scope("partial 2"):
        partial_low(2, cross)
        to_sib[0].wait_recv()
        pair[low] = (part[2, low].astype(F32) + sib_in[0, low].astype(F32)).astype(BF16)
        for copy in to_cross[:2]:
            copy.start()
        partial_top(2, cross)
        to_sib[1].wait_recv()
        pair[top] = (part[2, top].astype(F32) + sib_in[0, top].astype(F32)).astype(BF16)
        to_cross[2].start()

    @pl.when(end)
    def _():
        around.start()

    @pl.when(middle)
    def _():
        for copy in to_cross[3:5]:
            copy.start()

    with jax.named_scope("partial 1"):
        partial_low(1, sib)
        partial_top(1, sib)
    to_sib[2].start()
    with jax.named_scope("partial 3"):
        partial_low(3, q)
        partial_top(3, q)

    @pl.when(middle)
    def _():
        with jax.named_scope("pre wait"):
            to_pre.wait_recv()
        back[2] = (back[2].astype(F32) + pre_in[0].astype(F32)).astype(BF16)
        backs[0].start()
        with jax.named_scope("next wait"):
            to_next.wait_recv()
        back[3] = (back[3].astype(F32) + pre_in[1].astype(F32)).astype(BF16)
        backs[1].start()

    for d in range(3):
        for h in range(2):
            spread(h, cot_of(h), d, False)
            spread(2 + h, tok_of(h), d, False)

    with jax.named_scope("back wait"):
        for s in (1, 3):
            peer = (z + s) % 4
            link(BACK, back.at[1], rall.at[peer], "expert", peer, BACKED + peer).wait_recv()

    total = rall[z].astype(F32)
    for s in (1, 3):
        total += rall[(z + s) % 4].astype(F32)
    gfb[...] = total.astype(BF16)
    seq_g[q] = gfb[q]
    for copy in to_slabs:
        copy.wait_send()
    g_slabs = to_others(SLAB - 1, SLABBED - 1, lambda k: gfb.at[k], seq_g.at[q])
    for copy in g_slabs:
        copy.start()

    @pl.when(middle)
    def _():
        with jax.named_scope("part 0"):
            around.wait_recv()
            passed.start()

    for s in range(1, 4):
        peer = (z + s) % 4
        link(SUM, sums.at[s], sums_in.at[peer], "expert", peer, SUMMED + peer).wait_recv()
    gate_grads = jnp.zeros(ids.shape, F32)
    for s in range(4):
        gate_grads += jnp.where(ids == s, sums_in[s, 0:1], 0.0)
    gg_ref[...] = jnp.where(kept, gate_grads, 0.0).astype(BF16)

    with jax.named_scope("grad wait"):
        for copy in g_slabs:
            copy.wait_recv()

    @pl.when(middle)
    def _():
        to_cross[5].start()

    @pl.when(end)
    def _():
        to_cross[3].start()

    with jax.named_scope("tap grad"):
        forward(g_spec, length, whole(seq_g), False)
        gc, gs = g_spec[:half], g_spec[half:]
        xc, xs = x_spec[:half], x_spec[half:]
        prod = jnp.concatenate([gc * xc + gs * xs, gs * xc - gc * xs], axis=0)
        gfz[...] = backward(n_taps, prod, False).astype(BF16).reshape(4, piece, slab)
    near = [z, pick(1, 2, 1, 2), pick(2, 0, 3, 1), pick(3, 3, 0, 0)]
    fold = piece // 2

    def fold_of(ref, h, *at):
        return ref.at[*at, pl.ds(h * fold, fold)]

    tap_in = [
        link(
            TAP + 4 * h + s, fold_of(gfz, h, near[s]), fold_of(gfz_in, h, z), "expert", near[s],
            TAPPED + 4 * h + z,
        )
        for h in range(2) for s in (3, 2, 1)
    ]
    tap_out = [
        [
            link(
                OUT + 4 * h + s, fold_of(gf_ref, h, q, z), fold_of(gf_ref, h, q, z), "expert", near[s],
                OUTED + 4 * h + z,
            )
            for s in (3, 2, 1)
        ]
        for h in range(2)
    ]
    tap_cross = [
        [
            link(
                LAST + 4 * h + s, fold_of(gf_ref, h, q, near[s]), fold_of(gf_ref, h, q, near[s]), "seq",
                cross, LASTED + 4 * h + near[s],
            )
            for s in range(4)
        ]
        for h in range(2)
    ]
    for copy in tap_in:
        copy.start()

    with jax.named_scope("input grad"):
        gc, gs = g_spec[:half], g_spec[half:]
        hc, hs = tap_spec[:half], tap_spec[half:]
        prod = jnp.concatenate([gc * hc + gs * hs, gs * hc - gc * hs], axis=0)
        seq_in[...] = backward(length, prod).astype(BF16).reshape(4, tok, slab)
    for copy in to_rows:
        copy.wait_send()
    gin_out = to_others(ROW - 1, ROWED - 1, lambda k: seq_in.at[k], gin_ref.at[q])
    for copy in gin_out:
        copy.start()
    gin_ref[q] = seq_in[q]

    @pl.when(end)
    def _():
        to_cross[4].start()

    def tap_from(base, peer):
        link(TAP, fold_of(gfz, 0, 0), fold_of(gfz_in, 0, 0), "expert", peer, base + peer).wait_recv()

    with jax.named_scope("taps in"):
        for h in range(2):
            rows_h = pl.ds(h * fold, fold)
            mine = gfz[z, rows_h].astype(F32)
            for s in range(1, 4):
                tap_from(TAPPED + 4 * h, near[s])
                mine += gfz_in[near[s], rows_h].astype(F32)
            gf_ref[q, z, rows_h] = mine.astype(BF16)
            for copy in tap_out[h] + tap_cross[h][:1]:
                copy.start()

    with jax.named_scope("taps out"):
        for h in range(2):
            for s in range(1, 4):
                tap_from(OUTED + 4 * h, near[s])
                tap_cross[h][s].start()

    gf_sib = [
        link(SIB, gf_ref.at[q], gf_ref.at[q], "seq", sib, SIBBED),
        link(SIB + 1, gf_ref.at[cross], gf_ref.at[cross], "seq", sib, SIBBED + 1),
    ]
    for copy in w_sib:
        copy.wait_send()
    gf_sib[0].start()
    to_sib[2].wait_recv()
    with jax.named_scope("pair wait"):
        for copy in to_cross:
            copy.wait_recv()
    with jax.named_scope("weight sums"):
        dgu_ref[...] = (
            part[3, :slab].astype(F32) + sib_in[1, :slab].astype(F32) + cross_in[:slab].astype(F32)
        ).astype(BF16)
        dd_ref[...] = (
            part[3, slab:].astype(F32) + sib_in[1, slab:].astype(F32) + cross_in[slab:].astype(F32)
        ).astype(BF16)

    with jax.named_scope("taps cross"):
        for copy in tap_cross[0] + tap_cross[1]:
            copy.wait_recv()

    gf_sib[1].start()
    with jax.named_scope("last waits"):
        for copy in gin_out:
            copy.wait_recv()
        for copy in gf_sib:
            copy.wait_recv()
        @pl.when(middle)
        def _():
            for copy in to_cross[5:] + [passed]:
                copy.wait_send()

        @pl.when(end)
        def _():
            around.wait_send()

        for copy in (
            weighs + gate_sums + [to_pre] + backs + to_sib
            + to_cross[:5] + tap_in + tap_out[0] + tap_out[1] + tap_cross[0] + tap_cross[1] + g_slabs + gin_out + gf_sib
        ):
            copy.wait_send()


def finish_kernel(
    gin_ref, gg_ref, gf_ref, dgu_ref, dd_ref,
    gin_out, gg_out, gf_out, dg_out, du_out, dd_out, wide, sem,
):
    slab = gin_ref.shape[2]
    ff = dg_out.shape[2]
    pieces = [
        (gin_ref.at[k], gin_out.at[:, pl.ds(k * slab, slab)]) for k in range(4)
    ] + [
        (dgu_ref.at[:, pl.ds(0, ff)], dg_out.at[0]), (dgu_ref.at[:, pl.ds(ff, ff)], du_out.at[0]),
        (dd_ref, dd_out.at[0]), (gg_ref, gg_out),
    ]
    piece = gf_ref.shape[2]
    copies = []

    def send(source, dest):
        copies.append(pltpu.make_async_copy(source, dest, sem.at[len(copies)]))
        copies[-1].start()

    for a in range(4):
        span = pl.ds(a * piece, piece)
        for k in range(4):
            wide[span, pl.ds(k * slab, slab)] = gf_ref[k, a].astype(F32)
        send(wide.at[span], gf_out.at[span])
        for source, dest in pieces[2 * a:2 * a + 2]:
            send(source, dest)
    for copy in copies:
        copy.wait()


def dense_body(inputs, grad_out, gates, expert_ids, slot_index, filter_taps, w_gate, w_up, w_down):
    tok, width = inputs.shape
    taps = filter_taps.shape[0]
    ff = w_gate.shape[2]
    top = gates.shape[1]
    length = 4 * tok
    size = taps + length
    slab = width // 4
    rows = slab + ff // 4
    vm = lambda *shape: pltpu.VMEM(shape, BF16)
    vf = lambda *shape: pltpu.VMEM(shape, F32)
    st = lambda *shape: jax.ShapeDtypeStruct(shape, BF16)
    near = pl.BlockSpec(memory_space=pltpu.VMEM)
    hbm = pl.BlockSpec(memory_space=pltpu.HBM)
    far_away = lambda array: pltpu.with_memory_space_constraint(array, pltpu.HBM)
    fh, fl, ih, il = transforms(size)
    outs = pl.pallas_call(
        dense_kernel,
        out_shape=(
            vm(4, tok, slab), vm(top, tok), vm(4, 4, taps // 4, slab), vm(slab, 2 * ff),
            vm(ff // 4, width),
        ),
        in_specs=[hbm] * 13,
        out_specs=(near,) * 5,
        scratch_shapes=[
            vm(top, tok), pltpu.VMEM((top, tok), jnp.int32), pltpu.VMEM((top, tok), jnp.int32),
            vm(size, length), vm(size, length), vm(length, size), vm(length, size), vm(taps, slab),
            vf(size, slab), vf(size, slab), vf(size, slab),
            vm(4, tok, slab), vm(4, tok, slab), vm(4, tok, slab), vm(4, tok, slab),
            vm(4, 4, tok, slab), vm(4, tok, width), vm(4, slab, 2 * ff), vm(4, ff // 4, width),
            vm(length, ff), vm(length, 2 * ff), vm(length, width),
            vm(4, 4, tok, slab), vm(4, 4, tok, slab), vm(2, 4, tok, slab), vm(4, tok, slab),
            vm(4, rows, width), vm(2, rows, width), vm(rows, width), vm(rows, width), vm(rows // PARTS, width),
            vm(4, taps // 4, slab), vm(4, taps // 4, slab),
            vf(4, 8, tok), vf(4, 8, tok), vf(4, 8, tok),
            pltpu.SemaphoreType.DMA((13,)),
            pltpu.SemaphoreType.DMA((56,)), pltpu.SemaphoreType.DMA((65,)),
        ],
        compiler_params=pltpu.CompilerParams(
            collective_id=0, has_side_effects=True, vmem_limit_bytes=48 * 1024 * 1024
        ),
    )(
        *[far_away(m) for m in (inputs, grad_out, gates.T, expert_ids.T, slot_index.T)],
        *[far_away(m) for m in (w_gate, w_up, w_down, filter_taps)],
        *[far_away(jnp.asarray(m)) for m in (fh[:, :length], fl[:, :length], ih[:length], il[:length])],
    )
    grads = pl.pallas_call(
        finish_kernel,
        out_shape=(
            st(tok, width), st(top, tok), jax.ShapeDtypeStruct((taps, width), F32),
            st(*w_gate.shape), st(*w_up.shape), st(*w_down.shape),
        ),
        in_specs=[near] * 5,
        out_specs=(hbm,) * 6,
        scratch_shapes=[vf(taps, width), pltpu.SemaphoreType.DMA((12,))],
        compiler_params=pltpu.CompilerParams(vmem_limit_bytes=8 * 1024 * 1024),
    )(*[pltpu.with_memory_space_constraint(array, pltpu.VMEM) for array in outs])
    return (grads[0], grads[1].T) + grads[2:]


def body_of(mesh):
    def body(*args):
        top_count = args[3].shape[1]
        tok, taps, dq = args[0].shape[0], args[5].shape[0], args[6].shape[1]
        small = mesh.shape["expert"] == top_count == 4 and mesh.shape["seq"] == 4
        small = small and mesh.shape["groups"] == 2
        if small and tok == 128 and taps == 2 * tok and dq == 2 * tok and 2 * args[6].shape[2] == args[0].shape[1]:
            return dense_body(*args)
        return routed_body(*args)

    return body


def solution(mesh):
    return jax.shard_map(
        body_of(mesh),
        mesh=mesh,
        in_specs=(
            P(("groups", "expert", "seq"), None),
            P(("groups", "expert", "seq"), None),
            P(("groups", "expert", "seq"), None),
            P(("groups", "expert", "seq"), None),
            P(("groups", "expert", "seq"), None),
            P(),
            P("expert", "seq", None),
            P("expert", "seq", None),
            P("expert", "seq", None),
        ),
        out_specs=(
            P(("groups", "expert", "seq"), None),
            P(("groups", "expert", "seq"), None),
            P("groups", None),
            P(("groups", "expert"), "seq", None),
            P(("groups", "expert"), "seq", None),
            P(("groups", "expert"), "seq", None),
        ),
        check_vma=False,
    )
```

```python
import functools

import jax
import jax.numpy as jnp
import numpy as np
from jax import lax
from jax.experimental import pallas as pl
from jax.experimental.pallas import tpu as pltpu
from jax.sharding import PartitionSpec as P

MESH = pl.DeviceIdType.MESH
F32 = jnp.float32
BF16 = jnp.bfloat16


def from_behind(block, axis, distance):
    devices = range(lax.axis_size(axis))
    route = [(i - distance, i) for i in devices if i - distance in devices]
    return lax.ppermute(block, axis, route)


def depthwise(signal, kernel):
    return lax.conv_general_dilated(
        signal[None],
        kernel[:, None, :],
        (1,),
        "VALID",
        dimension_numbers=("NWC", "WIO", "NWC"),
        feature_group_count=signal.shape[1],
        preferred_element_type=jnp.float32,
    )[0]


def contract(left, right, left_dim, right_dim):
    return lax.dot_general(
        left, right, (((left_dim,), (right_dim,)), ((), ())), preferred_element_type=jnp.float32
    )


def expert_pass(token_rows, scaled_rows, gate_mat, up_mat, down_mat):
    pre_gate = jnp.dot(token_rows, gate_mat, preferred_element_type=jnp.float32)
    pre_up = jnp.dot(token_rows, up_mat, preferred_element_type=jnp.float32)
    sigma = jax.nn.sigmoid(pre_gate)
    swish = pre_gate * sigma
    hidden = (swish * pre_up).astype(jnp.bfloat16)
    outputs = jnp.dot(hidden, down_mat, preferred_element_type=jnp.float32).astype(jnp.bfloat16)
    grad_hidden = contract(scaled_rows, down_mat, 1, 1)
    grad_pre_gate = (grad_hidden * pre_up * (sigma * (1.0 + pre_gate * (1.0 - sigma)))).astype(
        jnp.bfloat16
    )
    grad_pre_up = (grad_hidden * swish).astype(jnp.bfloat16)
    part_gate = contract(token_rows, grad_pre_gate, 0, 0)
    part_up = contract(token_rows, grad_pre_up, 0, 0)
    part_down = contract(hidden, scaled_rows, 0, 0)
    grad_rows = (
        contract(grad_pre_gate, gate_mat, 1, 1) + contract(grad_pre_up, up_mat, 1, 1)
    ).astype(jnp.bfloat16)
    return (grad_rows, outputs, (part_gate, part_up, part_down))


def routed_body(inputs, grad_out, gates, expert_ids, slot_index, filter_taps, w_gate, w_up, w_down):
    tok_count, width = inputs.shape
    taps = filter_taps.shape[0]
    top_count = expert_ids.shape[1]
    experts = lax.axis_size("expert")
    capacity = tok_count * top_count // experts
    reach = taps - 1
    shift_count = (reach + tok_count - 1) // tok_count
    earlier = [from_behind(inputs, "seq", shift_by) for shift_by in range(shift_count, 0, -1)]
    extended = jnp.concatenate(earlier + [inputs], axis=0)[-(tok_count + reach) :]
    filtered = depthwise(extended, filter_taps[::-1]).astype(jnp.bfloat16)
    kept = slot_index < capacity
    dest = jnp.where(kept, expert_ids * capacity + slot_index, experts * capacity).reshape(-1)

    def place(values):
        rest = values.shape[1:]
        empty = jnp.zeros((experts * capacity,) + rest, values.dtype)
        return empty.at[dest].set(values, mode="drop").reshape((experts, capacity) + rest)

    def fetch(buffer):
        rest = buffer.shape[2:]
        flat = buffer.reshape((experts * capacity,) + rest)
        return jnp.take(flat, dest, axis=0, mode="fill", fill_value=0).reshape(
            (tok_count, top_count) + rest
        )

    token_send = place(
        jnp.broadcast_to(filtered[:, None, :], (tok_count, top_count, width)).reshape(-1, width)
    )
    gate_full, up_full, down_full = (
        lax.all_gather(w_gate, "seq", axis=1, tiled=True),
        lax.all_gather(w_up, "seq", axis=1, tiled=True),
        lax.all_gather(w_down, "seq", axis=1, tiled=True),
    )
    gate_mat = gate_full[0]
    up_mat = up_full[0]
    down_mat = down_full[0]
    scaled = (
        gates.astype(jnp.float32)[:, :, None] * grad_out.astype(jnp.float32)[:, None, :]
    ).astype(jnp.bfloat16)
    token_recv, scaled_recv = (
        lax.all_to_all(token_send, "expert", split_axis=0, concat_axis=0, tiled=True),
        lax.all_to_all(
            place(scaled.reshape(-1, width)), "expert", split_axis=0, concat_axis=0, tiled=True
        ),
    )
    grad_rows, outputs, partials = expert_pass(
        token_recv.reshape(-1, width), scaled_recv.reshape(-1, width), gate_mat, up_mat, down_mat
    )
    grad_back, output_back = (
        lax.all_to_all(
            grad_rows.reshape(experts, capacity, width),
            "expert",
            split_axis=0,
            concat_axis=0,
            tiled=True,
        ),
        lax.all_to_all(
            outputs.reshape(experts, capacity, width),
            "expert",
            split_axis=0,
            concat_axis=0,
            tiled=True,
        ),
    )
    output_rows = fetch(output_back)
    grad_gates = jnp.sum(
        grad_out.astype(jnp.float32)[:, None, :] * output_rows.astype(jnp.float32), axis=2
    ).astype(jnp.bfloat16)
    summed_gate, summed_up, summed_down = (
        lax.psum_scatter(
            partials[0][None].astype(jnp.bfloat16), "seq", scatter_dimension=1, tiled=True
        ).astype(jnp.float32),
        lax.psum_scatter(
            partials[1][None].astype(jnp.bfloat16), "seq", scatter_dimension=1, tiled=True
        ).astype(jnp.float32),
        lax.psum_scatter(
            partials[2][None].astype(jnp.bfloat16), "seq", scatter_dimension=1, tiled=True
        ).astype(jnp.float32),
    )
    grad_filtered = jnp.sum(fetch(grad_back).astype(jnp.float32), axis=1).astype(jnp.bfloat16)
    later = [from_behind(grad_filtered, "seq", -shift_by) for shift_by in range(1, shift_count + 1)]
    grad_extended = jnp.concatenate([grad_filtered] + later, axis=0)[: tok_count + reach]
    grad_inputs = depthwise(grad_extended, filter_taps).astype(jnp.bfloat16)
    local_taps = depthwise(extended, grad_filtered)[::-1]
    grad_filter = lax.psum(local_taps, ("expert", "seq"))
    return (
        grad_inputs,
        grad_gates,
        grad_filter,
        summed_gate.astype(jnp.bfloat16),
        summed_up.astype(jnp.bfloat16),
        summed_down.astype(jnp.bfloat16),
    )


def transforms(size):
    freq = 2.0 * np.pi * (np.arange(size // 2) + 0.5) / size
    angle = freq[:, None] * np.arange(size)[None, :]
    forward = np.concatenate([np.cos(angle), np.sin(angle)], axis=0)
    inverse = forward.T * (2.0 / size)

    def pieces(matrix):
        high = matrix.astype(jnp.bfloat16)
        low = (matrix - high.astype(np.float64)).astype(jnp.bfloat16)
        return high, low

    return pieces(forward) + pieces(inverse)


def mm(left, right):
    return jnp.dot(left, right, preferred_element_type=F32)


def turned(left, right):
    return lax.dot_general(left, right, (((1,), (1,)), ((), ())), preferred_element_type=F32)


def across(left, right):
    return lax.dot_general(left, right, (((0,), (0,)), ((), ())), preferred_element_type=F32)


PIECES = 3
PARTS = 6


def dense_kernel(
    rows_ref, cot_ref, gates_ref, ids_ref, slots_ref, wg_ref, wu_ref, wd_ref, taps_ref,
    fh_ref, fl_ref, ih_ref, il_ref,
    gin_ref, gg_ref, gf_ref, dgu_ref, dd_ref,
    gates_in, ids_in, slots_in, fh, fl, ih, il, taps, x_spec, tap_spec, g_spec, seq_x, seq_f, seq_g, seq_in,
    tall, gall, wgu, wdn, hid, gpre, scaled, back, rall, pre_in, gfb,
    part, sib_in, pair, cross_in, relay_in, gfz, gfz_in,
    weigh, sums, sums_in,
    send_sem, recv_sem,
):
    g = lax.axis_index("groups")
    z = lax.axis_index("expert")
    q = lax.axis_index("seq")
    tok, width = rows_ref.shape
    slab = width // 4
    ff = hid.shape[1]
    fq = ff // 4
    size = x_spec.shape[0]
    half = size // 2
    n_taps = taps.shape[0]
    piece = n_taps // 4
    length = 4 * tok
    sib = q + 1 - 2 * (q % 2)
    cross = (q + 2) % 4
    far = (sib + 2) % 4
    middle = jnp.logical_or(z == 1, z == 2)
    end = jnp.logical_or(z == 0, z == 3)

    across_end = {
        "expert": jnp.where(z < 2, 1 - z, 5 - z), "seq": cross
    }
    barrier = pltpu.get_barrier_semaphore()
    pl.semaphore_signal(barrier, inc=1, device_id=across_end, device_id_type=MESH)
    for s in range(1, 4):
        pl.semaphore_signal(barrier, inc=1, device_id={"expert": (z + s) % 4}, device_id_type=MESH)
        pl.semaphore_signal(barrier, inc=1, device_id={"seq": (q + s) % 4}, device_id_type=MESH)
    pl.semaphore_signal(barrier, inc=1, device_id={"groups": 1 - g}, device_id_type=MESH)

    def slab_at(k):
        return pl.ds(pl.multiple_of(k * slab, slab), slab)

    loads = [
        pltpu.make_async_copy(src, dst, send_sem.at[38 + n])
        for n, (src, dst) in enumerate([
            (cot_ref, gall.at[z]),
            (gates_ref, gates_in), (ids_ref, ids_in), (slots_ref, slots_in),
            (rows_ref.at[:, slab_at(q)], seq_x.at[q]),
            (wg_ref.at[0], wgu.at[q, :, pl.ds(0, ff)]),
            (wu_ref.at[0], wgu.at[q, :, pl.ds(ff, ff)]),
            (wd_ref.at[0], wdn.at[q]),
            (taps_ref.at[:, slab_at(q)], taps),
            (fh_ref, fh), (fl_ref, fl), (ih_ref, ih), (il_ref, il),
        ])
    ]
    for load in loads:
        load.start()

    def link(n, src, dst, axis, peer, arrival):
        device = peer if isinstance(peer, dict) else {axis: peer}
        return pltpu.make_async_remote_copy(
            src_ref=src, dst_ref=dst, send_sem=send_sem.at[n],
            recv_sem=recv_sem.at[arrival], device_id=device, device_id_type=MESH,
        )

    def pick(a, b, c, d):
        return jnp.where(z == 0, a, jnp.where(z == 1, b, jnp.where(z == 2, c, d)))

    GATHER, WEIGH, SUM, BACK, SLAB, ROW, WEIGHT, SIB, RELAY, FIRST = 0, 24, 27, 30, 32, 35, 38, 51, 53, 54
    TAP, OUT, LAST, PART, HALF = 0, 8, 16, WEIGHT, WEIGHT + 6
    GATHERED, WEIGHED, SUMMED, BACKED, SLABBED, ROWED, WEIGHTED, SIBBED = 0, 16, 20, 24, 30, 33, 36, 48
    PARTED, RELAYED, LASTED = 50, 56, 57
    TAPPED, OUTED, HALVED = 0, 8, WEIGHTED

    def hop(base, view, origin, step, distance):
        return link(
            GATHER + 6 * base + (0 if step > 0 else 3) + distance, view(origin), view(origin),
            "expert", (z + 4 + step) % 4, GATHERED + 4 * base + origin,
        )

    def spread(base, view, distance, send=True):
        for step in (1, -1):
            origin = z - step * distance
            has_origin = origin >= 0 if step > 0 else origin <= 3
            has_next = z < 3 if step > 0 else z > 0

            @pl.when(has_origin)
            def _(origin=origin, has_next=has_next, step=step):
                if distance and send:
                    hop(base, view, origin, step, 0).wait_recv()

                if distance < 3:
                    @pl.when(has_next)
                    def _():
                        if send:
                            hop(base, view, origin, step, distance).start()
                        else:
                            hop(base, view, origin, step, distance).wait_send()

    def cot_ahead(distance, first, last=2):
        for part in range(first, last):
            spread(part, cot_of(part), distance)

    def rows_ahead(distance, first, last=2):
        for part in range(first, last):
            spread(2 + part, tok_of(part), distance)

    def cot_of(part):
        return lambda origin: gall.at[origin, pl.ds(part * (tok // 2), tok // 2)]

    def tok_of(part):
        return lambda origin: tall.at[:, origin, pl.ds(part * (tok // 2), tok // 2)]

    for load in loads[:4]:
        load.wait()
    ids = ids_in[...]
    kept = slots_in[...] < tok
    held = jnp.where(kept, gates_in[...].astype(F32), 0.0)
    eye = lax.broadcasted_iota(jnp.int32, (tok, tok), 0) == lax.broadcasted_iota(
        jnp.int32, (tok, tok), 1
    )

    def as_row(column):
        return jnp.sum(jnp.where(eye, column, 0.0), axis=0, keepdims=True)

    def as_column(row):
        return jnp.sum(jnp.where(eye, row, 0.0), axis=1, keepdims=True)

    weigh[z] = jnp.zeros(weigh.shape[1:], F32)
    for e in range(4):
        weigh[z, e:e + 1] = jnp.sum(jnp.where(ids == e, held, 0.0), axis=0, keepdims=True)

    with jax.named_scope("entry"):
        pl.semaphore_wait(barrier, 8)

    cot_ahead(0, 0)

    def to_others(send, arrive, source, dest):
        return [
            link(send + s, source((q + s) % 4), dest, "seq", (q + s) % 4, arrive + s)
            for s in (2, 1, 3)
        ]

    to_slabs = to_others(
        SLAB - 1, SLABBED - 1, lambda k: rows_ref.at[:, slab_at(k)], seq_x.at[q]
    )
    for copy in to_slabs:
        copy.start()
    for load in loads[4:9]:
        load.wait()

    step = (slab + fq) // (2 * PIECES)
    wide_pieces = slab // (2 * step)

    def piece_of(k, n, part):
        if n < wide_pieces:
            return wgu.at[k, pl.ds(pl.multiple_of((2 * n + part) * step, step), step)]
        at = pl.multiple_of((2 * (n - wide_pieces) + part) * step, step)
        return wdn.at[k, pl.ds(at, step)]

    def weight_copy(kind, source, n, part, axis, peer):
        at = kind * PIECES + n
        return link(
            WEIGHT + at, piece_of(source, n, part), piece_of(source, n, part), axis, peer,
            WEIGHTED + at,
        )

    w_cross = [weight_copy(0, q, n, g, "seq", cross) for n in range(PIECES)]
    w_group = [weight_copy(1, cross, n, g, "groups", 1 - g) for n in range(PIECES)]
    w_far = [
        [weight_copy(2 + h, cross, n, (g + h) % 2, "seq", sib) for n in range(PIECES)]
        for h in range(2)
    ]

    def pass_on(n):
        w_cross[n].wait_recv()
        w_group[n].start()
        w_far[0][n].start()

    def take(n):
        w_group[n].wait_recv()
        w_far[1][n].start()

    w_sib = [
        link(SIB, wgu.at[q], wgu.at[q], "seq", sib, SIBBED),
        link(SIB + 1, wdn.at[q], wdn.at[q], "seq", sib, SIBBED + 1),
    ]
    weighs = [
        link(WEIGH + s - 1, weigh.at[z], weigh.at[z], "expert", (z + s) % 4, WEIGHED + z)
        for s in range(1, 4)
    ]
    for copy in weighs + w_sib:
        copy.start()

    def forward(dest, count, values, exact=True):
        for at in range(0, size, slab):
            span = pl.ds(at, slab)
            dest[span] = mm(fh[span, :count], values)
            if exact:
                dest[span] += mm(fl[span, :count], values)

    def backward(count, spec, exact=True):
        high = spec.astype(BF16)
        if not exact:
            return mm(ih[:count], high)
        low = (spec - high.astype(F32)).astype(BF16)
        return mm(ih[:count], high) + mm(il[:count], high) + mm(ih[:count], low)

    def whole(ref):
        return ref[...].reshape(length, slab)

    for load in loads[9:]:
        load.wait()
    with jax.named_scope("tap spectrum"):
        forward(tap_spec, n_taps, taps[...])
    with jax.named_scope("x wait"):
        for copy in to_slabs:
            copy.wait_recv()
    w_cross[0].start()
    with jax.named_scope("cot 1 first"):
        cot_ahead(1, 0, 1)
    with jax.named_scope("filter"):
        forward(x_spec, length, whole(seq_x))
        xc, xs = x_spec[:half], x_spec[half:]
        hc, hs = tap_spec[:half], tap_spec[half:]
        prod = jnp.concatenate([xc * hc - xs * hs, xc * hs + xs * hc], axis=0)
        seq_f[...] = backward(length, prod).astype(BF16).reshape(4, tok, slab)
    to_rows = to_others(ROW - 1, ROWED - 1, lambda k: seq_f.at[k], tall.at[q, z])
    for copy in to_rows + w_cross[1:]:
        copy.start()
    tall[q, z] = seq_f[q]
    with jax.named_scope("cot 1"):
        cot_ahead(1, 1)
    with jax.named_scope("rows wait"):
        for copy in to_rows:
            copy.wait_recv()
    rows_ahead(0, 0)
    with jax.named_scope("pass 0"):
        pass_on(0)
    with jax.named_scope("pass 1"):
        pass_on(1)

    @pl.when(middle)
    def _():
        with jax.named_scope("rows 1 first"):
            rows_ahead(1, 0, 1)

    with jax.named_scope("pass 2"):
        pass_on(2)
    with jax.named_scope("take 0"):
        take(0)

    @pl.when(middle)
    def _():
        with jax.named_scope("rows 1"):
            rows_ahead(1, 1)
        with jax.named_scope("cot 2"):
            cot_ahead(2, 0)

    with jax.named_scope("take 1"):
        take(1)
    with jax.named_scope("weigh wait"):
        for k in range(1, 4):
            peer = (z + k) % 4
            link(WEIGH, weigh.at[peer], weigh.at[peer], "expert", peer, WEIGHED + peer).wait_recv()

    @pl.when(middle)
    def _():
        with jax.named_scope("rows 2 middle first"):
            rows_ahead(2, 0, 1)

    with jax.named_scope("take 2"):
        take(2)
    with jax.named_scope("weights wait"):
        for copy in w_sib + w_far[0] + w_far[1]:
            copy.wait_recv()

    origins = [z, pick(2, 3, 0, 1), pick(1, 0, 3, 2), pick(3, 2, 1, 0)]
    sublanes = lax.broadcasted_iota(jnp.int32, weigh.shape[1:], 0)
    gate_sums = [
        link(SUM + s - 1, sums.at[s], sums_in.at[z], "expert", origins[s], SUMMED + z)
        for s in range(1, 4)
    ]
    backs = [
        link(BACK + s - 2, back.at[s], rall.at[z], "expert", origins[s], BACKED + z)
        for s in range(2, 4)
    ]
    to_pre = link(FIRST, back.at[1], pre_in.at[0], "expert", 3 - z, BACKED + 4)
    to_next = link(FIRST, back.at[1], pre_in.at[1], "expert", origins[2], BACKED + 5)

    def block(s):
        origin = origins[s]
        span = pl.ds(pl.multiple_of(origin * tok, tok), tok)
        pre = mm(tall[0, origin], wgu[0])
        for k in range(1, 4):
            pre += mm(tall[k, origin], wgu[k])
        cot = gall[origin]
        weight = as_column(
            jnp.sum(jnp.where(sublanes == z, weigh[origin], 0.0), axis=0, keepdims=True)
        )
        raw = turned(cot, wdn[...].reshape(ff, width))
        gate, up = pre[:, :ff], pre[:, ff:]
        sigma = jax.nn.sigmoid(gate)
        swish = gate * sigma
        hidden = (swish * up).astype(BF16)
        gg = jnp.sum(hidden.astype(F32) * raw, axis=1, keepdims=True)
        grad_hidden = raw * weight
        grad_gate = grad_hidden * up * (sigma * (1.0 + gate * (1.0 - sigma)))
        gp = jnp.concatenate([grad_gate.astype(BF16), (grad_hidden * swish).astype(BF16)], axis=1)
        hid[span] = hidden
        gpre[span] = gp
        scaled[span] = (weight * cot.astype(F32)).astype(BF16)
        target, at = (back, s) if s else (rall, z)
        for k in range(4):
            target[at, k] = turned(gp, wgu[k]).astype(BF16)
        (sums if s else sums_in)[at] = jnp.broadcast_to(as_row(gg), sums.shape[1:])

    with jax.named_scope("block 0"):
        block(0)

    @pl.when(middle)
    def _():
        with jax.named_scope("rows 2 middle"):
            rows_ahead(2, 1)

    @pl.when(end)
    def _():
        with jax.named_scope("rows 2 end"):
            cot_ahead(2, 0)
            rows_ahead(2, 0)

    with jax.named_scope("block 1"):
        block(1)
    gate_sums[0].start()

    @pl.when(middle)
    def _():
        to_pre.start()

    @pl.when(end)
    def _():
        to_next.start()
        with jax.named_scope("rows 1 end"):
            rows_ahead(1, 0)

    with jax.named_scope("block 2"):
        block(2)
    gate_sums[1].start()

    @pl.when(end)
    def _():
        backs[0].start()
        with jax.named_scope("rows 3"):
            cot_ahead(3, 0)
            rows_ahead(3, 0)

    with jax.named_scope("block 3"):
        block(3)
    gate_sums[2].start()

    @pl.when(end)
    def _():
        backs[1].start()

    def partial_low(slot, dest):
        thin = pl.ds(pl.multiple_of(dest * fq, fq), fq)
        part[slot, slab:] = across(hid[:, thin], scaled[...]).astype(BF16)

    def partial_top(slot, dest):
        top = across(tall[dest].reshape(length, slab), gpre[...])
        part[slot, :slab] = top.astype(BF16)

    rows = slab + fq
    share = rows // PARTS
    low, top = pl.ds(slab, fq), pl.ds(0, slab)
    to_sib = [
        link(HALF, part.at[0, low], sib_in.at[0, low], "seq", sib, HALVED),
        link(HALF + 1, part.at[0, top], sib_in.at[0, top], "seq", sib, HALVED + 1),
        link(HALF + 2, part.at[1], sib_in.at[1], "seq", sib, HALVED + 2),
    ]
    to_cross = [
        link(
            PART + n, pair.at[pl.ds(n * share, share)], cross_in.at[pl.ds(n * share, share)],
            "seq", cross, PARTED + n,
        )
        for n in [*range(slab // share, PARTS), *range(slab // share)]
    ]
    near_end = pick(1, 0, 3, 2)
    last = pl.ds((slab // share - 1) * share, share)
    around = link(FIRST + 1, pair.at[last], relay_in, "", across_end, RELAYED)
    passed = link(
        RELAY, relay_in, cross_in.at[last], "expert", near_end, PARTED + slab // share - 1
    )

    for copy in w_cross + w_group + w_far[0] + w_far[1]:
        copy.wait_send()
    with jax.named_scope("partial 0"):
        partial_low(0, far)
        to_sib[0].start()
        partial_top(0, far)
        to_sib[1].start()
    with jax.named_scope("partial 2"):
        partial_low(2, cross)
        to_sib[0].wait_recv()
        pair[low] = (part[2, low].astype(F32) + sib_in[0, low].astype(F32)).astype(BF16)
        for copy in to_cross[:2]:
            copy.start()
        partial_top(2, cross)
        to_sib[1].wait_recv()
        pair[top] = (part[2, top].astype(F32) + sib_in[0, top].astype(F32)).astype(BF16)
        to_cross[2].start()

    @pl.when(end)
    def _():
        around.start()

    @pl.when(middle)
    def _():
        for copy in to_cross[3:5]:
            copy.start()

    with jax.named_scope("partial 1"):
        partial_low(1, sib)
        partial_top(1, sib)
    to_sib[2].start()
    with jax.named_scope("partial 3"):
        partial_low(3, q)
        partial_top(3, q)

    @pl.when(middle)
    def _():
        with jax.named_scope("pre wait"):
            to_pre.wait_recv()
        back[2] = (back[2].astype(F32) + pre_in[0].astype(F32)).astype(BF16)
        backs[0].start()
        with jax.named_scope("next wait"):
            to_next.wait_recv()
        back[3] = (back[3].astype(F32) + pre_in[1].astype(F32)).astype(BF16)
        backs[1].start()

    for d in range(3):
        for h in range(2):
            spread(h, cot_of(h), d, False)
            spread(2 + h, tok_of(h), d, False)

    with jax.named_scope("back wait"):
        for s in (1, 3):
            peer = (z + s) % 4
            link(BACK, back.at[1], rall.at[peer], "expert", peer, BACKED + peer).wait_recv()

    total = rall[z].astype(F32)
    for s in (1, 3):
        total += rall[(z + s) % 4].astype(F32)
    gfb[...] = total.astype(BF16)
    seq_g[q] = gfb[q]
    for copy in to_slabs:
        copy.wait_send()
    g_slabs = to_others(SLAB - 1, SLABBED - 1, lambda k: gfb.at[k], seq_g.at[q])
    for copy in g_slabs:
        copy.start()

    @pl.when(middle)
    def _():
        with jax.named_scope("part 0"):
            around.wait_recv()
            passed.start()

    for s in range(1, 4):
        peer = (z + s) % 4
        link(SUM, sums.at[s], sums_in.at[peer], "expert", peer, SUMMED + peer).wait_recv()
    gate_grads = jnp.zeros(ids.shape, F32)
    for s in range(4):
        gate_grads += jnp.where(ids == s, sums_in[s, 0:1], 0.0)
    gg_ref[...] = jnp.where(kept, gate_grads, 0.0).astype(BF16)

    with jax.named_scope("grad wait"):
        for copy in g_slabs:
            copy.wait_recv()

    @pl.when(middle)
    def _():
        to_cross[5].start()

    @pl.when(end)
    def _():
        to_cross[3].start()

    with jax.named_scope("tap grad"):
        forward(g_spec, length, whole(seq_g), False)
        gc, gs = g_spec[:half], g_spec[half:]
        xc, xs = x_spec[:half], x_spec[half:]
        prod = jnp.concatenate([gc * xc + gs * xs, gs * xc - gc * xs], axis=0)
        gfz[...] = backward(n_taps, prod, False).astype(BF16).reshape(4, piece, slab)
    near = [z, pick(1, 2, 1, 2), pick(2, 0, 3, 1), pick(3, 3, 0, 0)]
    fold = piece // 2

    def fold_of(ref, h, *at):
        return ref.at[*at, pl.ds(h * fold, fold)]

    tap_in = [
        link(
            TAP + 4 * h + s, fold_of(gfz, h, near[s]), fold_of(gfz_in, h, z), "expert", near[s],
            TAPPED + 4 * h + z,
        )
        for h in range(2) for s in (3, 2, 1)
    ]
    tap_out = [
        [
            link(
                OUT + 4 * h + s, fold_of(gf_ref, h, q, z), fold_of(gf_ref, h, q, z), "expert", near[s],
                OUTED + 4 * h + z,
            )
            for s in (3, 2, 1)
        ]
        for h in range(2)
    ]
    tap_cross = [
        [
            link(
                LAST + 4 * h + s, fold_of(gf_ref, h, q, near[s]), fold_of(gf_ref, h, q, near[s]), "seq",
                cross, LASTED + 4 * h + near[s],
            )
            for s in range(4)
        ]
        for h in range(2)
    ]
    for copy in tap_in:
        copy.start()

    with jax.named_scope("input grad"):
        gc, gs = g_spec[:half], g_spec[half:]
        hc, hs = tap_spec[:half], tap_spec[half:]
        prod = jnp.concatenate([gc * hc + gs * hs, gs * hc - gc * hs], axis=0)
        seq_in[...] = backward(length, prod).astype(BF16).reshape(4, tok, slab)
    for copy in to_rows:
        copy.wait_send()
    gin_out = to_others(ROW - 1, ROWED - 1, lambda k: seq_in.at[k], gin_ref.at[q])
    for copy in gin_out:
        copy.start()
    gin_ref[q] = seq_in[q]

    @pl.when(end)
    def _():
        to_cross[4].start()

    def tap_from(base, peer):
        link(TAP, fold_of(gfz, 0, 0), fold_of(gfz_in, 0, 0), "expert", peer, base + peer).wait_recv()

    with jax.named_scope("taps in"):
        for h in range(2):
            rows_h = pl.ds(h * fold, fold)
            mine = gfz[z, rows_h].astype(F32)
            for s in range(1, 4):
                tap_from(TAPPED + 4 * h, near[s])
                mine += gfz_in[near[s], rows_h].astype(F32)
            gf_ref[q, z, rows_h] = mine.astype(BF16)
            for copy in tap_out[h] + tap_cross[h][:1]:
                copy.start()

    with jax.named_scope("taps out"):
        for h in range(2):
            for s in range(1, 4):
                tap_from(OUTED + 4 * h, near[s])
                tap_cross[h][s].start()

    gf_sib = [
        link(SIB, gf_ref.at[q], gf_ref.at[q], "seq", sib, SIBBED),
        link(SIB + 1, gf_ref.at[cross], gf_ref.at[cross], "seq", sib, SIBBED + 1),
    ]
    for copy in w_sib:
        copy.wait_send()
    gf_sib[0].start()
    to_sib[2].wait_recv()
    with jax.named_scope("pair wait"):
        for copy in to_cross:
            copy.wait_recv()
    with jax.named_scope("weight sums"):
        dgu_ref[...] = (
            part[3, :slab].astype(F32) + sib_in[1, :slab].astype(F32) + cross_in[:slab].astype(F32)
        ).astype(BF16)
        dd_ref[...] = (
            part[3, slab:].astype(F32) + sib_in[1, slab:].astype(F32) + cross_in[slab:].astype(F32)
        ).astype(BF16)

    with jax.named_scope("taps cross"):
        for copy in tap_cross[0] + tap_cross[1]:
            copy.wait_recv()

    gf_sib[1].start()
    with jax.named_scope("last waits"):
        for copy in gin_out:
            copy.wait_recv()
        for copy in gf_sib:
            copy.wait_recv()
        @pl.when(middle)
        def _():
            for copy in to_cross[5:] + [passed]:
                copy.wait_send()

        @pl.when(end)
        def _():
            around.wait_send()

        for copy in (
            weighs + gate_sums + [to_pre] + backs + to_sib
            + to_cross[:5] + tap_in + tap_out[0] + tap_out[1] + tap_cross[0] + tap_cross[1] + g_slabs + gin_out + gf_sib
        ):
            copy.wait_send()


def finish_kernel(
    gin_ref, gg_ref, gf_ref, dgu_ref, dd_ref,
    gin_out, gg_out, gf_out, dg_out, du_out, dd_out, wide, sem,
):
    slab = gin_ref.shape[2]
    ff = dg_out.shape[2]
    pieces = [
        (gin_ref.at[k], gin_out.at[:, pl.ds(k * slab, slab)]) for k in range(4)
    ] + [
        (dgu_ref.at[:, pl.ds(0, ff)], dg_out.at[0]), (dgu_ref.at[:, pl.ds(ff, ff)], du_out.at[0]),
        (dd_ref, dd_out.at[0]), (gg_ref, gg_out),
    ]
    piece = gf_ref.shape[2]
    copies = []

    def send(source, dest):
        copies.append(pltpu.make_async_copy(source, dest, sem.at[len(copies)]))
        copies[-1].start()

    for a in range(4):
        span = pl.ds(a * piece, piece)
        for k in range(4):
            wide[span, pl.ds(k * slab, slab)] = gf_ref[k, a].astype(F32)
        send(wide.at[span], gf_out.at[span])
        for source, dest in pieces[2 * a:2 * a + 2]:
            send(source, dest)
    for copy in copies:
        copy.wait()


def dense_body(inputs, grad_out, gates, expert_ids, slot_index, filter_taps, w_gate, w_up, w_down):
    tok, width = inputs.shape
    taps = filter_taps.shape[0]
    ff = w_gate.shape[2]
    top = gates.shape[1]
    length = 4 * tok
    size = taps + length
    slab = width // 4
    rows = slab + ff // 4
    vm = lambda *shape: pltpu.VMEM(shape, BF16)
    vf = lambda *shape: pltpu.VMEM(shape, F32)
    st = lambda *shape: jax.ShapeDtypeStruct(shape, BF16)
    near = pl.BlockSpec(memory_space=pltpu.VMEM)
    hbm = pl.BlockSpec(memory_space=pltpu.HBM)
    far_away = lambda array: pltpu.with_memory_space_constraint(array, pltpu.HBM)
    fh, fl, ih, il = transforms(size)
    outs = pl.pallas_call(
        dense_kernel,
        out_shape=(
            vm(4, tok, slab), vm(top, tok), vm(4, 4, taps // 4, slab), vm(slab, 2 * ff),
            vm(ff // 4, width),
        ),
        in_specs=[hbm] * 13,
        out_specs=(near,) * 5,
        scratch_shapes=[
            vm(top, tok), pltpu.VMEM((top, tok), jnp.int32), pltpu.VMEM((top, tok), jnp.int32),
            vm(size, length), vm(size, length), vm(length, size), vm(length, size), vm(taps, slab),
            vf(size, slab), vf(size, slab), vf(size, slab),
            vm(4, tok, slab), vm(4, tok, slab), vm(4, tok, slab), vm(4, tok, slab),
            vm(4, 4, tok, slab), vm(4, tok, width), vm(4, slab, 2 * ff), vm(4, ff // 4, width),
            vm(length, ff), vm(length, 2 * ff), vm(length, width),
            vm(4, 4, tok, slab), vm(4, 4, tok, slab), vm(2, 4, tok, slab), vm(4, tok, slab),
            vm(4, rows, width), vm(2, rows, width), vm(rows, width), vm(rows, width), vm(rows // PARTS, width),
            vm(4, taps // 4, slab), vm(4, taps // 4, slab),
            vf(4, 8, tok), vf(4, 8, tok), vf(4, 8, tok),
            pltpu.SemaphoreType.DMA((56,)), pltpu.SemaphoreType.DMA((65,)),
        ],
        compiler_params=pltpu.CompilerParams(
            collective_id=0, has_side_effects=True, vmem_limit_bytes=48 * 1024 * 1024
        ),
    )(
        *[far_away(m) for m in (inputs, grad_out, gates.T, expert_ids.T, slot_index.T)],
        *[far_away(m) for m in (w_gate, w_up, w_down, filter_taps)],
        *[far_away(jnp.asarray(m)) for m in (fh[:, :length], fl[:, :length], ih[:length], il[:length])],
    )
    grads = pl.pallas_call(
        finish_kernel,
        out_shape=(
            st(tok, width), st(top, tok), jax.ShapeDtypeStruct((taps, width), F32),
            st(*w_gate.shape), st(*w_up.shape), st(*w_down.shape),
        ),
        in_specs=[near] * 5,
        out_specs=(hbm,) * 6,
        scratch_shapes=[vf(taps, width), pltpu.SemaphoreType.DMA((12,))],
        compiler_params=pltpu.CompilerParams(vmem_limit_bytes=8 * 1024 * 1024),
    )(*[pltpu.with_memory_space_constraint(array, pltpu.VMEM) for array in outs])
    return (grads[0], grads[1].T) + grads[2:]


def body_of(mesh):
    def body(*args):
        top_count = args[3].shape[1]
        tok, taps, dq = args[0].shape[0], args[5].shape[0], args[6].shape[1]
        small = mesh.shape["expert"] == top_count == 4 and mesh.shape["seq"] == 4
        small = small and mesh.shape["groups"] == 2
        if small and tok == 128 and taps == 2 * tok and dq == 2 * tok and 2 * args[6].shape[2] == args[0].shape[1]:
            return dense_body(*args)
        return routed_body(*args)

    return body


def solution(mesh):
    return jax.shard_map(
        body_of(mesh),
        mesh=mesh,
        in_specs=(
            P(("groups", "expert", "seq"), None),
            P(("groups", "expert", "seq"), None),
            P(("groups", "expert", "seq"), None),
            P(("groups", "expert", "seq"), None),
            P(("groups", "expert", "seq"), None),
            P(),
            P("expert", "seq", None),
            P("expert", "seq", None),
            P("expert", "seq", None),
        ),
        out_specs=(
            P(("groups", "expert", "seq"), None),
            P(("groups", "expert", "seq"), None),
            P("groups", None),
            P(("groups", "expert"), "seq", None),
            P(("groups", "expert"), "seq", None),
            P(("groups", "expert"), "seq", None),
        ),
        check_vma=False,
    )
```
